32 devices in a mesh: dp: 4 (over y, x), fsdp: 8 (over z, core).
Axes of the slice: x: 2, y: 2, z: 4, core: 2. Of those that a mesh axis runs over, the one named last changes fastest.
Arguments:
- triplane: bfloat16 [8, 1024, 1024], P('dp', 'fsdp'), may hold values from -6 to 6
- image_tokens: bfloat16 [8, 4096, 1024], P('dp', 'fsdp'), may hold values from -6 to 6
- camera: float32 [8, 16], P('dp'), may hold values from -4 to 4
- view_tokens: int32 [8], P('dp'), may hold values from 1024 to 4096, as said below
- master: float32 [16, 1024, 1024], P('dp', 'fsdp'), may hold values from -0.1875 to 0.1875
- moment1: float32 [16, 1024, 1024], P('dp', 'fsdp'), may hold values from -162.9174 to 162.9174
- moment2: float32 [16, 1024, 1024], P('dp', 'fsdp'), may hold values from 819.2 to 3276.8
- tile_slots: int32 [16], replicated, may hold values from 0 to 15, each once
- modulation: float32 [17, 9216], P(None, ('dp', 'fsdp')), may hold values from -0.9 to 0.9
- mod_moment1: float32 [17, 9216], P(None, ('dp', 'fsdp')), may hold values from -162.9174 to 162.9174
- mod_moment2: float32 [17, 9216], P(None, ('dp', 'fsdp')), may hold values from 819.2 to 3276.8
- cotangent: bfloat16 [8, 1024, 1024], P('dp', 'fsdp'), may hold values from -6 to 6
Outputs:
- block_output: bfloat16 [8, 1024, 1024], P('dp', 'fsdp')
- grad_triplane: float32 [8, 1024, 1024], P('dp', 'fsdp')
- grad_image: float32 [8, 4096, 1024], P('dp', 'fsdp')
- new_master: float32 [16, 1024, 1024], P('dp', 'fsdp')
- new_moment1: float32 [16, 1024, 1024], P('dp', 'fsdp')
- new_moment2: float32 [16, 1024, 1024], P('dp', 'fsdp')
- master_copy: bfloat16 [16, 1024, 1024], P('dp', 'fsdp')
- new_modulation: float32 [17, 9216], P(None, ('dp', 'fsdp'))
- new_mod_moment1: float32 [17, 9216], P(None, ('dp', 'fsdp'))
- new_mod_moment2: float32 [17, 9216], P(None, ('dp', 'fsdp'))
The draws below stay inside these ranges and needn't reach their ends.
Inputs may be any that keep to these rules, and one draw needn't show every extreme that they name: `view_tokens`: each is a whole multiple of 1024. `tile_slots`: every slot is named by exactly one tile.
All inputs are finite; a program needn't handle non-finite values.
Results may differ from the reference program's by a relative error of at most 0.035.
The reference program's roundings to bfloat16 on the way count: a program that leaves them out, or rounds other values in their place, can miss the bound.
Values may be sent and summed in bfloat16 or wider, within the bound.
A program may use at most 384 MiB of HBM per device.

```python
import math
from functools import partial
import jax
import jax.numpy as jnp
from jax import lax

D = 1024
H = 16
HD = 64
CAM = 16
TRI = 1024
VIEW = 1024
VIEWS = 4
STEP = 5
OBJECTS = 8
IMG = 4096
TILES = 16
MODW = 9216


def draw_view_tokens(key, part):
    view_count = jax.random.randint(jax.random.fold_in(key, 11), (OBJECTS,), 1, VIEWS + 1)
    chosen = jax.random.randint(jax.random.fold_in(key, 12), (), 0, OBJECTS)
    places = jnp.arange(OBJECTS, dtype=jnp.int32)
    view_count = jnp.where(places == chosen, VIEWS, view_count)
    return (view_count * VIEW).astype(jnp.int32)


def shard_levels(rng, dims, pieces, smallest, largest):
    level, own = 1.0, jax.random.fold_in(rng, 6)
    for axis_at, blocks in pieces:
        draws = jnp.exp(jax.random.uniform(jax.random.fold_in(own, axis_at), (blocks,), jnp.float32, smallest / len(pieces), largest / len(pieces)))
        level = level * jnp.repeat(draws, dims[axis_at] // blocks).reshape([-1 if axis == axis_at else 1 for axis in range(len(dims))])
    return level


def centred(own_key, shape, scale, limit, cuts=(), held_as=jnp.bfloat16):
    array = scale * jax.random.normal(own_key, shape, jnp.float32)
    if cuts:
        array = array * shard_levels(own_key, shape, cuts, -0.22, 0.18)
    return jnp.clip(array, -limit, limit).astype(held_as)


def setup_inputs(seed: int = 0) -> dict:
    streams_of = jax.random.split(jax.random.key(seed), 13)
    triplane = centred(streams_of[0], (OBJECTS, TRI, D), 1.0, 6.0, ((0, 4), (1, 8)))
    image_tokens = centred(streams_of[1], (OBJECTS, IMG, D), 1.0, 6.0, ((0, 4), (1, 8)))
    camera = centred(streams_of[2], (OBJECTS, CAM), 1.0, 4.0, ((0, 4),), jnp.float32)
    view_tokens = draw_view_tokens(jax.random.fold_in(streams_of[12], 71), 0)
    master = centred(streams_of[4], (TILES, D, D), D ** -0.5, 0.1875, ((0, 4), (1, 8)), jnp.float32)
    moment1 = centred(streams_of[5], (TILES, D, D), (0.3 * (OBJECTS * TRI) ** 0.5), 162.9174, ((0, 4), (1, 8)), jnp.float32)
    moment2 = jnp.clip(jnp.exp(math.log(3276.8) - 1.3862944 * jax.random.uniform(streams_of[6], (TILES, D, D), jnp.float32) ** shard_levels(streams_of[6], (TILES, D, D), ((0, 4), (1, 8)), -0.2, 0.2)), 819.2, 3276.8)
    tile_slots = jax.random.permutation(streams_of[7], TILES).astype(jnp.int32)
    modulation = centred(streams_of[8], (CAM + 1, MODW), 0.15, 0.9, ((1, 32),), jnp.float32)
    mod_moment1 = centred(streams_of[9], (CAM + 1, MODW), (0.3 * (OBJECTS * TRI) ** 0.5), 162.9174, ((1, 32),), jnp.float32)
    mod_moment2 = jnp.clip(jnp.exp(math.log(3276.8) - 1.3862944 * jax.random.uniform(streams_of[10], (CAM + 1, MODW), jnp.float32) ** shard_levels(streams_of[10], (CAM + 1, MODW), ((1, 32),), -0.2, 0.2)), 819.2, 3276.8)
    cotangent = centred(streams_of[11], (OBJECTS, TRI, D), 1.0, 6.0, ((0, 4), (1, 8)))
    return {"triplane": triplane, "image_tokens": image_tokens, "camera": camera, "view_tokens": view_tokens, "master": master, "moment1": moment1, "moment2": moment2, "tile_slots": tile_slots, "modulation": modulation, "mod_moment1": mod_moment1, "mod_moment2": mod_moment2, "cotangent": cotangent}


HIGHEST = lax.Precision.HIGHEST
NEGATIVE = -1e+30
BETA_ONE = 0.5
BETA_TWO = 0.5
EPSILON = 1e-08
WEIGHT_DECAY = 0.01
RATE_TILES = 0.03
RATE_MODULATION = 0.15

@jax.custom_vjp
def low(v):
    return lax.optimization_barrier(v.astype(jnp.bfloat16)).astype(jnp.float32)

@jax.custom_vjp
def low_back(v):
    return v

def low_keep(v):
    return (low(v), None)

def low_pass(kept, grad):
    return (grad,)

def back_keep(v):
    return (v, None)

def back_low(kept, grad):
    return (low(grad),)
low.defvjp(low_keep, low_pass)
low_back.defvjp(back_keep, back_low)

def matmul(left, right):
    return jnp.dot(left, right, precision=HIGHEST, preferred_element_type=jnp.float32)

def layer_norm(values):
    center = values - lax.optimization_barrier(jnp.mean(values, axis=-1, keepdims=True))
    spread = lax.optimization_barrier(jnp.mean(center * center, axis=-1, keepdims=True))
    return center * lax.rsqrt(spread + 1e-06)

def modulate(values, shift, scale):
    return layer_norm(values) * (1.0 + scale) + shift

def attend(queries, key_rows, value_rows, key_mask):
    scores = low_back(jnp.einsum('lhe,she->hls', queries, key_rows, precision=HIGHEST) * 0.125)
    scores = jnp.where(key_mask[None, None, :], scores, NEGATIVE)
    probs = jax.nn.softmax(scores, axis=-1)
    return jnp.einsum('hls,she->lhe', low(probs), value_rows, precision=HIGHEST)

def one_object(residual_in, image_rows, modrow, live_count, tiles_all):
    blocks = [modrow[position * D:(position + 1) * D] for position in range(9)]
    w_qkv = jnp.concatenate([tiles_all[0], tiles_all[1], tiles_all[2]], axis=1)
    w_kv = jnp.concatenate([tiles_all[5], tiles_all[6]], axis=1)
    w_up = jnp.concatenate([tiles_all[8], tiles_all[9], tiles_all[10], tiles_all[11]], axis=1)
    w_down = jnp.concatenate([tiles_all[12], tiles_all[13], tiles_all[14], tiles_all[15]], axis=0)
    normed_one = low(modulate(residual_in, blocks[0], blocks[1]))
    triples = low_back(low(matmul(normed_one, w_qkv)))
    self_query = triples[:, 0:D].reshape(TRI, H, HD)
    self_keys = triples[:, D:2 * D].reshape(TRI, H, HD)
    self_values = triples[:, 2 * D:3 * D].reshape(TRI, H, HD)
    every_key = jnp.ones((TRI,), dtype=bool)
    merged_one = low_back(low(attend(self_query, self_keys, self_values, every_key).reshape(TRI, D)))
    branch_one = low_back(matmul(merged_one, tiles_all[3]))
    residual_mid = residual_in + blocks[2] * branch_one
    normed_two = low(modulate(residual_mid, blocks[3], blocks[4]))
    cross_query = low_back(low(matmul(normed_two, tiles_all[4]))).reshape(TRI, H, HD)
    image_pairs = low_back(low(matmul(image_rows, w_kv)))
    cross_keys = image_pairs[:, 0:D].reshape(IMG, H, HD)
    cross_values = image_pairs[:, D:2 * D].reshape(IMG, H, HD)
    live_mask = lax.broadcasted_iota(jnp.int32, (IMG,), 0) < live_count
    merged_two = low_back(low(attend(cross_query, cross_keys, cross_values, live_mask).reshape(TRI, D)))
    branch_two = low_back(matmul(merged_two, tiles_all[7]))
    residual_late = residual_mid + blocks[5] * branch_two
    normed_three = low(modulate(residual_late, blocks[6], blocks[7]))
    hidden_pre = low_back(matmul(normed_three, w_up))
    hidden = low(jax.nn.gelu(hidden_pre, approximate=True))
    branch_three = low_back(matmul(hidden, w_down))
    return residual_late + blocks[8] * branch_three

def forward(camera, view_tokens, tile_slots, triplane_all, image_all, master, modulation):
    tiles_all = jnp.take(low(master), tile_slots, axis=0)
    mod_low = low(modulation)
    modulations = matmul(camera, mod_low[0:CAM]) + mod_low[CAM]

    def scan_step(carried, item):
        residual_in, image_rows, modrow, live_count = item
        result = jax.checkpoint(one_object)(residual_in, image_rows, modrow, live_count, tiles_all)
        return (carried, result)
    unused, outputs = lax.scan(scan_step, jnp.zeros((), jnp.float32), (triplane_all, image_all, modulations, view_tokens))
    return outputs

def adamw(weights, grads, first, second, rate):
    first_new = BETA_ONE * first + (1.0 - BETA_ONE) * grads
    second_new = BETA_TWO * second + (1.0 - BETA_TWO) * grads * grads
    first_hat = first_new / (1.0 - BETA_ONE ** STEP)
    second_hat = second_new / (1.0 - BETA_TWO ** STEP)
    weights_new = weights - rate * (first_hat / (jnp.sqrt(second_hat) + EPSILON) + WEIGHT_DECAY * weights)
    return (weights_new, first_new, second_new)

def reference(triplane, image_tokens, camera, view_tokens, master, moment1, moment2, tile_slots, modulation, mod_moment1, mod_moment2, cotangent):
    triplane_in = triplane.astype(jnp.float32)
    image_in = image_tokens.astype(jnp.float32)
    bound = partial(forward, camera, view_tokens, tile_slots)
    outputs, pull = jax.vjp(bound, triplane_in, image_in, master, modulation)
    grad_triplane, grad_image, grad_master, grad_modulation = pull(cotangent.astype(jnp.float32))
    new_master, new_moment1, new_moment2 = adamw(master, grad_master, moment1, moment2, RATE_TILES)
    new_modulation, new_mod_moment1, new_mod_moment2 = adamw(modulation, grad_modulation, mod_moment1, mod_moment2, RATE_MODULATION)
    return (outputs.astype(jnp.bfloat16), grad_triplane, grad_image, new_master, new_moment1, new_moment2, new_master.astype(jnp.bfloat16), new_modulation, new_mod_moment1, new_mod_moment2)
```

```python
import functools

import jax
import jax.numpy as jnp
from jax import lax
from jax.experimental import pallas as pl
from jax.experimental.pallas import tpu as pltpu
from jax.sharding import PartitionSpec as P

HD = 64
STEP = 5
VIEW = 1024
LANES = 128


HIGHEST = lax.Precision.HIGHEST
NEGATIVE = -1e30
BETA_ONE = 0.5
BETA_TWO = 0.5
EPSILON = 1e-08
WEIGHT_DECAY = 0.01
RATE_TILES = 0.03
RATE_MODULATION = 0.15


def contract(form, left, right):
    return jnp.einsum(form, left, right, preferred_element_type=jnp.float32)


def layer_norm(values):
    center = values - jnp.mean(values, axis=-1, keepdims=True)
    spread = jnp.mean(center * center, axis=-1, keepdims=True)
    return center * lax.rsqrt(spread + 1e-06)


def modulate(values, shift, scale):
    return layer_norm(values) * (1.0 + scale) + shift


def modulate_back(values, shift, scale, grad_normed):
    unused, pull = jax.vjp(modulate, values, shift, scale)
    return pull(grad_normed)


def gelu_tanh(values):
    return jax.nn.gelu(values, approximate=True)


NT = (((1,), (1,)), ((), ()))
NN = (((1,), (0,)), ((), ()))
TN = (((0,), (0,)), ((), ()))


def dot(left, right, dims):
    return lax.dot_general(left, right, dims, preferred_element_type=jnp.float32)


def head_part(values, head, heads):
    if heads == 1:
        return values
    lanes = lax.broadcasted_iota(jnp.int32, values.shape, 1)
    return jnp.where(lanes // HD == head, values, jnp.zeros_like(values))


def rows_of(ref, start, amount):
    block = ref[pl.ds(start, amount), 0]
    return block.reshape(block.shape[0] * block.shape[1], block.shape[2])


def forward_body(step_rows, live_ref, q_ref, k_ref, v_ref, out_ref, lse_ref):
    key_groups, unused_one, key_rows, width = k_ref.shape
    heads = width // HD
    per_block = step_rows // key_rows
    blocks = live_ref[pl.program_id(0)] // step_rows
    queries = rows_of(q_ref, 0, q_ref.shape[0]) * jnp.bfloat16(0.125)
    result = jnp.zeros(queries.shape, jnp.float32)
    for head in range(heads):
        own = head_part(queries, head, heads)

        def step(position, carried, own=own):
            highest, total, acc = carried
            keys = rows_of(k_ref, position * per_block, per_block)
            values = rows_of(v_ref, position * per_block, per_block)
            scores = dot(own, keys, NT)
            new_highest = jnp.maximum(highest, jnp.max(scores, axis=1, keepdims=True))
            weights = jnp.exp(scores - new_highest)
            scale = jnp.exp(highest - new_highest)
            total = total * scale + jnp.sum(weights, axis=1, keepdims=True)
            acc = acc * scale + dot(weights.astype(jnp.bfloat16), values, NN)
            return (new_highest, total, acc)

        first = (
            jnp.full((own.shape[0], 1), -jnp.inf, jnp.float32),
            jnp.zeros((own.shape[0], 1), jnp.float32),
            jnp.zeros(own.shape, jnp.float32),
        )
        highest, total, acc = lax.fori_loop(0, blocks, step, first)
        result = result + head_part(acc / total, head, heads)
        level = jnp.broadcast_to(highest + jnp.log(total), (own.shape[0], 128))
        lse_ref[0, head] = jnp.transpose(level)[0:1]
    out_ref[...] = result.astype(jnp.bfloat16).reshape(out_ref.shape)


def attend_forward(live, query_source, key_source, value_source, query_block, step_rows):
    (q_array, q_at), (k_array, k_at), (v_array, v_at) = query_source, key_source, value_source
    groups, objects, q_rows, unused_width = q_array.shape
    k_rows = k_array.shape[2]
    width = q_at[1]
    heads = width // HD
    total_q = groups * q_rows
    per_q = query_block // q_rows
    grid = (objects, total_q // query_block)
    whole = lambda index: (lambda o, j, live: (0, o, 0, index))
    part = lambda index: (lambda o, j, live: (j, o, 0, index))
    return pl.pallas_call(
        functools.partial(forward_body, step_rows),
        grid_spec=pltpu.PrefetchScalarGridSpec(
            num_scalar_prefetch=1,
            grid=grid,
            in_specs=[
                pl.BlockSpec((per_q, 1, q_rows, width), part(q_at[0])),
                pl.BlockSpec((groups, 1, k_rows, width), whole(k_at[0])),
                pl.BlockSpec((groups, 1, k_rows, width), whole(v_at[0])),
            ],
            out_specs=[
                pl.BlockSpec((per_q, 1, q_rows, width), part(0)),
                pl.BlockSpec((1, heads, 1, query_block), lambda o, j, live: (o, 0, 0, j)),
            ],
        ),
        out_shape=[
            jax.ShapeDtypeStruct((groups, objects, q_rows, width), jnp.bfloat16),
            jax.ShapeDtypeStruct((objects, heads, 1, total_q), jnp.float32),
        ],
        cost_estimate=pl.CostEstimate(
            flops=4 * objects * total_q * groups * k_rows * width,
            bytes_accessed=4 * objects * groups * (q_rows + k_rows) * width,
            transcendentals=objects * heads * total_q * groups * k_rows,
        ),
    )(live, q_array, k_array, v_array)


def backward_prepare(q_ref, out_ref, grad_ref, qs, gs, delta):
    heads = qs.shape[0]
    queries = rows_of(q_ref, 0, q_ref.shape[0]) * jnp.bfloat16(0.125)
    grads = rows_of(grad_ref, 0, grad_ref.shape[0])
    outs = rows_of(out_ref, 0, out_ref.shape[0])
    product = jnp.transpose(grads.astype(jnp.float32) * outs.astype(jnp.float32))
    for head in range(heads):
        qs[head] = head_part(queries, head, heads)
        gs[head] = head_part(grads, head, heads)
        delta[head] = jnp.sum(product[head * HD : (head + 1) * HD], axis=0, keepdims=True)


def backward_block(keys, values, lse_ref, qs, gs, delta):
    heads = qs.shape[0]
    grad_q, grad_k, grad_v = None, None, None
    for head in range(heads):
        own, grads = qs[head], gs[head]
        weights = jnp.exp(dot(keys, own, NT) - lse_ref[0, head])
        grad_weights = dot(values, grads, NT)
        grad_scores = (weights * (grad_weights - delta[head])).astype(jnp.bfloat16)
        new_v = dot(weights.astype(jnp.bfloat16), grads, NN)
        new_k = dot(grad_scores, own, NN)
        new_q = dot(grad_scores, head_part(keys, head, heads), TN)
        grad_q = new_q if grad_q is None else grad_q + new_q
        grad_k = new_k if grad_k is None else grad_k + new_k
        grad_v = new_v if grad_v is None else grad_v + new_v
    return grad_q, grad_k, grad_v


def cross_backward_body(
    live_ref, q_ref, k_ref, v_ref, out_ref, lse_ref, grad_ref, dq_ref, dkv_ref, qs, gs, delta, dq_acc
):
    position = pl.program_id(1)
    width = q_ref.shape[3]
    rows = k_ref.shape[0] * k_ref.shape[2]

    @pl.when(position == 0)
    def _():
        backward_prepare(q_ref, out_ref, grad_ref, qs, gs, delta)
        dq_acc[...] = jnp.zeros_like(dq_acc)

    alive = position * rows < live_ref[pl.program_id(0)]

    @pl.when(alive)
    def _():
        keys = rows_of(k_ref, 0, k_ref.shape[0])
        values = rows_of(v_ref, 0, v_ref.shape[0])
        grad_q, grad_k, grad_v = backward_block(keys, values, lse_ref, qs, gs, delta)
        dq_acc[...] += grad_q
        shape = (k_ref.shape[0], 1, k_ref.shape[2], width)
        dkv_ref[:, :, :, 0:width] = grad_k.astype(jnp.bfloat16).reshape(shape)
        dkv_ref[:, :, :, width : 2 * width] = grad_v.astype(jnp.bfloat16).reshape(shape)

    @pl.when(jnp.logical_not(alive))
    def _():
        dkv_ref[...] = jnp.zeros_like(dkv_ref)

    @pl.when(position == pl.num_programs(1) - 1)
    def _():
        dq_ref[...] = (dq_acc[...] * 0.125).astype(jnp.bfloat16).reshape(dq_ref.shape)


def attend_backward(live, query_source, key_source, value_source, outs, lse, grads, step_rows):
    (q_array, q_at), (k_array, k_at), (v_array, v_at) = query_source, key_source, value_source
    groups, objects, q_rows, unused_width = q_array.shape
    k_rows = k_array.shape[2]
    width = q_at[1]
    heads = width // HD
    total_q = groups * q_rows
    per_k = max(step_rows // k_rows, 1)
    grid = (objects, groups // per_k)
    whole = lambda index: (lambda o, j, live: (0, o, 0, index))
    part = lambda index: (lambda o, j, live: (j, o, 0, index))
    return pl.pallas_call(
        cross_backward_body,
        grid_spec=pltpu.PrefetchScalarGridSpec(
            num_scalar_prefetch=1,
            grid=grid,
            in_specs=[
                pl.BlockSpec((groups, 1, q_rows, width), whole(q_at[0])),
                pl.BlockSpec((per_k, 1, k_rows, width), part(k_at[0])),
                pl.BlockSpec((per_k, 1, k_rows, width), part(v_at[0])),
                pl.BlockSpec((groups, 1, q_rows, width), whole(0)),
                pl.BlockSpec((1, heads, 1, total_q), lambda o, j, live: (o, 0, 0, 0)),
                pl.BlockSpec((groups, 1, q_rows, width), whole(0)),
            ],
            out_specs=[
                pl.BlockSpec((groups, 1, q_rows, width), whole(0)),
                pl.BlockSpec((per_k, 1, k_rows, 2 * width), part(0)),
            ],
            scratch_shapes=[
                pltpu.VMEM((heads, total_q, width), jnp.bfloat16),
                pltpu.VMEM((heads, total_q, width), jnp.bfloat16),
                pltpu.VMEM((heads, 1, total_q), jnp.float32),
                pltpu.VMEM((total_q, width), jnp.float32),
            ],
        ),
        out_shape=[
            jax.ShapeDtypeStruct((groups, objects, q_rows, width), jnp.bfloat16),
            jax.ShapeDtypeStruct((groups, objects, k_rows, 2 * width), jnp.bfloat16),
        ],
        cost_estimate=pl.CostEstimate(
            flops=10 * objects * total_q * groups * k_rows * width,
            bytes_accessed=8 * objects * groups * (q_rows + k_rows) * width,
            transcendentals=objects * heads * total_q * groups * k_rows,
        ),
    )(live, q_array, k_array, v_array, outs, lse, grads)

CHUNKS = ((0, 1, 2), (5, 6), (3, 4, 7), (8, 9, 10, 11), (12, 13, 14, 15))
MOD_ROWS = 16
MESH = pl.DeviceIdType.MESH


def fetch_generic(master, modulation, tile_slots):
    narrow = master.astype(jnp.bfloat16)
    mod_narrow = modulation.astype(jnp.bfloat16)[:, None, None, :]
    row_blocks = lax.all_gather(narrow, "fsdp", axis=1, tiled=True)
    mod_blocks = lax.all_gather(mod_narrow, "fsdp", axis=2, tiled=True)
    gathered = lax.all_gather(row_blocks, "dp", axis=0, tiled=True)
    mod_all = lax.all_gather(mod_blocks, "dp", axis=1, tiled=True)
    chunks = [
        jnp.stack(
            [lax.dynamic_index_in_dim(gathered, tile_slots[tile], 0, keepdims=False) for tile in chunk]
        )
        for chunk in CHUNKS
    ]
    return chunks, mod_all.reshape(mod_all.shape[0], -1)


def pick_body(index_ref, source_ref, out_ref):
    out_ref[...] = source_ref[...]


def pick_rows(source, index):
    count = index.shape[0]
    block = (1,) + source.shape[1:]
    return pl.pallas_call(
        pick_body,
        grid_spec=pltpu.PrefetchScalarGridSpec(
            num_scalar_prefetch=1,
            grid=(count,),
            in_specs=[pl.BlockSpec(block, lambda t, index: (index[t], 0, 0))],
            out_specs=pl.BlockSpec(block, lambda t, index: (t, 0, 0)),
        ),
        out_shape=jax.ShapeDtypeStruct((count,) + source.shape[1:], source.dtype),
    )(index, source)


def move_dp(value, flip):
    owners = lax.axis_size("dp")
    return lax.ppermute(value, "dp", [(i, i ^ flip) for i in range(owners)])


def move_z(value, shift):
    groups = lax.axis_size("fsdp")
    return lax.ppermute(value, "fsdp", [(i, (i + 2 * shift) % groups) for i in range(groups)])


def assemble_body(tiles, rows, extra, *refs):
    pieces, refs = refs[:8], refs[8:]
    out_ref, refs = refs[0], refs[1:]
    extra_ref, refs = (refs[0], refs[1:]) if extra else (None, refs)
    hold, in_sem, out_sem, send_sem, recv_sem = refs
    dp_index = lax.axis_index("dp")
    fsdp_index = lax.axis_index("fsdp")
    z_index, core = fsdp_index // 2, fsdp_index % 2
    partner = {"fsdp": fsdp_index + 1 - 2 * core}
    loads = []
    for position in range(16):
        half, side, turn = position // 8, (position // 4) % 2, position % 4
        load = pltpu.make_async_copy(
            pieces[half * 4 + turn].at[side], hold.at[position], in_sem.at[position]
        )
        load.start()
        loads.append(load)
    barrier = pltpu.get_barrier_semaphore()
    pl.semaphore_signal(barrier, inc=1, device_id=partner, device_id_type=MESH)
    pl.semaphore_wait(barrier, 1)
    copies = []
    for position in range(16):
        half, side, turn = position // 8, (position // 4) % 2, position % 4
        z_from = (z_index + 8 - (2 * half + side)) % 4
        quarter = dp_index ^ turn
        loads[position].wait()
        targets = [(slice(tile * rows, (tile + 1) * rows), out_ref.at[tile]) for tile in range(tiles)]
        if extra:
            targets.append((slice(tiles * rows, tiles * rows + extra), extra_ref))
        for place, (window, target) in enumerate(targets):
            source = hold.at[position, window]
            target = target.at[z_from, core, quarter]
            away = pltpu.make_async_remote_copy(
                source,
                target,
                send_sem.at[position, place],
                recv_sem.at[position, place],
                device_id=partner,
                device_id_type=MESH,
            )
            away.start()
            here = pltpu.make_async_copy(source, target, out_sem.at[position, place])
            here.start()
            copies.append((away, here))
    for away, here in copies:
        away.wait()
        here.wait()


def assemble(pieces, tiles, rows, extra, collective):
    width = pieces[0].shape[2]
    places = tiles + (1 if extra else 0)
    out_shape = [jax.ShapeDtypeStruct((tiles, 4, 2, 4, rows, width), jnp.bfloat16)]
    if extra:
        out_shape.append(jax.ShapeDtypeStruct((4, 2, 4, extra, width), jnp.bfloat16))
    any_spec = pl.BlockSpec(memory_space=pl.ANY)
    return pl.pallas_call(
        functools.partial(assemble_body, tiles, rows, extra),
        out_shape=out_shape,
        in_specs=[any_spec] * 8,
        out_specs=[any_spec] * len(out_shape),
        scratch_shapes=[
            pltpu.VMEM((16, tiles * rows + extra, width), jnp.bfloat16),
            pltpu.SemaphoreType.DMA((16,)),
            pltpu.SemaphoreType.DMA((16, places)),
            pltpu.SemaphoreType.DMA((16, places)),
            pltpu.SemaphoreType.DMA((16, places)),
        ],
        compiler_params=pltpu.CompilerParams(collective_id=collective, has_side_effects=True),
        cost_estimate=pl.CostEstimate(
            flops=0, bytes_accessed=5 * tiles * 16 * rows * width * 2, transcendentals=0
        ),
    )(*pieces)


def fetch_weights(master, modulation, tile_slots):
    owners, groups = lax.axis_size("dp"), lax.axis_size("fsdp")
    if owners != 4 or groups != 8 or master.shape[1] != 128:
        return fetch_generic(master, modulation, tile_slots)
    slots_here, row_count, width = master.shape
    rows = row_count // owners
    dp_index = lax.axis_index("dp")
    narrow = master.astype(jnp.bfloat16).reshape(slots_here, owners, rows, width)
    parts = []
    for flip in range(4):
        part = lax.dynamic_index_in_dim(narrow, dp_index ^ flip, 1, keepdims=False)
        parts.append(part if flip == 0 else move_dp(part, flip))
    stacked = jnp.concatenate(parts, axis=0)
    index = ((tile_slots // slots_here) ^ dp_index) * slots_here + tile_slots % slots_here
    order = jnp.array([tile for chunk in CHUNKS for tile in chunk], jnp.int32)
    mine = pick_rows(stacked, index[order]).reshape(-1, width)
    mod_rows, mod_columns = modulation.shape
    mod_flat = modulation.astype(jnp.bfloat16).reshape(-1)
    mod_flat = jnp.pad(mod_flat, (0, MOD_ROWS * width - mod_flat.shape[0])).reshape(MOD_ROWS, width)
    chunks, mod_all, start, previous = [], None, 0, None
    for number, chunk in enumerate(CHUNKS):
        tiles = len(chunk)
        local = mine[start * rows : (start + tiles) * rows]
        start += tiles
        extra = MOD_ROWS if number == 0 else 0
        if extra:
            local = jnp.concatenate([local, mod_flat], axis=0)
        if previous is not None:
            local, unused_order = lax.optimization_barrier((local, previous))
        arrived = [local] + [move_z(local, shift) for shift in (1, 2, 3)]
        low, high = jnp.stack(arrived[:2]), jnp.stack(arrived[2:])
        previous = high
        low_x, high_y = move_dp(low, 1), move_dp(high, 2)
        low_y, high_x = move_dp(low, 2), move_dp(high, 1)
        low_xy, high_xy = move_dp(low_x, 2), move_dp(high_y, 1)
        pieces = (low, low_x, low_y, low_xy, high, high_x, high_y, high_xy)
        outs = assemble(pieces, tiles, rows, extra, number)
        chunks.append(outs[0].reshape(tiles, 32 * rows, width))
        if extra:
            flat = outs[1].reshape(8, 4, MOD_ROWS * width)[:, :, : mod_rows * mod_columns]
            mod_all = flat.reshape(8, 4, mod_rows, mod_columns).transpose(2, 1, 0, 3)
            mod_all = mod_all.reshape(mod_rows, -1)
    return chunks, mod_all


def exchange(pieces):
    return lax.all_to_all(pieces, "fsdp", split_axis=0, concat_axis=0, tiled=True)


def by_head(values, groups):
    objects, rows, blocks, width = values.shape
    share = width // groups
    moved = values.reshape(objects, rows, blocks, groups, share).transpose(3, 0, 1, 2, 4)
    return moved.reshape(groups, objects, rows, blocks * share)


def from_head(pieces, blocks):
    groups, objects, rows, share = pieces.shape
    share = share // blocks
    moved = pieces.reshape(groups, objects, rows, blocks, share).transpose(1, 2, 3, 0, 4)
    return moved.reshape(objects, rows, blocks, groups * share)


def source(array, index, width):
    if width % LANES == 0:
        return (array, (index, width))
    return (array[..., index * width : (index + 1) * width], (0, width))


def adamw(weights, grads, first, second, rate):
    first_new = BETA_ONE * first + (1.0 - BETA_ONE) * grads
    second_new = BETA_TWO * second + (1.0 - BETA_TWO) * grads * grads
    first_hat = first_new / (1.0 - BETA_ONE**STEP)
    second_hat = second_new / (1.0 - BETA_TWO**STEP)
    weights_new = weights - rate * (
        first_hat / (jnp.sqrt(second_hat) + EPSILON) + WEIGHT_DECAY * weights
    )
    return (weights_new, first_new, second_new)


def shards(
    triplane,
    image_tokens,
    camera,
    view_tokens,
    master,
    moment1,
    moment2,
    tile_slots,
    modulation,
    mod_moment1,
    mod_moment2,
    cotangent,
):
    objects, tri_local, model_width = triplane.shape
    img_local = image_tokens.shape[1]
    groups = lax.axis_size("fsdp")
    owners = lax.axis_size("dp")
    tri_total = tri_local * groups
    head_width = model_width // groups
    tile_count = master.shape[0] * owners
    chunks, mod_all = fetch_weights(master, modulation, tile_slots)
    mod_full = mod_all.astype(jnp.float32)
    modulations = (
        jnp.dot(camera, mod_full[:-1], precision=HIGHEST, preferred_element_type=jnp.float32)
        + mod_full[-1]
    )
    blocks = [
        modulations[:, position * model_width : (position + 1) * model_width][:, None, :]
        for position in range(9)
    ]
    tiles_qkv, tiles_pair, tiles_mixed, tiles_up, tiles_down = chunks
    tile_out_one, tile_query_two, tile_out_two = tiles_mixed[0], tiles_mixed[1], tiles_mixed[2]
    residual_in = triplane.astype(jnp.float32)
    normed_one = modulate(residual_in, blocks[0], blocks[1]).astype(jnp.bfloat16)
    triples = contract("otd,kde->otke", normed_one, tiles_qkv).astype(jnp.bfloat16)
    triple_heads = exchange(by_head(triples, groups))
    every_key = jnp.full((objects,), tri_total, jnp.int32)
    self_sources = [source(triple_heads, index, head_width) for index in range(3)]
    self_result, self_logsum = attend_forward(every_key, *self_sources, tri_total, VIEW)
    merged_one = from_head(exchange(self_result), 1)[:, :, 0]
    branch_one = contract("otd,de->ote", merged_one, tile_out_one)
    residual_mid = residual_in + blocks[2] * branch_one
    normed_two = modulate(residual_mid, blocks[3], blocks[4]).astype(jnp.bfloat16)
    cross_query = contract("otd,de->ote", normed_two, tile_query_two).astype(jnp.bfloat16)
    image_pairs = contract("oid,kde->oike", image_tokens, tiles_pair).astype(jnp.bfloat16)
    query_heads = exchange(by_head(cross_query[:, :, None], groups))
    pair_heads = exchange(by_head(image_pairs, groups))
    cross_sources = [
        source(query_heads, 0, head_width),
        source(pair_heads, 0, head_width),
        source(pair_heads, 1, head_width),
    ]
    cross_result, cross_logsum = attend_forward(view_tokens, *cross_sources, tri_total, VIEW)
    merged_two = from_head(exchange(cross_result), 1)[:, :, 0]
    branch_two = contract("otd,de->ote", merged_two, tile_out_two)
    residual_late = residual_mid + blocks[5] * branch_two
    normed_three = modulate(residual_late, blocks[6], blocks[7]).astype(jnp.bfloat16)
    hidden_pre = contract("otd,kde->otke", normed_three, tiles_up)
    hidden = gelu_tanh(hidden_pre).astype(jnp.bfloat16)
    branch_three = contract("otkd,kde->ote", hidden, tiles_down)
    block_output = (residual_late + blocks[8] * branch_three).astype(jnp.bfloat16)
    grad_final = cotangent.astype(jnp.float32)
    grad_gate_three = jnp.sum(grad_final * branch_three, axis=1)
    grad_branch_three = (blocks[8] * grad_final).astype(jnp.bfloat16)
    grad_down = contract("otkd,ote->kde", hidden, grad_branch_three)
    grad_hidden = contract("ote,kde->otkd", grad_branch_three, tiles_down)
    unused_gelu, gelu_pull = jax.vjp(gelu_tanh, hidden_pre)
    grad_pre = gelu_pull(grad_hidden)[0].astype(jnp.bfloat16)
    grad_up = contract("otd,otke->kde", normed_three, grad_pre)
    grad_normed_three = contract("otke,kde->otd", grad_pre, tiles_up)
    grad_late_norm, grad_shift_three, grad_scale_three = modulate_back(
        residual_late, blocks[6], blocks[7], grad_normed_three
    )
    grad_late = grad_final + grad_late_norm
    grad_gate_two = jnp.sum(grad_late * branch_two, axis=1)
    grad_branch_two = (blocks[5] * grad_late).astype(jnp.bfloat16)
    grad_out_two = contract("otd,ote->de", merged_two, grad_branch_two)
    grad_merged_two = contract("ote,de->otd", grad_branch_two, tile_out_two).astype(jnp.bfloat16)
    grad_cross_heads = exchange(by_head(grad_merged_two[:, :, None], groups))
    grad_query_heads, grad_pair_heads = attend_backward(
        view_tokens, *cross_sources, cross_result, cross_logsum, grad_cross_heads, VIEW
    )
    grad_query_two = from_head(exchange(grad_query_heads), 1)[:, :, 0]
    grad_pairs = from_head(exchange(grad_pair_heads), 2)
    grad_tile_query = contract("otd,ote->de", normed_two, grad_query_two)
    grad_tiles_pair = contract("oid,oike->kde", image_tokens, grad_pairs)
    grad_image = contract("oike,kde->oid", grad_pairs, tiles_pair)
    grad_normed_two = contract("ote,de->otd", grad_query_two, tile_query_two)
    grad_mid_norm, grad_shift_two, grad_scale_two = modulate_back(
        residual_mid, blocks[3], blocks[4], grad_normed_two
    )
    grad_mid = grad_late + grad_mid_norm
    grad_gate_one = jnp.sum(grad_mid * branch_one, axis=1)
    grad_branch_one = (blocks[2] * grad_mid).astype(jnp.bfloat16)
    grad_out_one = contract("otd,ote->de", merged_one, grad_branch_one)
    grad_merged_one = contract("ote,de->otd", grad_branch_one, tile_out_one).astype(jnp.bfloat16)
    grad_self_heads = exchange(by_head(grad_merged_one[:, :, None], groups))
    grad_self_query, grad_self_pair = attend_backward(
        every_key, *self_sources, self_result, self_logsum, grad_self_heads, VIEW
    )
    grad_triple_heads = jnp.concatenate([grad_self_query, grad_self_pair], axis=-1)
    grad_triples = from_head(exchange(grad_triple_heads), 3)
    grad_qkv = contract("otd,otke->kde", normed_one, grad_triples)
    grad_normed_one = contract("otke,kde->otd", grad_triples, tiles_qkv)
    grad_in_norm, grad_shift_one, grad_scale_one = modulate_back(
        residual_in, blocks[0], blocks[1], grad_normed_one
    )
    grad_triplane = grad_mid + grad_in_norm
    grad_mods = jnp.concatenate(
        [
            grad_shift_one[:, 0],
            grad_scale_one[:, 0],
            grad_gate_one,
            grad_shift_two[:, 0],
            grad_scale_two[:, 0],
            grad_gate_two,
            grad_shift_three[:, 0],
            grad_scale_three[:, 0],
            grad_gate_three,
        ],
        axis=-1,
    )
    grad_mod_rows = jnp.dot(
        camera.T, grad_mods, precision=HIGHEST, preferred_element_type=jnp.float32
    )
    grad_modulation = jnp.concatenate(
        [grad_mod_rows, jnp.sum(grad_mods, axis=0, keepdims=True)], axis=0
    )
    mod_columns = modulation.shape[1]
    grad_mod_blocks = grad_modulation.reshape(grad_modulation.shape[0], owners, groups, mod_columns)
    logical = [
        grad_qkv[0],
        grad_qkv[1],
        grad_qkv[2],
        grad_out_one,
        grad_tile_query,
        grad_tiles_pair[0],
        grad_tiles_pair[1],
        grad_out_two,
        grad_up[0],
        grad_up[1],
        grad_up[2],
        grad_up[3],
        grad_down[0],
        grad_down[1],
        grad_down[2],
        grad_down[3],
    ]
    slot_grads = jnp.zeros((tile_count, model_width, model_width), jnp.float32)
    for position in range(tile_count):
        slot_grads = lax.dynamic_update_index_in_dim(
            slot_grads, logical[position], tile_slots[position], 0
        )
    row_sums, mod_row_sums = (
        lax.psum_scatter(
            slot_grads.astype(jnp.bfloat16), "fsdp", scatter_dimension=1, tiled=True
        ).astype(jnp.float32),
        lax.psum_scatter(
            grad_mod_blocks.astype(jnp.bfloat16), "fsdp", scatter_dimension=2, tiled=True
        ).astype(jnp.float32),
    )
    tile_grad, mod_grad = (
        lax.psum_scatter(
            row_sums.astype(jnp.bfloat16), "dp", scatter_dimension=0, tiled=True
        ).astype(jnp.float32),
        lax.psum_scatter(
            mod_row_sums.astype(jnp.bfloat16), "dp", scatter_dimension=1, tiled=True
        ).astype(jnp.float32),
    )
    mod_grad = mod_grad.reshape(mod_grad.shape[0], mod_columns)
    new_master, new_moment1, new_moment2 = adamw(master, tile_grad, moment1, moment2, RATE_TILES)
    new_modulation, new_mod_moment1, new_mod_moment2 = adamw(
        modulation, mod_grad, mod_moment1, mod_moment2, RATE_MODULATION
    )
    return (
        block_output,
        grad_triplane,
        grad_image,
        new_master,
        new_moment1,
        new_moment2,
        new_master.astype(jnp.bfloat16),
        new_modulation,
        new_mod_moment1,
        new_mod_moment2,
    )


def solution(mesh):
    in_specs = (
        P("dp", "fsdp", None),
        P("dp", "fsdp", None),
        P("dp", None),
        P("dp"),
        P("dp", "fsdp", None),
        P("dp", "fsdp", None),
        P("dp", "fsdp", None),
        P(),
        P(None, ("dp", "fsdp")),
        P(None, ("dp", "fsdp")),
        P(None, ("dp", "fsdp")),
        P("dp", "fsdp", None),
    )
    out_specs = (
        P("dp", "fsdp", None),
        P("dp", "fsdp", None),
        P("dp", "fsdp", None),
        P("dp", "fsdp", None),
        P("dp", "fsdp", None),
        P("dp", "fsdp", None),
        P("dp", "fsdp", None),
        P(None, ("dp", "fsdp")),
        P(None, ("dp", "fsdp")),
        P(None, ("dp", "fsdp")),
    )
    return jax.shard_map(shards, mesh=mesh, in_specs=in_specs, out_specs=out_specs, check_vma=False)
```

```python
import functools

import jax
import jax.numpy as jnp
from jax import lax
from jax.experimental import pallas as pl
from jax.experimental.pallas import tpu as pltpu
from jax.sharding import PartitionSpec as P

HD = 64
STEP = 5
VIEW = 1024
LANES = 128


HIGHEST = lax.Precision.HIGHEST
NEGATIVE = -1e30
BETA_ONE = 0.5
BETA_TWO = 0.5
EPSILON = 1e-08
WEIGHT_DECAY = 0.01
RATE_TILES = 0.03
RATE_MODULATION = 0.15


def contract(form, left, right):
    return jnp.einsum(form, left, right, preferred_element_type=jnp.float32)


def layer_norm(values):
    center = values - jnp.mean(values, axis=-1, keepdims=True)
    spread = jnp.mean(center * center, axis=-1, keepdims=True)
    return center * lax.rsqrt(spread + 1e-06)


def modulate(values, shift, scale):
    return layer_norm(values) * (1.0 + scale) + shift


def modulate_back(values, shift, scale, grad_normed):
    unused, pull = jax.vjp(modulate, values, shift, scale)
    return pull(grad_normed)


def gelu_tanh(values):
    return jax.nn.gelu(values, approximate=True)


NT = (((1,), (1,)), ((), ()))
NN = (((1,), (0,)), ((), ()))
TN = (((0,), (0,)), ((), ()))


def dot(left, right, dims):
    return lax.dot_general(left, right, dims, preferred_element_type=jnp.float32)


def head_part(values, head, heads):
    if heads == 1:
        return values
    lanes = lax.broadcasted_iota(jnp.int32, values.shape, 1)
    return jnp.where(lanes // HD == head, values, jnp.zeros_like(values))


def rows_of(ref, start, amount):
    block = ref[pl.ds(start, amount), 0]
    return block.reshape(block.shape[0] * block.shape[1], block.shape[2])


def forward_body(step_rows, live_ref, q_ref, k_ref, v_ref, out_ref, lse_ref):
    key_groups, unused_one, key_rows, width = k_ref.shape
    heads = width // HD
    per_block = step_rows // key_rows
    blocks = live_ref[pl.program_id(0)] // step_rows
    queries = rows_of(q_ref, 0, q_ref.shape[0]) * jnp.bfloat16(0.125)
    result = jnp.zeros(queries.shape, jnp.float32)
    for head in range(heads):
        own = head_part(queries, head, heads)

        def step(position, carried, own=own):
            highest, total, acc = carried
            keys = rows_of(k_ref, position * per_block, per_block)
            values = rows_of(v_ref, position * per_block, per_block)
            scores = dot(own, keys, NT)
            new_highest = jnp.maximum(highest, jnp.max(scores, axis=1, keepdims=True))
            weights = jnp.exp(scores - new_highest)
            scale = jnp.exp(highest - new_highest)
            total = total * scale + jnp.sum(weights, axis=1, keepdims=True)
            acc = acc * scale + dot(weights.astype(jnp.bfloat16), values, NN)
            return (new_highest, total, acc)

        first = (
            jnp.full((own.shape[0], 1), -jnp.inf, jnp.float32),
            jnp.zeros((own.shape[0], 1), jnp.float32),
            jnp.zeros(own.shape, jnp.float32),
        )
        highest, total, acc = lax.fori_loop(0, blocks, step, first)
        result = result + head_part(acc / total, head, heads)
        level = jnp.broadcast_to(highest + jnp.log(total), (own.shape[0], 128))
        lse_ref[0, head] = jnp.transpose(level)[0:1]
    out_ref[...] = result.astype(jnp.bfloat16).reshape(out_ref.shape)


def attend_forward(live, query_source, key_source, value_source, query_block, step_rows):
    (q_array, q_at), (k_array, k_at), (v_array, v_at) = query_source, key_source, value_source
    groups, objects, q_rows, unused_width = q_array.shape
    k_rows = k_array.shape[2]
    width = q_at[1]
    heads = width // HD
    total_q = groups * q_rows
    per_q = query_block // q_rows
    grid = (objects, total_q // query_block)
    whole = lambda index: (lambda o, j, live: (0, o, 0, index))
    part = lambda index: (lambda o, j, live: (j, o, 0, index))
    return pl.pallas_call(
        functools.partial(forward_body, step_rows),
        grid_spec=pltpu.PrefetchScalarGridSpec(
            num_scalar_prefetch=1,
            grid=grid,
            in_specs=[
                pl.BlockSpec((per_q, 1, q_rows, width), part(q_at[0])),
                pl.BlockSpec((groups, 1, k_rows, width), whole(k_at[0])),
                pl.BlockSpec((groups, 1, k_rows, width), whole(v_at[0])),
            ],
            out_specs=[
                pl.BlockSpec((per_q, 1, q_rows, width), part(0)),
                pl.BlockSpec((1, heads, 1, query_block), lambda o, j, live: (o, 0, 0, j)),
            ],
        ),
        out_shape=[
            jax.ShapeDtypeStruct((groups, objects, q_rows, width), jnp.bfloat16),
            jax.ShapeDtypeStruct((objects, heads, 1, total_q), jnp.float32),
        ],
        cost_estimate=pl.CostEstimate(
            flops=4 * objects * total_q * groups * k_rows * width,
            bytes_accessed=4 * objects * groups * (q_rows + k_rows) * width,
            transcendentals=objects * heads * total_q * groups * k_rows,
        ),
    )(live, q_array, k_array, v_array)


def backward_prepare(q_ref, out_ref, grad_ref, qs, gs, delta):
    heads = qs.shape[0]
    queries = rows_of(q_ref, 0, q_ref.shape[0]) * jnp.bfloat16(0.125)
    grads = rows_of(grad_ref, 0, grad_ref.shape[0])
    outs = rows_of(out_ref, 0, out_ref.shape[0])
    product = jnp.transpose(grads.astype(jnp.float32) * outs.astype(jnp.float32))
    for head in range(heads):
        qs[head] = head_part(queries, head, heads)
        gs[head] = head_part(grads, head, heads)
        delta[head] = jnp.sum(product[head * HD : (head + 1) * HD], axis=0, keepdims=True)


def backward_block(keys, values, lse_ref, qs, gs, delta):
    heads = qs.shape[0]
    grad_q, grad_k, grad_v = None, None, None
    for head in range(heads):
        own, grads = qs[head], gs[head]
        weights = jnp.exp(dot(keys, own, NT) - lse_ref[0, head])
        grad_weights = dot(values, grads, NT)
        grad_scores = (weights * (grad_weights - delta[head])).astype(jnp.bfloat16)
        new_v = dot(weights.astype(jnp.bfloat16), grads, NN)
        new_k = dot(grad_scores, own, NN)
        new_q = dot(grad_scores, head_part(keys, head, heads), TN)
        grad_q = new_q if grad_q is None else grad_q + new_q
        grad_k = new_k if grad_k is None else grad_k + new_k
        grad_v = new_v if grad_v is None else grad_v + new_v
    return grad_q, grad_k, grad_v


def cross_backward_body(
    live_ref, q_ref, k_ref, v_ref, out_ref, lse_ref, grad_ref, dq_ref, dkv_ref, qs, gs, delta, dq_acc
):
    position = pl.program_id(1)
    width = q_ref.shape[3]
    rows = k_ref.shape[0] * k_ref.shape[2]

    @pl.when(position == 0)
    def _():
        backward_prepare(q_ref, out_ref, grad_ref, qs, gs, delta)
        dq_acc[...] = jnp.zeros_like(dq_acc)

    alive = position * rows < live_ref[pl.program_id(0)]

    @pl.when(alive)
    def _():
        keys = rows_of(k_ref, 0, k_ref.shape[0])
        values = rows_of(v_ref, 0, v_ref.shape[0])
        grad_q, grad_k, grad_v = backward_block(keys, values, lse_ref, qs, gs, delta)
        dq_acc[...] += grad_q
        shape = (k_ref.shape[0], 1, k_ref.shape[2], width)
        dkv_ref[:, :, :, 0:width] = grad_k.astype(jnp.bfloat16).reshape(shape)
        dkv_ref[:, :, :, width : 2 * width] = grad_v.astype(jnp.bfloat16).reshape(shape)

    @pl.when(jnp.logical_not(alive))
    def _():
        dkv_ref[...] = jnp.zeros_like(dkv_ref)

    @pl.when(position == pl.num_programs(1) - 1)
    def _():
        dq_ref[...] = (dq_acc[...] * 0.125).astype(jnp.bfloat16).reshape(dq_ref.shape)


def attend_backward(live, query_source, key_source, value_source, outs, lse, grads, step_rows):
    (q_array, q_at), (k_array, k_at), (v_array, v_at) = query_source, key_source, value_source
    groups, objects, q_rows, unused_width = q_array.shape
    k_rows = k_array.shape[2]
    width = q_at[1]
    heads = width // HD
    total_q = groups * q_rows
    per_k = max(step_rows // k_rows, 1)
    grid = (objects, groups // per_k)
    whole = lambda index: (lambda o, j, live: (0, o, 0, index))
    part = lambda index: (lambda o, j, live: (j, o, 0, index))
    return pl.pallas_call(
        cross_backward_body,
        grid_spec=pltpu.PrefetchScalarGridSpec(
            num_scalar_prefetch=1,
            grid=grid,
            in_specs=[
                pl.BlockSpec((groups, 1, q_rows, width), whole(q_at[0])),
                pl.BlockSpec((per_k, 1, k_rows, width), part(k_at[0])),
                pl.BlockSpec((per_k, 1, k_rows, width), part(v_at[0])),
                pl.BlockSpec((groups, 1, q_rows, width), whole(0)),
                pl.BlockSpec((1, heads, 1, total_q), lambda o, j, live: (o, 0, 0, 0)),
                pl.BlockSpec((groups, 1, q_rows, width), whole(0)),
            ],
            out_specs=[
                pl.BlockSpec((groups, 1, q_rows, width), whole(0)),
                pl.BlockSpec((per_k, 1, k_rows, 2 * width), part(0)),
            ],
            scratch_shapes=[
                pltpu.VMEM((heads, total_q, width), jnp.bfloat16),
                pltpu.VMEM((heads, total_q, width), jnp.bfloat16),
                pltpu.VMEM((heads, 1, total_q), jnp.float32),
                pltpu.VMEM((total_q, width), jnp.float32),
            ],
        ),
        out_shape=[
            jax.ShapeDtypeStruct((groups, objects, q_rows, width), jnp.bfloat16),
            jax.ShapeDtypeStruct((groups, objects, k_rows, 2 * width), jnp.bfloat16),
        ],
        cost_estimate=pl.CostEstimate(
            flops=10 * objects * total_q * groups * k_rows * width,
            bytes_accessed=8 * objects * groups * (q_rows + k_rows) * width,
            transcendentals=objects * heads * total_q * groups * k_rows,
        ),
    )(live, q_array, k_array, v_array, outs, lse, grads)

CHUNKS = ((0, 1, 2), (5, 6), (3, 4, 7), (8, 9, 10, 11), (12, 13, 14, 15))
EARLY = 8
MOD_ROWS = 16
MESH = pl.DeviceIdType.MESH


def places():
    dp_index, fsdp_index = lax.axis_index("dp"), lax.axis_index("fsdp")
    return dp_index, fsdp_index, fsdp_index // 2, fsdp_index % 2


def z_peer(fsdp_index, shift):
    return {"fsdp": (fsdp_index + 2 * shift) % 8}


def core_peer(fsdp_index):
    return {"fsdp": fsdp_index + 1 - 2 * (fsdp_index % 2)}


def dp_peer(dp_index, flip):
    return {"dp": dp_index ^ flip}


def greet(peers):
    barrier = pltpu.get_barrier_semaphore()
    for peer in peers:
        pl.semaphore_signal(barrier, inc=1, device_id=peer, device_id_type=MESH)
    pl.semaphore_wait(barrier, len(peers))


def remote(source, target, send_sem, recv_sem, peer):
    copy = pltpu.make_async_remote_copy(
        source, target, send_sem, recv_sem, device_id=peer, device_id_type=MESH
    )
    copy.start()
    return copy


def send_z(unit, full, fsdp_index, dp_index, z_index, sems):
    own = full.at[z_index, dp_index]
    return [
        remote(own, own, sems[0].at[unit, shift - 1], sems[1].at[unit, shift - 1], z_peer(fsdp_index, shift))
        for shift in (1, 2, 3)
    ]


def spread(units, fulls, outs, z_copies, z_local, sems, where):
    send_sems, recv_sems, out_sems = sems
    dp_index, fsdp_index, z_index, core = where
    near_x, near_y = dp_peer(dp_index, 1), dp_peer(dp_index, 2)
    first, second, last = {}, {}, []
    for step in range(units + 2):
        if step < units:
            unit, full = step, fulls[step]
            for copy in z_copies[unit]:
                copy.wait() if z_local else copy.wait_recv()
            low, high = full.at[0:2, dp_index], full.at[2:4, dp_index]
            pairs = [(low, near_x), (high, near_y), (low, near_y), (high, near_x)]
            first[unit] = [
                remote(ref, ref, send_sems.at[unit, 3 + n], recv_sems.at[unit, 3 + n], peer)
                for n, (ref, peer) in enumerate(pairs)
            ]
        if 0 <= step - 1 < units:
            unit, full = step - 1, fulls[step - 1]
            first[unit][0].wait_recv()
            first[unit][1].wait_recv()
            low, high = full.at[0:2, dp_index ^ 1], full.at[2:4, dp_index ^ 2]
            pairs = [(low, near_y), (high, near_x)]
            second[unit] = [
                remote(ref, ref, send_sems.at[unit, 7 + n], recv_sems.at[unit, 7 + n], peer)
                for n, (ref, peer) in enumerate(pairs)
            ]
        if 0 <= step - 2 < units:
            unit, full, out = step - 2, fulls[step - 2], outs[step - 2]
            for copy in first[unit][2:] + second[unit]:
                copy.wait_recv()
            target = out.at[:, core]
            last.append(
                remote(full, target, send_sems.at[unit, 9], recv_sems.at[unit, 9], core_peer(fsdp_index))
            )
            here = pltpu.make_async_copy(full, target, out_sems.at[unit])
            here.start()
            last.append(here)
    for unit in range(units):
        for copy in first[unit] + second[unit]:
            copy.wait_send()
    for copy in last:
        copy.wait()


def first_gather_body(tiles, rows, index_ref, narrow_ref, mod_ref, out_ref, mod_out_ref, wait_ref, rest_ref, stacked, mine, full, mod_full, zoned, swap_sems, load_sems, send_sems, recv_sems, out_sems, zone_sems):
    where = places()
    dp_index, fsdp_index, z_index, core = where
    peers = [z_peer(fsdp_index, shift) for shift in (1, 2, 3)]
    peers += [dp_peer(dp_index, flip) for flip in (1, 2, 3)] + [core_peer(fsdp_index)]
    greet(peers)
    swaps = [
        remote(narrow_ref.at[:, dp_index ^ flip], stacked.at[pl.ds(4 * flip, 4)], swap_sems.at[0, flip], swap_sems.at[1, flip], dp_peer(dp_index, flip))
        for flip in (1, 2, 3)
    ]
    own = pltpu.make_async_copy(narrow_ref.at[:, dp_index], stacked.at[pl.ds(0, 4)], load_sems.at[0])
    own.start()
    mod_load = pltpu.make_async_copy(mod_ref, mod_full.at[z_index, dp_index], load_sems.at[1])
    mod_load.start()
    mod_load.wait()
    z_copies = {tiles: send_z(tiles, mod_full, fsdp_index, dp_index, z_index, (send_sems, recv_sems))}
    own.wait()
    for swap in swaps:
        swap.wait()
    for tile in range(tiles):
        full[tile, z_index, dp_index] = stacked[index_ref[tile]]
        z_copies[tile] = send_z(tile, full.at[tile], fsdp_index, dp_index, z_index, (send_sems, recv_sems))

    def take(position, carried):
        mine[position] = stacked[index_ref[position + tiles]]
        return carried

    lax.fori_loop(0, 16 - tiles, take, 0)
    early = EARLY - tiles
    zone = [
        remote(mine.at[pl.ds(0, early)], zoned.at[z_index], zone_sems.at[0, shift - 1], zone_sems.at[1, shift - 1], z_peer(fsdp_index, shift))
        for shift in (1, 2, 3)
    ]
    zone_own = pltpu.make_async_copy(mine.at[pl.ds(0, early)], wait_ref.at[z_index], load_sems.at[2])
    zone_own.start()
    rest = pltpu.make_async_copy(mine.at[pl.ds(early, 16 - EARLY)], rest_ref, load_sems.at[3])
    rest.start()
    fulls = [full.at[tile] for tile in range(tiles)] + [mod_full]
    outs = [out_ref.at[tile] for tile in range(tiles)] + [mod_out_ref]
    spread(tiles + 1, fulls, outs, z_copies, False, (send_sems, recv_sems, out_sems), where)
    for unit in range(tiles + 1):
        for copy in z_copies[unit]:
            copy.wait_send()
    for copy in zone:
        copy.wait()
    zone_own.wait()
    rest.wait()
    stores = []
    for shift in (1, 2, 3):
        z_from = (z_index + shift) % 4
        store = pltpu.make_async_copy(zoned.at[z_from], wait_ref.at[z_from], load_sems.at[3 + shift])
        store.start()
        stores.append(store)
    for store in stores:
        store.wait()


ANY = pl.BlockSpec(memory_space=pl.ANY)


def comm_params(collective):
    return pltpu.CompilerParams(
        collective_id=collective, has_side_effects=True, vmem_limit_bytes=58 * 1024 * 1024
    )


def first_gather(narrow, mod_rows, index):
    tiles = len(CHUNKS[0])
    slots, owners, rows, width = narrow.shape
    bf = jnp.bfloat16
    return pl.pallas_call(
        functools.partial(first_gather_body, tiles, rows),
        grid_spec=pltpu.PrefetchScalarGridSpec(
            num_scalar_prefetch=1,
            grid=(),
            in_specs=[ANY, ANY],
            out_specs=[ANY] * 4,
            scratch_shapes=[
                pltpu.VMEM((16, rows, width), bf),
                pltpu.VMEM((16 - tiles, rows, width), bf),
                pltpu.VMEM((tiles, 4, 4, rows, width), bf),
                pltpu.VMEM((4, 4, MOD_ROWS, width), bf),
                pltpu.VMEM((4, EARLY - tiles, rows, width), bf),
                pltpu.SemaphoreType.DMA((2, 4)),
                pltpu.SemaphoreType.DMA((8,)),
                pltpu.SemaphoreType.DMA((tiles + 1, 10)),
                pltpu.SemaphoreType.DMA((tiles + 1, 10)),
                pltpu.SemaphoreType.DMA((tiles + 1,)),
                pltpu.SemaphoreType.DMA((2, 3)),
            ],
        ),
        out_shape=[
            jax.ShapeDtypeStruct((tiles, 4, 2, 4, rows, width), bf),
            jax.ShapeDtypeStruct((4, 2, 4, MOD_ROWS, width), bf),
            jax.ShapeDtypeStruct((4, EARLY - tiles, rows, width), bf),
            jax.ShapeDtypeStruct((16 - EARLY, rows, width), bf),
        ],
        compiler_params=comm_params(0),
        cost_estimate=pl.CostEstimate(flops=0, bytes_accessed=200_000_000, transcendentals=0),
    )(index, narrow, mod_rows)


def next_gather_body(tiles, start, zoned, source_ref, out_ref, full, load_sems, send_sems, recv_sems, out_sems):
    where = places()
    dp_index, fsdp_index, z_index, core = where
    loads = []
    for tile in range(tiles):
        if zoned:
            load = pltpu.make_async_copy(source_ref.at[:, start + tile], full.at[tile, :, dp_index], load_sems.at[tile])
        else:
            load = pltpu.make_async_copy(source_ref.at[start + tile], full.at[tile, z_index, dp_index], load_sems.at[tile])
        load.start()
        loads.append(load)
    peers = [dp_peer(dp_index, flip) for flip in (1, 2)] + [core_peer(fsdp_index)]
    if not zoned:
        peers += [z_peer(fsdp_index, shift) for shift in (1, 2, 3)]
    greet(peers)
    z_copies = {}
    for tile in range(tiles):
        if zoned:
            z_copies[tile] = [loads[tile]]
        else:
            loads[tile].wait()
            z_copies[tile] = send_z(tile, full.at[tile], fsdp_index, dp_index, z_index, (send_sems, recv_sems))
    fulls = [full.at[tile] for tile in range(tiles)]
    outs = [out_ref.at[tile] for tile in range(tiles)]
    spread(tiles, fulls, outs, z_copies, zoned, (send_sems, recv_sems, out_sems), where)
    if not zoned:
        for tile in range(tiles):
            for copy in z_copies[tile]:
                copy.wait_send()


def next_gather(source, tiles, start, zoned, collective):
    rows, width = source.shape[-2:]
    bf = jnp.bfloat16
    return pl.pallas_call(
        functools.partial(next_gather_body, tiles, start, zoned),
        in_specs=[ANY],
        out_specs=ANY,
        scratch_shapes=[
            pltpu.VMEM((tiles, 4, 4, rows, width), bf),
            pltpu.SemaphoreType.DMA((tiles,)),
            pltpu.SemaphoreType.DMA((tiles, 10)),
            pltpu.SemaphoreType.DMA((tiles, 10)),
            pltpu.SemaphoreType.DMA((tiles,)),
        ],
        out_shape=jax.ShapeDtypeStruct((tiles, 4, 2, 4, rows, width), bf),
        compiler_params=comm_params(collective),
        cost_estimate=pl.CostEstimate(flops=0, bytes_accessed=tiles * 30_000_000, transcendentals=0),
    )(source).reshape(tiles, 32 * rows, width)


def fast_layout(master):
    owners, groups = lax.axis_size("dp"), lax.axis_size("fsdp")
    return owners == 4 and groups == 8 and master.shape[1:] == (128, 1024)


def fetch_generic(master, modulation, tile_slots):
    narrow = master.astype(jnp.bfloat16)
    mod_narrow = modulation.astype(jnp.bfloat16)[:, None, None, :]
    row_blocks = lax.all_gather(narrow, "fsdp", axis=1, tiled=True)
    mod_blocks = lax.all_gather(mod_narrow, "fsdp", axis=2, tiled=True)
    gathered = lax.all_gather(row_blocks, "dp", axis=0, tiled=True)
    mod_all = lax.all_gather(mod_blocks, "dp", axis=1, tiled=True)
    chunks = [
        jnp.stack(
            [lax.dynamic_index_in_dim(gathered, tile_slots[tile], 0, keepdims=False) for tile in chunk]
        )
        for chunk in CHUNKS
    ]
    return chunks, mod_all.reshape(mod_all.shape[0], -1)


def sums_generic(logical, tile_slots):
    slot_grads = jnp.zeros((len(logical),) + logical[0].shape, jnp.bfloat16)
    for position, grad in enumerate(logical):
        slot_grads = lax.dynamic_update_index_in_dim(
            slot_grads, grad.astype(jnp.bfloat16), tile_slots[position], 0
        )
    row_sums = lax.psum_scatter(slot_grads, "fsdp", scatter_dimension=1, tiled=True)
    return lax.psum_scatter(row_sums, "dp", scatter_dimension=0, tiled=True)


def mod_generic(grad_modulation):
    owners, groups = lax.axis_size("dp"), lax.axis_size("fsdp")
    rows, width = grad_modulation.shape
    blocks = grad_modulation.reshape(rows, owners, groups, width // (owners * groups))
    sums = lax.psum_scatter(blocks.astype(jnp.bfloat16), "fsdp", scatter_dimension=2, tiled=True)
    sums = lax.psum_scatter(sums, "dp", scatter_dimension=1, tiled=True)
    return sums.reshape(rows, -1).astype(jnp.float32)


def wide(value):
    return value.astype(jnp.float32)


def reduce_scratch(tiles, rows, width):
    bf, f32 = jnp.bfloat16, jnp.float32
    return [
        pltpu.VMEM((2, tiles, 4, 4, rows, width), bf),
        pltpu.VMEM((4, tiles, 2, 2, rows, width), bf),
        pltpu.VMEM((2, tiles, 2, 2, rows, width), f32),
        pltpu.VMEM((4, tiles, 2, rows, width), bf),
        pltpu.VMEM((tiles, 4, rows, width), f32),
        pltpu.VMEM((2, 3, tiles, rows, width), bf),
        pltpu.VMEM((tiles, rows, width), bf),
        pltpu.SemaphoreType.DMA((2, tiles)),
        pltpu.SemaphoreType.DMA((8, tiles)),
        pltpu.SemaphoreType.DMA((8, tiles)),
    ]


def reduce_stages(tiles, scratch, out_ref, where):
    core_buf, swap, kept, swap_two, whole, zbuf, out_buf, load_sems, send_sems, recv_sems = scratch
    dp_index, fsdp_index, z_index, core = where
    x_bit, y_bit = dp_index % 2, dp_index // 2
    near_x, near_y = dp_peer(dp_index, 1), dp_peer(dp_index, 2)

    def moved(stage, tile):
        if stage == 1:
            ends = (swap.at[0, tile], swap.at[1, tile], near_x)
        elif stage == 2:
            ends = (swap.at[2, tile], swap.at[3, tile], near_y)
        elif stage == 3:
            ends = (swap_two.at[0, tile], swap_two.at[1, tile], near_y)
        elif stage == 4:
            ends = (swap_two.at[2, tile], swap_two.at[3, tile], near_x)
        else:
            shift = stage - 4
            ends = (zbuf.at[0, shift - 1, tile], zbuf.at[1, shift - 1, tile], z_peer(fsdp_index, shift))
        return pltpu.make_async_remote_copy(
            ends[0], ends[1], send_sems.at[stage, tile], recv_sems.at[stage, tile], device_id=ends[2], device_id_type=MESH
        )

    def both(tile, z_place, quarter):
        return wide(core_buf[0, tile, z_place, quarter]) + wide(core_buf[1, tile, z_place, quarter])

    def add_core(tile):
        for side in range(2):
            for other in range(2):
                kept[0, tile, side, other] = both(tile, side, 2 * other + x_bit)
                swap[0, tile, side, other] = both(tile, side, 2 * other + 1 - x_bit).astype(jnp.bfloat16)
                kept[1, tile, side, other] = both(tile, 2 + side, 2 * y_bit + other)
                swap[2, tile, side, other] = both(tile, 2 + side, 2 * (1 - y_bit) + other).astype(jnp.bfloat16)
        moved(1, tile).start()
        moved(2, tile).start()

    def add_first(tile):
        moved(1, tile).wait_recv()
        moved(2, tile).wait_recv()
        for side in range(2):
            whole[tile, side] = kept[0, tile, side, y_bit] + wide(swap[1, tile, side, y_bit])
            away = kept[0, tile, side, 1 - y_bit] + wide(swap[1, tile, side, 1 - y_bit])
            swap_two[0, tile, side] = away.astype(jnp.bfloat16)
            whole[tile, 2 + side] = kept[1, tile, side, x_bit] + wide(swap[3, tile, side, x_bit])
            away = kept[1, tile, side, 1 - x_bit] + wide(swap[3, tile, side, 1 - x_bit])
            swap_two[2, tile, side] = away.astype(jnp.bfloat16)
        moved(3, tile).start()
        moved(4, tile).start()

    def add_second(tile):
        moved(3, tile).wait_recv()
        moved(4, tile).wait_recv()
        for side in range(2):
            whole[tile, side] = whole[tile, side] + wide(swap_two[1, tile, side])
            whole[tile, 2 + side] = whole[tile, 2 + side] + wide(swap_two[3, tile, side])
        for shift in (1, 2, 3):
            zbuf[0, shift - 1, tile] = whole[tile, (z_index + shift) % 4].astype(jnp.bfloat16)
            moved(4 + shift, tile).start()

    def add_z(tile):
        total = whole[tile, z_index]
        for shift in (1, 2, 3):
            moved(4 + shift, tile).wait_recv()
            total = total + wide(zbuf[1, shift - 1, tile])
        out_buf[tile] = total.astype(jnp.bfloat16)

    def finish(tile):
        for stage in range(1, 8):
            moved(stage, tile).wait_send()

    return add_core, add_first, add_second, add_z, finish


def core_copies(entries, scratch, where):
    core_buf, load_sems, send_sems, recv_sems = scratch[0], scratch[-3], scratch[-2], scratch[-1]
    copies = []
    for tile, (theirs, ours) in enumerate(entries):
        away = remote(theirs, core_buf.at[1, tile], send_sems.at[0, tile], recv_sems.at[0, tile], core_peer(where[1]))
        load = pltpu.make_async_copy(ours, core_buf.at[0, tile], load_sems.at[0, tile])
        load.start()
        copies.append((away, load))
    return copies


def reduce_body(counts, extra, *refs):
    groups = len(counts)
    tiles = sum(counts)
    theirs, refs = refs[:groups], refs[groups:]
    ours, refs = refs[:groups], refs[groups:]
    if extra:
        mod_theirs, mod_ours, out_ref, mod_out_ref = refs[:4]
        refs = refs[4:]
    else:
        out_ref, refs = refs[0], refs[1:]
    scratch, mod_scratch = refs[:10], refs[10:]
    where = places()
    dp_index, fsdp_index = where[0], where[1]
    peers = [z_peer(fsdp_index, shift) for shift in (1, 2, 3)]
    peers += [dp_peer(dp_index, flip) for flip in (1, 2)] + [core_peer(fsdp_index)]
    greet(peers)
    entries = [
        (theirs[group].at[tile], ours[group].at[tile])
        for group in range(groups)
        for tile in range(counts[group])
    ]
    mod_copies = core_copies([(mod_theirs, mod_ours)], mod_scratch, where) if extra else []
    copies = core_copies(entries, scratch, where)
    stages = reduce_stages(tiles, scratch, out_ref, where)
    if extra:
        mod_stages = reduce_stages(1, mod_scratch, mod_out_ref, where)
        mod_copies[0][0].wait()
        mod_copies[0][1].wait()
        mod_stages[0](0)

    def arrive(tile):
        pltpu.make_async_copy(scratch[0].at[0, tile], scratch[0].at[0, tile], scratch[-3].at[0, tile]).wait()
        pltpu.make_async_remote_copy(
            scratch[0].at[1, tile], scratch[0].at[1, tile], scratch[-2].at[0, tile], scratch[-1].at[0, tile],
            device_id=core_peer(fsdp_index), device_id_type=MESH,
        ).wait_recv()

    def step(position, carried):
        @pl.when(position < tiles)
        def _():
            arrive(position)
            stages[0](position)

        for place in (1, 2, 3):
            tile = position - place

            @pl.when((tile >= 0) & (tile < tiles))
            def _():
                stages[place](tile)

        return carried

    if extra:
        step(0, 0)
        mod_stages[1](0)
        step(1, 0)
        mod_stages[2](0)
        step(2, 0)
        mod_stages[3](0)
        lax.fori_loop(3, tiles + 3, step, 0)
        mod_stages[4](0)
    else:
        lax.fori_loop(0, tiles + 3, step, 0)

    def close(tile, carried):
        stages[4](tile)
        return carried

    lax.fori_loop(0, tiles, close, 0)
    for away, load in copies:
        away.wait_send()
    store = pltpu.make_async_copy(scratch[6], out_ref, scratch[-3].at[1, 0])
    store.start()
    if extra:
        mod_store = pltpu.make_async_copy(mod_scratch[6], mod_out_ref, mod_scratch[-3].at[1, 0])
        mod_store.start()
        mod_store.wait()
    store.wait()


def reduce_tiles(theirs, ours, mods, collective):
    counts = tuple(part.shape[0] for part in theirs)
    tiles = sum(counts)
    rows, width = theirs[0].shape[-2:]
    bf = jnp.bfloat16
    operands = list(theirs) + list(ours)
    out_shape = [jax.ShapeDtypeStruct((tiles, rows, width), bf)]
    scratch = reduce_scratch(tiles, rows, width)
    if mods is not None:
        operands += list(mods)
        out_shape.append(jax.ShapeDtypeStruct((1, MOD_ROWS, width), bf))
        scratch = scratch + reduce_scratch(1, MOD_ROWS, width)
    return pl.pallas_call(
        functools.partial(reduce_body, counts, mods is not None),
        in_specs=[ANY] * len(operands),
        out_specs=[ANY] * len(out_shape),
        scratch_shapes=scratch,
        out_shape=out_shape,
        compiler_params=comm_params(collective),
        cost_estimate=pl.CostEstimate(flops=0, bytes_accessed=tiles * 40_000_000, transcendentals=0),
    )(*operands)


def owner_body(counts, index_ref, *refs):
    sources, refs = refs[: len(counts)], refs[len(counts) :]
    out_ref, held, picked, load_sems, send_sems, recv_sems = refs
    dp_index = lax.axis_index("dp")
    loads, start = [], 0
    for place, count in enumerate(counts):
        load = pltpu.make_async_copy(sources[place], held.at[pl.ds(start, count)], load_sems.at[place])
        load.start()
        loads.append(load)
        start += count
    greet([dp_peer(dp_index, flip) for flip in (1, 2, 3)])
    for load in loads:
        load.wait()
    copies = []
    for flip in (3, 1, 2, 0):
        for slot in range(4):
            picked[flip, slot] = held[index_ref[4 * flip + slot]]
        target = out_ref.at[:, dp_index]
        if flip:
            copies.append(
                remote(picked.at[flip], target, send_sems.at[flip], recv_sems.at[flip], dp_peer(dp_index, flip))
            )
        else:
            here = pltpu.make_async_copy(picked.at[flip], target, load_sems.at[0])
            here.start()
            copies.append(here)
    for copy in copies:
        copy.wait()


def to_owners(sums, order, tile_slots, collective):
    rows, width = sums[0].shape[-2:]
    counts = tuple(part.shape[0] for part in sums)
    dp_index = lax.axis_index("dp")
    spots = jnp.arange(16, dtype=jnp.int32)
    wanted = ((spots // 4) ^ dp_index) * 4 + spots % 4
    slots = tile_slots[jnp.array(order, jnp.int32)]
    matches = slots[None, :] == wanted[:, None]
    index = jnp.sum(jnp.where(matches, spots[None, :], 0), axis=1).astype(jnp.int32)
    bf = jnp.bfloat16
    return pl.pallas_call(
        functools.partial(owner_body, counts),
        grid_spec=pltpu.PrefetchScalarGridSpec(
            num_scalar_prefetch=1,
            grid=(),
            in_specs=[ANY] * len(counts),
            out_specs=ANY,
            scratch_shapes=[
                pltpu.VMEM((16, rows, width), bf),
                pltpu.VMEM((4, 4, rows, width), bf),
                pltpu.SemaphoreType.DMA((len(counts),)),
                pltpu.SemaphoreType.DMA((4,)),
                pltpu.SemaphoreType.DMA((4,)),
            ],
        ),
        out_shape=jax.ShapeDtypeStruct((4, 4, rows, width), bf),
        compiler_params=comm_params(collective),
        cost_estimate=pl.CostEstimate(flops=0, bytes_accessed=50_000_000, transcendentals=0),
    )(index, *sums)


def half_sums(form, left, right):
    core = lax.axis_index("fsdp") % 2
    parts = left.reshape(left.shape[:-1] + (4, 2, left.shape[-1] // 8))
    shape = parts.shape[:-3] + (left.shape[-1] // 2,)
    halves = []
    for side in (1 - core, core):
        half = lax.dynamic_index_in_dim(parts, side, parts.ndim - 2, keepdims=False).reshape(shape)
        total = contract(form, half, right).astype(jnp.bfloat16)
        halves.append(total.reshape(-1, 4, 4, total.shape[-2] // 16, total.shape[-1]))
    return halves


def mod_halves(grad_modulation):
    rows, width = grad_modulation.shape
    columns = width // 32
    core = lax.axis_index("fsdp") % 2
    blocks = grad_modulation.reshape(rows, 4, 4, 2, columns).transpose(3, 2, 1, 0, 4)
    flat = blocks.astype(jnp.bfloat16).reshape(2, 4, 4, rows * columns)
    flat = jnp.pad(flat, ((0, 0), (0, 0), (0, 0), (0, MOD_ROWS * 1024 - rows * columns)))
    flat = flat.reshape(2, 4, 4, MOD_ROWS, 1024)
    return [lax.dynamic_index_in_dim(flat, side, 0, keepdims=False) for side in (1 - core, core)]

def after(value, *others):
    return lax.optimization_barrier((value,) + others)[0]


def weight_source(master, modulation, tile_slots):
    if not fast_layout(master):
        chunks, mod_all = fetch_generic(master, modulation, tile_slots)
        return (lambda number, *others: chunks[number]), mod_all
    slots_here, row_count, width = master.shape
    dp_index = lax.axis_index("dp")
    narrow = master.astype(jnp.bfloat16).reshape(slots_here, 4, row_count // 4, width)
    index = ((tile_slots // slots_here) ^ dp_index) * slots_here + tile_slots % slots_here
    index = index[jnp.array([tile for chunk in CHUNKS for tile in chunk], jnp.int32)]
    mod_rows, mod_columns = modulation.shape
    mod_flat = modulation.astype(jnp.bfloat16).reshape(-1)
    mod_flat = jnp.pad(mod_flat, (0, MOD_ROWS * width - mod_flat.shape[0])).reshape(MOD_ROWS, width)
    first, mods, zoned, rest = first_gather(narrow, mod_flat, index)
    flat = mods.reshape(8, 4, MOD_ROWS * width)[:, :, : mod_rows * mod_columns]
    mod_all = flat.reshape(8, 4, mod_rows, mod_columns).transpose(2, 1, 0, 3).reshape(mod_rows, -1)

    def chunk(number, *others):
        tiles = len(CHUNKS[number])
        if number == 0:
            return first.reshape(tiles, row_count * 8, width)
        if number < 3:
            return next_gather(after(zoned, *others), tiles, (0, 2)[number - 1], True, number)
        return next_gather(after(rest, *others), tiles, (0, 4)[number - 3], False, number)

    return chunk, mod_all


def exchange(pieces):
    return lax.all_to_all(pieces, "fsdp", split_axis=0, concat_axis=0, tiled=True)


def by_head(values, groups):
    objects, rows, blocks, width = values.shape
    share = width // groups
    moved = values.reshape(objects, rows, blocks, groups, share).transpose(3, 0, 1, 2, 4)
    return moved.reshape(groups, objects, rows, blocks * share)


def from_head(pieces, blocks):
    groups, objects, rows, share = pieces.shape
    share = share // blocks
    moved = pieces.reshape(groups, objects, rows, blocks, share).transpose(1, 2, 3, 0, 4)
    return moved.reshape(objects, rows, blocks, groups * share)


def source(array, index, width):
    if width % LANES == 0:
        return (array, (index, width))
    return (array[..., index * width : (index + 1) * width], (0, width))


def adamw(weights, grads, first, second, rate):
    first_new = BETA_ONE * first + (1.0 - BETA_ONE) * grads
    second_new = BETA_TWO * second + (1.0 - BETA_TWO) * grads * grads
    first_hat = first_new / (1.0 - BETA_ONE**STEP)
    second_hat = second_new / (1.0 - BETA_TWO**STEP)
    weights_new = weights - rate * (
        first_hat / (jnp.sqrt(second_hat) + EPSILON) + WEIGHT_DECAY * weights
    )
    return (weights_new, first_new, second_new)


def shards(
    triplane,
    image_tokens,
    camera,
    view_tokens,
    master,
    moment1,
    moment2,
    tile_slots,
    modulation,
    mod_moment1,
    mod_moment2,
    cotangent,
):
    objects, tri_local, model_width = triplane.shape
    groups = lax.axis_size("fsdp")
    tri_total = tri_local * groups
    head_width = model_width // groups
    fast = fast_layout(master)
    partial_sums = half_sums if fast else contract
    chunk, mod_all = weight_source(master, modulation, tile_slots)
    mod_full = mod_all.astype(jnp.float32)
    modulations = (
        jnp.dot(camera, mod_full[:-1], precision=HIGHEST, preferred_element_type=jnp.float32)
        + mod_full[-1]
    )
    blocks = [
        modulations[:, position * model_width : (position + 1) * model_width][:, None, :]
        for position in range(9)
    ]
    tiles_qkv = chunk(0)
    residual_in = triplane.astype(jnp.float32)
    normed_one = modulate(residual_in, blocks[0], blocks[1]).astype(jnp.bfloat16)
    triples = contract("otd,kde->otke", normed_one, tiles_qkv).astype(jnp.bfloat16)
    triple_sent = by_head(triples, groups)
    triple_heads = exchange(triple_sent)
    tiles_pair = chunk(1, triple_sent)
    triple_heads = after(triple_heads, tiles_pair)
    image_pairs = contract("oid,kde->oike", image_tokens, tiles_pair).astype(jnp.bfloat16)
    pair_sent = by_head(image_pairs, groups)
    pair_heads = exchange(pair_sent)
    triple_heads = after(triple_heads, pair_sent)
    every_key = jnp.full((objects,), tri_total, jnp.int32)
    self_sources = [source(triple_heads, index, head_width) for index in range(3)]
    self_result, self_logsum = attend_forward(every_key, *self_sources, tri_total, VIEW)
    tiles_mixed = chunk(2, self_result, pair_sent)
    tile_out_one, tile_query_two, tile_out_two = tiles_mixed[0], tiles_mixed[1], tiles_mixed[2]
    merged_one = from_head(after(exchange(self_result), tiles_mixed), 1)[:, :, 0]
    branch_one = contract("otd,de->ote", merged_one, tile_out_one)
    residual_mid = residual_in + blocks[2] * branch_one
    normed_two = modulate(residual_mid, blocks[3], blocks[4]).astype(jnp.bfloat16)
    cross_query = contract("otd,de->ote", normed_two, tile_query_two).astype(jnp.bfloat16)
    query_sent = by_head(cross_query[:, :, None], groups)
    query_heads = exchange(query_sent)
    tiles_up = chunk(3, query_sent)
    query_heads = after(query_heads, tiles_up)
    cross_sources = [
        source(query_heads, 0, head_width),
        source(pair_heads, 0, head_width),
        source(pair_heads, 1, head_width),
    ]
    cross_result, cross_logsum = attend_forward(view_tokens, *cross_sources, tri_total, VIEW)
    tiles_down = chunk(4, cross_result)
    merged_two = from_head(after(exchange(cross_result), tiles_down), 1)[:, :, 0]
    branch_two = contract("otd,de->ote", merged_two, tile_out_two)
    residual_late = residual_mid + blocks[5] * branch_two
    normed_three = modulate(residual_late, blocks[6], blocks[7]).astype(jnp.bfloat16)
    hidden_pre = contract("otd,kde->otke", normed_three, tiles_up)
    hidden = gelu_tanh(hidden_pre).astype(jnp.bfloat16)
    branch_three = contract("otkd,kde->ote", hidden, tiles_down)
    block_output = (residual_late + blocks[8] * branch_three).astype(jnp.bfloat16)
    grad_final = cotangent.astype(jnp.float32)
    grad_gate_three = jnp.sum(grad_final * branch_three, axis=1)
    grad_branch_three = (blocks[8] * grad_final).astype(jnp.bfloat16)
    grad_hidden = contract("ote,kde->otkd", grad_branch_three, tiles_down)
    unused_gelu, gelu_pull = jax.vjp(gelu_tanh, hidden_pre)
    grad_pre = gelu_pull(grad_hidden)[0].astype(jnp.bfloat16)
    grad_normed_three = contract("otke,kde->otd", grad_pre, tiles_up)
    grad_late_norm, grad_shift_three, grad_scale_three = modulate_back(
        residual_late, blocks[6], blocks[7], grad_normed_three
    )
    grad_late = grad_final + grad_late_norm
    grad_gate_two = jnp.sum(grad_late * branch_two, axis=1)
    grad_branch_two = (blocks[5] * grad_late).astype(jnp.bfloat16)
    grad_merged_two = contract("ote,de->otd", grad_branch_two, tile_out_two).astype(jnp.bfloat16)
    grad_cross_sent = by_head(grad_merged_two[:, :, None], groups)
    grad_cross_heads = exchange(grad_cross_sent)
    grad_down = partial_sums("otkd,ote->kde", hidden, grad_branch_three)
    grad_up = partial_sums("otd,otke->kde", normed_three, grad_pre)
    grad_out_two = partial_sums("otd,ote->de", merged_two, grad_branch_two)
    if fast:
        theirs, ours = after(tuple(grad_down), grad_cross_sent)
        (sums_down,) = reduce_tiles([theirs], [ours], None, 5)
        grad_cross_heads = after(grad_cross_heads, sums_down)
    grad_query_heads, grad_pair_heads = attend_backward(
        view_tokens, *cross_sources, cross_result, cross_logsum, grad_cross_heads, VIEW
    )
    grad_query_back = exchange(grad_query_heads)
    grad_pair_back = exchange(grad_pair_heads)
    if fast:
        theirs, ours = after(tuple(grad_up), grad_pair_heads, sums_down)
        (sums_up,) = reduce_tiles([theirs], [ours], None, 6)
        grad_query_back = after(grad_query_back, sums_up)
    grad_query_two = from_head(grad_query_back, 1)[:, :, 0]
    grad_tile_query = partial_sums("otd,ote->de", normed_two, grad_query_two)
    grad_normed_two = contract("ote,de->otd", grad_query_two, tile_query_two)
    grad_mid_norm, grad_shift_two, grad_scale_two = modulate_back(
        residual_mid, blocks[3], blocks[4], grad_normed_two
    )
    grad_mid = grad_late + grad_mid_norm
    grad_gate_one = jnp.sum(grad_mid * branch_one, axis=1)
    grad_branch_one = (blocks[2] * grad_mid).astype(jnp.bfloat16)
    grad_merged_one = contract("ote,de->otd", grad_branch_one, tile_out_one).astype(jnp.bfloat16)
    grad_self_sent = by_head(grad_merged_one[:, :, None], groups)
    grad_self_heads = exchange(grad_self_sent)
    grad_out_one = partial_sums("otd,ote->de", merged_one, grad_branch_one)
    if fast:
        halves = after(tuple(grad_out_two) + tuple(grad_tile_query), grad_self_sent, sums_up)
        (sums_mid,) = reduce_tiles([halves[0], halves[2]], [halves[1], halves[3]], None, 7)
        grad_self_heads = after(grad_self_heads, sums_mid)
    grad_self_query, grad_self_pair = attend_backward(
        every_key, *self_sources, self_result, self_logsum, grad_self_heads, VIEW
    )
    grad_triple_heads = jnp.concatenate([grad_self_query, grad_self_pair], axis=-1)
    grad_triple_back = exchange(grad_triple_heads)
    if fast:
        grad_pair_back = after(grad_pair_back, grad_triple_heads)
    grad_pairs = from_head(grad_pair_back, 2)
    grad_tiles_pair = partial_sums("oid,oike->kde", image_tokens, grad_pairs)
    grad_image = contract("oike,kde->oid", grad_pairs, tiles_pair)
    if fast:
        halves = after(tuple(grad_tiles_pair) + tuple(grad_out_one), grad_triple_heads, sums_mid)
        (sums_late,) = reduce_tiles([halves[0], halves[2]], [halves[1], halves[3]], None, 8)
        grad_triple_back = after(grad_triple_back, sums_late)
    grad_triples = from_head(grad_triple_back, 3)
    grad_qkv = partial_sums("otd,otke->kde", normed_one, grad_triples)
    grad_normed_one = contract("otke,kde->otd", grad_triples, tiles_qkv)
    grad_in_norm, grad_shift_one, grad_scale_one = modulate_back(
        residual_in, blocks[0], blocks[1], grad_normed_one
    )
    grad_triplane = grad_mid + grad_in_norm
    grad_mods = jnp.concatenate(
        [
            grad_shift_one[:, 0],
            grad_scale_one[:, 0],
            grad_gate_one,
            grad_shift_two[:, 0],
            grad_scale_two[:, 0],
            grad_gate_two,
            grad_shift_three[:, 0],
            grad_scale_three[:, 0],
            grad_gate_three,
        ],
        axis=-1,
    )
    grad_mod_rows = jnp.dot(
        camera.T, grad_mods, precision=HIGHEST, preferred_element_type=jnp.float32
    )
    grad_modulation = jnp.concatenate(
        [grad_mod_rows, jnp.sum(grad_mods, axis=0, keepdims=True)], axis=0
    )
    if fast:
        theirs, ours = after(tuple(grad_qkv), sums_late)
        sums_qkv, mod_sum = reduce_tiles([theirs], [ours], mod_halves(grad_modulation), 9)
        sums = [sums_qkv, sums_late, sums_mid, sums_up, sums_down]
        order = (0, 1, 2, 5, 6, 3, 7, 4, 8, 9, 10, 11, 12, 13, 14, 15)
        tile_grad = to_owners(sums, order, tile_slots, 10).reshape(master.shape)
        mod_grad = mod_sum.reshape(-1)[: modulation.size].reshape(modulation.shape)
        tile_grad, mod_grad = tile_grad.astype(jnp.float32), mod_grad.astype(jnp.float32)
    else:
        logical = [grad_qkv[0], grad_qkv[1], grad_qkv[2], grad_out_one, grad_tile_query]
        logical = logical + [grad_tiles_pair[0], grad_tiles_pair[1], grad_out_two]
        logical = logical + [grad_up[tile] for tile in range(4)]
        logical = logical + [grad_down[tile] for tile in range(4)]
        tile_grad = sums_generic(logical, tile_slots).astype(jnp.float32)
        mod_grad = mod_generic(grad_modulation)
    new_master, new_moment1, new_moment2 = adamw(master, tile_grad, moment1, moment2, RATE_TILES)
    new_modulation, new_mod_moment1, new_mod_moment2 = adamw(
        modulation, mod_grad, mod_moment1, mod_moment2, RATE_MODULATION
    )
    return (
        block_output,
        grad_triplane,
        grad_image,
        new_master,
        new_moment1,
        new_moment2,
        new_master.astype(jnp.bfloat16),
        new_modulation,
        new_mod_moment1,
        new_mod_moment2,
    )


def solution(mesh):
    in_specs = (
        P("dp", "fsdp", None),
        P("dp", "fsdp", None),
        P("dp", None),
        P("dp"),
        P("dp", "fsdp", None),
        P("dp", "fsdp", None),
        P("dp", "fsdp", None),
        P(),
        P(None, ("dp", "fsdp")),
        P(None, ("dp", "fsdp")),
        P(None, ("dp", "fsdp")),
        P("dp", "fsdp", None),
    )
    out_specs = (
        P("dp", "fsdp", None),
        P("dp", "fsdp", None),
        P("dp", "fsdp", None),
        P("dp", "fsdp", None),
        P("dp", "fsdp", None),
        P("dp", "fsdp", None),
        P("dp", "fsdp", None),
        P(None, ("dp", "fsdp")),
        P(None, ("dp", "fsdp")),
        P(None, ("dp", "fsdp")),
    )
    return jax.shard_map(shards, mesh=mesh, in_specs=in_specs, out_specs=out_specs, check_vma=False)
```

```python
import functools

import jax
import jax.numpy as jnp
from jax import lax
from jax.experimental import pallas as pl
from jax.experimental.pallas import tpu as pltpu
from jax.sharding import PartitionSpec as P

HD = 64
STEP = 5
VIEW = 1024
LANES = 128


HIGHEST = lax.Precision.HIGHEST
NEGATIVE = -1e30
BETA_ONE = 0.5
BETA_TWO = 0.5
EPSILON = 1e-08
WEIGHT_DECAY = 0.01
RATE_TILES = 0.03
RATE_MODULATION = 0.15


def contract(form, left, right):
    return jnp.einsum(form, left, right, preferred_element_type=jnp.float32)


def layer_norm(values):
    center = values - jnp.mean(values, axis=-1, keepdims=True)
    spread = jnp.mean(center * center, axis=-1, keepdims=True)
    return center * lax.rsqrt(spread + 1e-06)


def modulate(values, shift, scale):
    return layer_norm(values) * (1.0 + scale) + shift


def modulate_back(values, shift, scale, grad_normed):
    unused, pull = jax.vjp(modulate, values, shift, scale)
    return pull(grad_normed)


def gelu_tanh(values):
    return jax.nn.gelu(values, approximate=True)


NT = (((1,), (1,)), ((), ()))
NN = (((1,), (0,)), ((), ()))
TN = (((0,), (0,)), ((), ()))


def dot(left, right, dims):
    return lax.dot_general(left, right, dims, preferred_element_type=jnp.float32)


def head_part(values, head, heads):
    if heads == 1:
        return values
    lanes = lax.broadcasted_iota(jnp.int32, values.shape, 1)
    return jnp.where(lanes // HD == head, values, jnp.zeros_like(values))


def rows_of(ref, start, amount):
    block = ref[pl.ds(start, amount), 0]
    return block.reshape(block.shape[0] * block.shape[1], block.shape[2])


def forward_body(step_rows, live_ref, q_ref, k_ref, v_ref, out_ref, lse_ref):
    key_groups, unused_one, key_rows, width = k_ref.shape
    heads = width // HD
    per_block = step_rows // key_rows
    blocks = live_ref[pl.program_id(0)] // step_rows
    queries = rows_of(q_ref, 0, q_ref.shape[0]) * jnp.bfloat16(0.125)
    result = jnp.zeros(queries.shape, jnp.float32)
    for head in range(heads):
        own = head_part(queries, head, heads)

        def step(position, carried, own=own):
            highest, total, acc = carried
            keys = rows_of(k_ref, position * per_block, per_block)
            values = rows_of(v_ref, position * per_block, per_block)
            scores = dot(own, keys, NT)
            new_highest = jnp.maximum(highest, jnp.max(scores, axis=1, keepdims=True))
            weights = jnp.exp(scores - new_highest)
            scale = jnp.exp(highest - new_highest)
            total = total * scale + jnp.sum(weights, axis=1, keepdims=True)
            acc = acc * scale + dot(weights.astype(jnp.bfloat16), values, NN)
            return (new_highest, total, acc)

        first = (
            jnp.full((own.shape[0], 1), -jnp.inf, jnp.float32),
            jnp.zeros((own.shape[0], 1), jnp.float32),
            jnp.zeros(own.shape, jnp.float32),
        )
        highest, total, acc = lax.fori_loop(0, blocks, step, first)
        result = result + head_part(acc / total, head, heads)
        level = jnp.broadcast_to(highest + jnp.log(total), (own.shape[0], 128))
        lse_ref[0, head] = jnp.transpose(level)[0:1]
    out_ref[...] = result.astype(jnp.bfloat16).reshape(out_ref.shape)


def attend_forward(live, query_source, key_source, value_source, query_block, step_rows):
    (q_array, q_at), (k_array, k_at), (v_array, v_at) = query_source, key_source, value_source
    groups, unused_blocks, objects, q_rows, width = q_array.shape
    k_rows = k_array.shape[3]
    heads = width // HD
    total_q = groups * q_rows
    per_q = query_block // q_rows
    grid = (objects, total_q // query_block)
    whole = lambda index: (lambda o, j, live: (0, index, o, 0, 0))
    part = lambda index: (lambda o, j, live: (j, index, o, 0, 0))
    return pl.pallas_call(
        functools.partial(forward_body, step_rows),
        grid_spec=pltpu.PrefetchScalarGridSpec(
            num_scalar_prefetch=1,
            grid=grid,
            in_specs=[
                pl.BlockSpec((per_q, None, 1, q_rows, width), part(q_at)),
                pl.BlockSpec((groups, None, 1, k_rows, width), whole(k_at)),
                pl.BlockSpec((groups, None, 1, k_rows, width), whole(v_at)),
            ],
            out_specs=[
                pl.BlockSpec((per_q, 1, q_rows, width), lambda o, j, live: (j, o, 0, 0)),
                pl.BlockSpec((1, heads, 1, query_block), lambda o, j, live: (o, 0, 0, j)),
            ],
        ),
        out_shape=[
            jax.ShapeDtypeStruct((groups, objects, q_rows, width), jnp.bfloat16),
            jax.ShapeDtypeStruct((objects, heads, 1, total_q), jnp.float32),
        ],
        cost_estimate=pl.CostEstimate(
            flops=4 * objects * total_q * groups * k_rows * width,
            bytes_accessed=4 * objects * groups * (q_rows + k_rows) * width,
            transcendentals=objects * heads * total_q * groups * k_rows,
        ),
    )(live, q_array, k_array, v_array)


def backward_prepare(q_ref, out_ref, grad_ref, qs, gs, delta):
    heads = qs.shape[0]
    queries = rows_of(q_ref, 0, q_ref.shape[0]) * jnp.bfloat16(0.125)
    grads = rows_of(grad_ref, 0, grad_ref.shape[0])
    outs = rows_of(out_ref, 0, out_ref.shape[0])
    product = jnp.transpose(grads.astype(jnp.float32) * outs.astype(jnp.float32))
    for head in range(heads):
        qs[head] = head_part(queries, head, heads)
        gs[head] = head_part(grads, head, heads)
        delta[head] = jnp.sum(product[head * HD : (head + 1) * HD], axis=0, keepdims=True)


def backward_block(keys, values, lse_ref, qs, gs, delta):
    heads = qs.shape[0]
    grad_q, grad_k, grad_v = None, None, None
    for head in range(heads):
        own, grads = qs[head], gs[head]
        weights = jnp.exp(dot(keys, own, NT) - lse_ref[0, head])
        grad_weights = dot(values, grads, NT)
        grad_scores = (weights * (grad_weights - delta[head])).astype(jnp.bfloat16)
        new_v = dot(weights.astype(jnp.bfloat16), grads, NN)
        new_k = dot(grad_scores, own, NN)
        new_q = dot(grad_scores, head_part(keys, head, heads), TN)
        grad_q = new_q if grad_q is None else grad_q + new_q
        grad_k = new_k if grad_k is None else grad_k + new_k
        grad_v = new_v if grad_v is None else grad_v + new_v
    return grad_q, grad_k, grad_v


def cross_backward_body(
    live_ref, q_ref, k_ref, v_ref, out_ref, lse_ref, grad_ref, dq_ref, dkv_ref, qs, gs, delta, dq_acc
):
    position = pl.program_id(1)
    width = q_ref.shape[3]
    rows = k_ref.shape[0] * k_ref.shape[2]

    @pl.when(position == 0)
    def _():
        backward_prepare(q_ref, out_ref, grad_ref, qs, gs, delta)
        dq_acc[...] = jnp.zeros_like(dq_acc)

    alive = position * rows < live_ref[pl.program_id(0)]

    @pl.when(alive)
    def _():
        keys = rows_of(k_ref, 0, k_ref.shape[0])
        values = rows_of(v_ref, 0, v_ref.shape[0])
        grad_q, grad_k, grad_v = backward_block(keys, values, lse_ref, qs, gs, delta)
        dq_acc[...] += grad_q
        shape = (k_ref.shape[0], 1, k_ref.shape[2], width)
        dkv_ref[:, 0] = grad_k.astype(jnp.bfloat16).reshape(shape)
        dkv_ref[:, 1] = grad_v.astype(jnp.bfloat16).reshape(shape)

    @pl.when(jnp.logical_not(alive))
    def _():
        dkv_ref[...] = jnp.zeros_like(dkv_ref)

    @pl.when(position == pl.num_programs(1) - 1)
    def _():
        dq_ref[...] = (dq_acc[...] * 0.125).astype(jnp.bfloat16).reshape(dq_ref.shape)


def attend_backward(live, query_source, key_source, value_source, outs, lse, grads, step_rows):
    (q_array, q_at), (k_array, k_at), (v_array, v_at) = query_source, key_source, value_source
    groups, unused_blocks, objects, q_rows, width = q_array.shape
    k_rows = k_array.shape[3]
    heads = width // HD
    total_q = groups * q_rows
    per_k = max(step_rows // k_rows, 1)
    grid = (objects, groups // per_k)
    whole = lambda index: (lambda o, j, live: (0, index, o, 0, 0))
    part = lambda index: (lambda o, j, live: (j, index, o, 0, 0))
    tokens = pl.BlockSpec((groups, 1, q_rows, width), lambda o, j, live: (0, o, 0, 0))
    return pl.pallas_call(
        cross_backward_body,
        grid_spec=pltpu.PrefetchScalarGridSpec(
            num_scalar_prefetch=1,
            grid=grid,
            in_specs=[
                pl.BlockSpec((groups, None, 1, q_rows, width), whole(q_at)),
                pl.BlockSpec((per_k, None, 1, k_rows, width), part(k_at)),
                pl.BlockSpec((per_k, None, 1, k_rows, width), part(v_at)),
                tokens,
                pl.BlockSpec((1, heads, 1, total_q), lambda o, j, live: (o, 0, 0, 0)),
                pl.BlockSpec((groups, None, 1, q_rows, width), whole(0)),
            ],
            out_specs=[
                tokens,
                pl.BlockSpec((per_k, 2, 1, k_rows, width), part(0)),
            ],
            scratch_shapes=[
                pltpu.VMEM((heads, total_q, width), jnp.bfloat16),
                pltpu.VMEM((heads, total_q, width), jnp.bfloat16),
                pltpu.VMEM((heads, 1, total_q), jnp.float32),
                pltpu.VMEM((total_q, width), jnp.float32),
            ],
        ),
        out_shape=[
            jax.ShapeDtypeStruct((groups, objects, q_rows, width), jnp.bfloat16),
            jax.ShapeDtypeStruct((groups, 2, objects, k_rows, width), jnp.bfloat16),
        ],
        cost_estimate=pl.CostEstimate(
            flops=10 * objects * total_q * groups * k_rows * width,
            bytes_accessed=8 * objects * groups * (q_rows + k_rows) * width,
            transcendentals=objects * heads * total_q * groups * k_rows,
        ),
    )(live, q_array, k_array, v_array, outs, lse, grads)

CHUNKS = ((5, 6), (0, 1, 2), (3, 4, 7), (8, 9, 10, 11), (12, 13, 14, 15))
EARLY = 8
MOD_ROWS = 16
MESH = pl.DeviceIdType.MESH


def places():
    dp_index, fsdp_index = lax.axis_index("dp"), lax.axis_index("fsdp")
    return dp_index, fsdp_index, fsdp_index // 2, fsdp_index % 2


def z_peer(fsdp_index, shift):
    return {"fsdp": (fsdp_index + 2 * shift) % 8}


def core_peer(fsdp_index):
    return {"fsdp": fsdp_index + 1 - 2 * (fsdp_index % 2)}


def dp_peer(dp_index, flip):
    return {"dp": dp_index ^ flip}


def greet(peers):
    barrier = pltpu.get_barrier_semaphore()
    for peer in peers:
        pl.semaphore_signal(barrier, inc=1, device_id=peer, device_id_type=MESH)
    pl.semaphore_wait(barrier, len(peers))


def remote(source, target, send_sem, recv_sem, peer):
    copy = pltpu.make_async_remote_copy(
        source, target, send_sem, recv_sem, device_id=peer, device_id_type=MESH
    )
    copy.start()
    return copy


def columns(index):
    return pl.ds(pl.multiple_of(index * LANES, LANES), LANES)


def fsdp_peers(fsdp_index):
    return [{"fsdp": (fsdp_index + shift) % 8} for shift in range(1, 8)]


def mix_begin(kind, sources, target, scratch, fsdp_index):
    sems, holds = scratch[0], scratch[1:]

    def ends(place, peer):
        if kind == "heads":
            return sources[0].at[:, :, :, columns(peer)], target.at[fsdp_index]
        mine = columns(fsdp_index)
        if len(sources[place].shape) == 4:
            return sources[place].at[peer], target.at[place, :, :, mine]
        return sources[place].at[peer], target.at[place : place + 2, :, :, mine]

    copies, stays = [], []
    for shift in (4, 5, 3, 6, 2, 7, 1):
        peer = (fsdp_index + shift) % 8
        for place in range(len(sources)):
            theirs, there = ends(place, peer)
            copies.append(
                remote(theirs, there, sems.at[0, place, shift], sems.at[1, place, shift], {"fsdp": peer})
            )
    for place in range(len(sources)):
        ours, here = ends(place, fsdp_index)
        load = pltpu.make_async_copy(ours, holds[place], sems.at[0, place, 0])
        load.start()
        stays.append((load, pltpu.make_async_copy(holds[place], here, sems.at[1, place, 0])))
    return copies, stays


def mix_own(moving):
    for load, store in moving[1]:
        load.wait()
        store.start()


def mix_end(moving):
    for load, store in moving[1]:
        store.wait()
    for copy in moving[0]:
        copy.wait()


def mix_plan(mix):
    kind, sources = mix
    bf = jnp.bfloat16
    holds, blocks = [], 0
    for array in sources:
        if kind == "heads":
            holds.append(array.shape[:3] + (array.shape[3] // 8,))
            result = (8,) + holds[0]
        else:
            holds.append(array.shape[1:])
            blocks += 1 if len(array.shape) == 4 else array.shape[1]
            result = (blocks,) + array.shape[-3:-1] + (8 * array.shape[-1],)
    scratch = [pltpu.SemaphoreType.DMA((2, len(sources), 8))] + [pltpu.VMEM(hold, bf) for hold in holds]
    return scratch, jax.ShapeDtypeStruct(result, bf)


def mix_body(kind, amount, *refs):
    sources, target, scratch = refs[:amount], refs[amount], refs[amount + 1 :]
    fsdp_index = lax.axis_index("fsdp")
    greet(fsdp_peers(fsdp_index))
    moving = mix_begin(kind, sources, target, scratch, fsdp_index)
    mix_own(moving)
    mix_end(moving)


def mix_alone(mix, collective):
    kind, sources = mix
    scratch, result = mix_plan(mix)
    return pl.pallas_call(
        functools.partial(mix_body, kind, len(sources)),
        in_specs=[ANY] * len(sources),
        out_specs=ANY,
        scratch_shapes=scratch,
        out_shape=result,
        compiler_params=comm_params(collective),
        cost_estimate=pl.CostEstimate(flops=0, bytes_accessed=30_000_000, transcendentals=0),
    )(*sources)


def send_z(unit, full, fsdp_index, dp_index, z_index, sems):
    own = full.at[z_index, dp_index]
    return [
        remote(own, own, sems[0].at[unit, shift - 1], sems[1].at[unit, shift - 1], z_peer(fsdp_index, shift))
        for shift in (1, 2, 3)
    ]


def spread(units, fulls, outs, z_copies, z_local, sems, where):
    send_sems, recv_sems, out_sems = sems
    dp_index, fsdp_index, z_index, core = where
    near_x, near_y = dp_peer(dp_index, 1), dp_peer(dp_index, 2)
    first, second, last = {}, {}, []
    for step in range(units + 2):
        if step < units:
            unit, full = step, fulls[step]
            for copy in z_copies[unit]:
                copy.wait() if z_local else copy.wait_recv()
            low, high = full.at[0:2, dp_index], full.at[2:4, dp_index]
            pairs = [(low, near_x), (high, near_y), (low, near_y), (high, near_x)]
            first[unit] = [
                remote(ref, ref, send_sems.at[unit, 3 + n], recv_sems.at[unit, 3 + n], peer)
                for n, (ref, peer) in enumerate(pairs)
            ]
        if 0 <= step - 1 < units:
            unit, full = step - 1, fulls[step - 1]
            first[unit][0].wait_recv()
            first[unit][1].wait_recv()
            low, high = full.at[0:2, dp_index ^ 1], full.at[2:4, dp_index ^ 2]
            pairs = [(low, near_y), (high, near_x)]
            second[unit] = [
                remote(ref, ref, send_sems.at[unit, 7 + n], recv_sems.at[unit, 7 + n], peer)
                for n, (ref, peer) in enumerate(pairs)
            ]
        if 0 <= step - 2 < units:
            unit, full, out = step - 2, fulls[step - 2], outs[step - 2]
            for copy in first[unit][2:] + second[unit]:
                copy.wait_recv()
            target = out.at[:, core]
            last.append(
                remote(full, target, send_sems.at[unit, 9], recv_sems.at[unit, 9], core_peer(fsdp_index))
            )
            here = pltpu.make_async_copy(full, target, out_sems.at[unit])
            here.start()
            last.append(here)
    for unit in range(units):
        for copy in first[unit] + second[unit]:
            copy.wait_send()
    for copy in last:
        copy.wait()


def first_gather_body(tiles, rows, index_ref, narrow_ref, mod_ref, out_ref, mod_out_ref, wait_ref, rest_ref, stacked, mine, full, mod_full, zoned, swap_sems, load_sems, send_sems, recv_sems, out_sems, zone_sems):
    where = places()
    dp_index, fsdp_index, z_index, core = where
    peers = [z_peer(fsdp_index, shift) for shift in (1, 2, 3)]
    peers += [dp_peer(dp_index, flip) for flip in (1, 2, 3)] + [core_peer(fsdp_index)]
    greet(peers)
    swaps = [
        remote(narrow_ref.at[:, dp_index ^ flip], stacked.at[pl.ds(4 * flip, 4)], swap_sems.at[0, flip], swap_sems.at[1, flip], dp_peer(dp_index, flip))
        for flip in (1, 2, 3)
    ]
    own = pltpu.make_async_copy(narrow_ref.at[:, dp_index], stacked.at[pl.ds(0, 4)], load_sems.at[0])
    own.start()
    mod_load = pltpu.make_async_copy(mod_ref, mod_full.at[z_index, dp_index], load_sems.at[1])
    mod_load.start()
    mod_load.wait()
    z_copies = {tiles: send_z(tiles, mod_full, fsdp_index, dp_index, z_index, (send_sems, recv_sems))}
    own.wait()
    for swap in swaps:
        swap.wait()
    for tile in range(tiles):
        full[tile, z_index, dp_index] = stacked[index_ref[tile]]
        z_copies[tile] = send_z(tile, full.at[tile], fsdp_index, dp_index, z_index, (send_sems, recv_sems))

    def take(position, carried):
        mine[position] = stacked[index_ref[position + tiles]]
        return carried

    lax.fori_loop(0, 16 - tiles, take, 0)
    early = EARLY - tiles
    zone = [
        remote(mine.at[pl.ds(0, early)], zoned.at[z_index], zone_sems.at[0, shift - 1], zone_sems.at[1, shift - 1], z_peer(fsdp_index, shift))
        for shift in (1, 2, 3)
    ]
    zone_own = pltpu.make_async_copy(mine.at[pl.ds(0, early)], wait_ref.at[z_index], load_sems.at[2])
    zone_own.start()
    rest = pltpu.make_async_copy(mine.at[pl.ds(early, 16 - EARLY)], rest_ref, load_sems.at[3])
    rest.start()
    fulls = [full.at[tile] for tile in range(tiles)] + [mod_full]
    outs = [out_ref.at[tile] for tile in range(tiles)] + [mod_out_ref]
    spread(tiles + 1, fulls, outs, z_copies, False, (send_sems, recv_sems, out_sems), where)
    for unit in range(tiles + 1):
        for copy in z_copies[unit]:
            copy.wait_send()
    for copy in zone:
        copy.wait()
    zone_own.wait()
    rest.wait()
    stores = []
    for shift in (1, 2, 3):
        z_from = (z_index + shift) % 4
        store = pltpu.make_async_copy(zoned.at[z_from], wait_ref.at[z_from], load_sems.at[3 + shift])
        store.start()
        stores.append(store)
    for store in stores:
        store.wait()


ANY = pl.BlockSpec(memory_space=pl.ANY)


def comm_params(collective):
    return pltpu.CompilerParams(
        collective_id=collective, has_side_effects=True, vmem_limit_bytes=58 * 1024 * 1024
    )


def first_gather(narrow, mod_rows, index):
    tiles = len(CHUNKS[0])
    slots, owners, rows, width = narrow.shape
    bf = jnp.bfloat16
    return pl.pallas_call(
        functools.partial(first_gather_body, tiles, rows),
        grid_spec=pltpu.PrefetchScalarGridSpec(
            num_scalar_prefetch=1,
            grid=(),
            in_specs=[ANY, ANY],
            out_specs=[ANY] * 4,
            scratch_shapes=[
                pltpu.VMEM((16, rows, width), bf),
                pltpu.VMEM((16 - tiles, rows, width), bf),
                pltpu.VMEM((tiles, 4, 4, rows, width), bf),
                pltpu.VMEM((4, 4, MOD_ROWS, width), bf),
                pltpu.VMEM((4, EARLY - tiles, rows, width), bf),
                pltpu.SemaphoreType.DMA((2, 4)),
                pltpu.SemaphoreType.DMA((8,)),
                pltpu.SemaphoreType.DMA((tiles + 1, 10)),
                pltpu.SemaphoreType.DMA((tiles + 1, 10)),
                pltpu.SemaphoreType.DMA((tiles + 1,)),
                pltpu.SemaphoreType.DMA((2, 3)),
            ],
        ),
        out_shape=[
            jax.ShapeDtypeStruct((tiles, 4, 2, 4, rows, width), bf),
            jax.ShapeDtypeStruct((4, 2, 4, MOD_ROWS, width), bf),
            jax.ShapeDtypeStruct((4, EARLY - tiles, rows, width), bf),
            jax.ShapeDtypeStruct((16 - EARLY, rows, width), bf),
        ],
        compiler_params=comm_params(0),
        cost_estimate=pl.CostEstimate(flops=0, bytes_accessed=200_000_000, transcendentals=0),
    )(index, narrow, mod_rows)


def next_gather_body(tiles, start, zoned, kind, amount, source_ref, *refs):
    mix_sources, refs = refs[:amount], refs[amount:]
    out_ref, refs = refs[0], refs[1:]
    if amount:
        mixed_ref, refs = refs[0], refs[1:]
    full, load_sems, send_sems, recv_sems, out_sems = refs[:5]
    where = places()
    dp_index, fsdp_index, z_index, core = where
    loads = []
    for tile in range(tiles):
        if zoned:
            load = pltpu.make_async_copy(source_ref.at[:, start + tile], full.at[tile, :, dp_index], load_sems.at[tile])
        else:
            load = pltpu.make_async_copy(source_ref.at[start + tile], full.at[tile, z_index, dp_index], load_sems.at[tile])
        load.start()
        loads.append(load)
    peers = [dp_peer(dp_index, flip) for flip in (1, 2)]
    if amount:
        peers += fsdp_peers(fsdp_index)
    else:
        peers += [core_peer(fsdp_index)]
        peers += [] if zoned else [z_peer(fsdp_index, shift) for shift in (1, 2, 3)]
    greet(peers)
    if amount:
        moving = mix_begin(kind, mix_sources, mixed_ref, refs[5:], fsdp_index)
    z_copies = {}
    for tile in range(tiles):
        if zoned:
            z_copies[tile] = [loads[tile]]
        else:
            loads[tile].wait()
            z_copies[tile] = send_z(tile, full.at[tile], fsdp_index, dp_index, z_index, (send_sems, recv_sems))
    if amount:
        mix_own(moving)
    fulls = [full.at[tile] for tile in range(tiles)]
    outs = [out_ref.at[tile] for tile in range(tiles)]
    spread(tiles, fulls, outs, z_copies, zoned, (send_sems, recv_sems, out_sems), where)
    if not zoned:
        for tile in range(tiles):
            for copy in z_copies[tile]:
                copy.wait_send()
    if amount:
        mix_end(moving)


def next_gather(source, tiles, start, zoned, mix, collective):
    rows, width = source.shape[-2:]
    bf = jnp.bfloat16
    kind, mix_sources = mix if mix else (None, [])
    out_shape = [jax.ShapeDtypeStruct((tiles, 4, 2, 4, rows, width), bf)]
    scratch = [
        pltpu.VMEM((tiles, 4, 4, rows, width), bf),
        pltpu.SemaphoreType.DMA((tiles,)),
        pltpu.SemaphoreType.DMA((tiles, 10)),
        pltpu.SemaphoreType.DMA((tiles, 10)),
        pltpu.SemaphoreType.DMA((tiles,)),
    ]
    if mix:
        extra, result = mix_plan(mix)
        scratch, out_shape = scratch + extra, out_shape + [result]
    results = pl.pallas_call(
        functools.partial(next_gather_body, tiles, start, zoned, kind, len(mix_sources)),
        in_specs=[ANY] * (1 + len(mix_sources)),
        out_specs=[ANY] * len(out_shape),
        scratch_shapes=scratch,
        out_shape=out_shape,
        compiler_params=comm_params(collective),
        cost_estimate=pl.CostEstimate(flops=0, bytes_accessed=tiles * 30_000_000, transcendentals=0),
    )(source, *mix_sources)
    return results[0].reshape(tiles, 32 * rows, width), (results[1] if mix else None)


def fast_layout(master):
    owners, groups = lax.axis_size("dp"), lax.axis_size("fsdp")
    return owners == 4 and groups == 8 and master.shape[1:] == (128, 1024)


def fetch_generic(master, modulation, tile_slots):
    narrow = master.astype(jnp.bfloat16)
    mod_narrow = modulation.astype(jnp.bfloat16)[:, None, None, :]
    row_blocks = lax.all_gather(narrow, "fsdp", axis=1, tiled=True)
    mod_blocks = lax.all_gather(mod_narrow, "fsdp", axis=2, tiled=True)
    gathered = lax.all_gather(row_blocks, "dp", axis=0, tiled=True)
    mod_all = lax.all_gather(mod_blocks, "dp", axis=1, tiled=True)
    chunks = [
        jnp.stack(
            [lax.dynamic_index_in_dim(gathered, tile_slots[tile], 0, keepdims=False) for tile in chunk]
        )
        for chunk in CHUNKS
    ]
    return chunks, mod_all.reshape(mod_all.shape[0], -1)


def sums_generic(logical, tile_slots):
    slot_grads = jnp.zeros((len(logical),) + logical[0].shape, jnp.bfloat16)
    for position, grad in enumerate(logical):
        slot_grads = lax.dynamic_update_index_in_dim(
            slot_grads, grad.astype(jnp.bfloat16), tile_slots[position], 0
        )
    row_sums = lax.psum_scatter(slot_grads, "fsdp", scatter_dimension=1, tiled=True)
    return lax.psum_scatter(row_sums, "dp", scatter_dimension=0, tiled=True)


def mod_generic(grad_modulation):
    owners, groups = lax.axis_size("dp"), lax.axis_size("fsdp")
    rows, width = grad_modulation.shape
    blocks = grad_modulation.reshape(rows, owners, groups, width // (owners * groups))
    sums = lax.psum_scatter(blocks.astype(jnp.bfloat16), "fsdp", scatter_dimension=2, tiled=True)
    sums = lax.psum_scatter(sums, "dp", scatter_dimension=1, tiled=True)
    return sums.reshape(rows, -1).astype(jnp.float32)


def wide(value):
    return value.astype(jnp.float32)


def reduce_scratch(tiles, rows, width):
    bf, f32 = jnp.bfloat16, jnp.float32
    return [
        pltpu.VMEM((2, tiles, 4, 4, rows, width), bf),
        pltpu.VMEM((4, tiles, 2, 2, rows, width), bf),
        pltpu.VMEM((2, tiles, 2, 2, rows, width), f32),
        pltpu.VMEM((4, tiles, 2, rows, width), bf),
        pltpu.VMEM((tiles, 4, rows, width), f32),
        pltpu.VMEM((2, 3, tiles, rows, width), bf),
        pltpu.VMEM((tiles, rows, width), bf),
        pltpu.SemaphoreType.DMA((2, tiles)),
        pltpu.SemaphoreType.DMA((8, tiles)),
        pltpu.SemaphoreType.DMA((8, tiles)),
    ]


def reduce_stages(tiles, scratch, out_ref, where):
    core_buf, swap, kept, swap_two, whole, zbuf, out_buf, load_sems, send_sems, recv_sems = scratch
    dp_index, fsdp_index, z_index, core = where
    x_bit, y_bit = dp_index % 2, dp_index // 2
    near_x, near_y = dp_peer(dp_index, 1), dp_peer(dp_index, 2)

    def moved(stage, tile):
        if stage == 1:
            ends = (swap.at[0, tile], swap.at[1, tile], near_x)
        elif stage == 2:
            ends = (swap.at[2, tile], swap.at[3, tile], near_y)
        elif stage == 3:
            ends = (swap_two.at[0, tile], swap_two.at[1, tile], near_y)
        elif stage == 4:
            ends = (swap_two.at[2, tile], swap_two.at[3, tile], near_x)
        else:
            shift = stage - 4
            ends = (zbuf.at[0, shift - 1, tile], zbuf.at[1, shift - 1, tile], z_peer(fsdp_index, shift))
        return pltpu.make_async_remote_copy(
            ends[0], ends[1], send_sems.at[stage, tile], recv_sems.at[stage, tile], device_id=ends[2], device_id_type=MESH
        )

    def both(tile, z_place, quarter):
        return wide(core_buf[0, tile, z_place, quarter]) + wide(core_buf[1, tile, z_place, quarter])

    def add_core(tile):
        for side in range(2):
            for other in range(2):
                kept[0, tile, side, other] = both(tile, side, 2 * other + x_bit)
                swap[0, tile, side, other] = both(tile, side, 2 * other + 1 - x_bit).astype(jnp.bfloat16)
                kept[1, tile, side, other] = both(tile, 2 + side, 2 * y_bit + other)
                swap[2, tile, side, other] = both(tile, 2 + side, 2 * (1 - y_bit) + other).astype(jnp.bfloat16)
        moved(1, tile).start()
        moved(2, tile).start()

    def add_first(tile):
        moved(1, tile).wait_recv()
        moved(2, tile).wait_recv()
        for side in range(2):
            whole[tile, side] = kept[0, tile, side, y_bit] + wide(swap[1, tile, side, y_bit])
            away = kept[0, tile, side, 1 - y_bit] + wide(swap[1, tile, side, 1 - y_bit])
            swap_two[0, tile, side] = away.astype(jnp.bfloat16)
            whole[tile, 2 + side] = kept[1, tile, side, x_bit] + wide(swap[3, tile, side, x_bit])
            away = kept[1, tile, side, 1 - x_bit] + wide(swap[3, tile, side, 1 - x_bit])
            swap_two[2, tile, side] = away.astype(jnp.bfloat16)
        moved(3, tile).start()
        moved(4, tile).start()

    def add_second(tile):
        moved(3, tile).wait_recv()
        moved(4, tile).wait_recv()
        for side in range(2):
            whole[tile, side] = whole[tile, side] + wide(swap_two[1, tile, side])
            whole[tile, 2 + side] = whole[tile, 2 + side] + wide(swap_two[3, tile, side])
        for shift in (1, 2, 3):
            zbuf[0, shift - 1, tile] = whole[tile, (z_index + shift) % 4].astype(jnp.bfloat16)
            moved(4 + shift, tile).start()

    def add_z(tile):
        total = whole[tile, z_index]
        for shift in (1, 2, 3):
            moved(4 + shift, tile).wait_recv()
            total = total + wide(zbuf[1, shift - 1, tile])
        out_buf[tile] = total.astype(jnp.bfloat16)

    def finish(tile):
        for stage in range(1, 8):
            moved(stage, tile).wait_send()

    return add_core, add_first, add_second, add_z, finish


def core_copies(entries, scratch, where):
    core_buf, load_sems, send_sems, recv_sems = scratch[0], scratch[-3], scratch[-2], scratch[-1]
    copies = []
    for tile, (theirs, ours) in enumerate(entries):
        away = remote(theirs, core_buf.at[1, tile], send_sems.at[0, tile], recv_sems.at[0, tile], core_peer(where[1]))
        load = pltpu.make_async_copy(ours, core_buf.at[0, tile], load_sems.at[0, tile])
        load.start()
        copies.append((away, load))
    return copies


def reduce_body(counts, extra, kind, amount, *refs):
    groups = len(counts)
    tiles = sum(counts)
    grads, refs = refs[:groups], refs[groups:]
    if extra:
        mod_grads, refs = refs[0], refs[1:]
    mix_sources, refs = refs[:amount], refs[amount:]
    out_ref, refs = refs[0], refs[1:]
    if extra:
        mod_out_ref, refs = refs[0], refs[1:]
    if amount:
        mixed_ref, refs = refs[0], refs[1:]
    scratch, refs = refs[:10], refs[10:]
    if extra:
        mod_scratch, refs = refs[:10], refs[10:]
    where = places()
    dp_index, fsdp_index, core = where[0], where[1], where[3]
    peers = [dp_peer(dp_index, flip) for flip in (1, 2)]
    if amount:
        peers += fsdp_peers(fsdp_index)
    else:
        peers += [z_peer(fsdp_index, shift) for shift in (1, 2, 3)] + [core_peer(fsdp_index)]
    greet(peers)
    if amount:
        moving = mix_begin(kind, mix_sources, mixed_ref, refs, fsdp_index)
    entries = [
        (grads[group].at[tile, :, 1 - core], grads[group].at[tile, :, core])
        for group in range(groups)
        for tile in range(counts[group])
    ]
    mod_entry = [(mod_grads.at[0, :, 1 - core], mod_grads.at[0, :, core])] if extra else []
    mod_copies = core_copies(mod_entry, mod_scratch, where) if extra else []
    copies = core_copies(entries, scratch, where)
    if amount:
        mix_own(moving)
    stages = reduce_stages(tiles, scratch, out_ref, where)
    if extra:
        mod_stages = reduce_stages(1, mod_scratch, mod_out_ref, where)
        mod_copies[0][0].wait()
        mod_copies[0][1].wait()
        mod_stages[0](0)

    def arrive(tile):
        pltpu.make_async_copy(scratch[0].at[0, tile], scratch[0].at[0, tile], scratch[-3].at[0, tile]).wait()
        pltpu.make_async_remote_copy(
            scratch[0].at[1, tile], scratch[0].at[1, tile], scratch[-2].at[0, tile], scratch[-1].at[0, tile],
            device_id=core_peer(fsdp_index), device_id_type=MESH,
        ).wait_recv()

    def step(position, carried):
        @pl.when(position < tiles)
        def _():
            arrive(position)
            stages[0](position)

        for place in (1, 2, 3):
            tile = position - place

            @pl.when((tile >= 0) & (tile < tiles))
            def _():
                stages[place](tile)

        return carried

    if extra:
        step(0, 0)
        mod_stages[1](0)
        step(1, 0)
        mod_stages[2](0)
        step(2, 0)
        mod_stages[3](0)
        lax.fori_loop(3, tiles + 3, step, 0)
        mod_stages[4](0)
    else:
        lax.fori_loop(0, tiles + 3, step, 0)

    store = pltpu.make_async_copy(scratch[6], out_ref, scratch[-3].at[1, 0])
    store.start()

    def close(tile, carried):
        stages[4](tile)
        return carried

    lax.fori_loop(0, tiles, close, 0)
    for away, load in copies:
        away.wait_send()
    if extra:
        mod_store = pltpu.make_async_copy(mod_scratch[6], mod_out_ref, mod_scratch[-3].at[1, 0])
        mod_store.start()
        mod_store.wait()
    store.wait()
    if amount:
        mix_end(moving)


def reduce_tiles(grads, mods, mix, collective):
    counts = tuple(part.shape[0] for part in grads)
    tiles = sum(counts)
    rows, width = grads[0].shape[-2:]
    bf = jnp.bfloat16
    kind, mix_sources = mix if mix else (None, [])
    operands = list(grads)
    out_shape = [jax.ShapeDtypeStruct((tiles, rows, width), bf)]
    scratch = reduce_scratch(tiles, rows, width)
    if mods is not None:
        operands.append(mods)
        out_shape.append(jax.ShapeDtypeStruct((1, MOD_ROWS, width), bf))
        scratch = scratch + reduce_scratch(1, MOD_ROWS, width)
    if mix:
        operands += list(mix_sources)
        extra, result = mix_plan(mix)
        scratch, out_shape = scratch + extra, out_shape + [result]
    return pl.pallas_call(
        functools.partial(reduce_body, counts, mods is not None, kind, len(mix_sources)),
        in_specs=[ANY] * len(operands),
        out_specs=[ANY] * len(out_shape),
        scratch_shapes=scratch,
        out_shape=out_shape,
        compiler_params=comm_params(collective),
        cost_estimate=pl.CostEstimate(flops=0, bytes_accessed=tiles * 40_000_000, transcendentals=0),
    )(*operands)


def owner_body(counts, index_ref, *refs):
    sources, refs = refs[: len(counts)], refs[len(counts) :]
    out_ref, held, picked, load_sems, send_sems, recv_sems = refs
    dp_index = lax.axis_index("dp")
    loads, start = [], 0
    for place, count in enumerate(counts):
        load = pltpu.make_async_copy(sources[place], held.at[pl.ds(start, count)], load_sems.at[place])
        load.start()
        loads.append(load)
        start += count
    greet([dp_peer(dp_index, flip) for flip in (1, 2, 3)])
    for load in loads:
        load.wait()
    copies = []
    for flip in (3, 1, 2, 0):
        for slot in range(4):
            picked[flip, slot] = held[index_ref[4 * flip + slot]]
        target = out_ref.at[:, dp_index]
        if flip:
            copies.append(
                remote(picked.at[flip], target, send_sems.at[flip], recv_sems.at[flip], dp_peer(dp_index, flip))
            )
        else:
            here = pltpu.make_async_copy(picked.at[flip], target, load_sems.at[0])
            here.start()
            copies.append(here)
    for copy in copies:
        copy.wait()


def to_owners(sums, order, tile_slots, collective):
    rows, width = sums[0].shape[-2:]
    counts = tuple(part.shape[0] for part in sums)
    dp_index = lax.axis_index("dp")
    spots = jnp.arange(16, dtype=jnp.int32)
    wanted = ((spots // 4) ^ dp_index) * 4 + spots % 4
    slots = tile_slots[jnp.array(order, jnp.int32)]
    matches = slots[None, :] == wanted[:, None]
    index = jnp.sum(jnp.where(matches, spots[None, :], 0), axis=1).astype(jnp.int32)
    bf = jnp.bfloat16
    return pl.pallas_call(
        functools.partial(owner_body, counts),
        grid_spec=pltpu.PrefetchScalarGridSpec(
            num_scalar_prefetch=1,
            grid=(),
            in_specs=[ANY] * len(counts),
            out_specs=ANY,
            scratch_shapes=[
                pltpu.VMEM((16, rows, width), bf),
                pltpu.VMEM((4, 4, rows, width), bf),
                pltpu.SemaphoreType.DMA((len(counts),)),
                pltpu.SemaphoreType.DMA((4,)),
                pltpu.SemaphoreType.DMA((4,)),
            ],
        ),
        out_shape=jax.ShapeDtypeStruct((4, 4, rows, width), bf),
        compiler_params=comm_params(collective),
        cost_estimate=pl.CostEstimate(flops=0, bytes_accessed=50_000_000, transcendentals=0),
    )(index, *sums)


def tile_sums(form, left, right):
    total = contract(form, left, right).astype(jnp.bfloat16)
    return total.reshape(-1, 4, 2, 4, total.shape[-2] // 32, total.shape[-1])


def mod_sums(grad_modulation):
    rows, width = grad_modulation.shape
    columns_here = width // 32
    blocks = grad_modulation.reshape(rows, 4, 4, 2, columns_here).transpose(2, 3, 1, 0, 4)
    flat = blocks.astype(jnp.bfloat16).reshape(1, 4, 2, 4, rows * columns_here)
    flat = jnp.pad(flat, ((0, 0),) * 4 + ((0, MOD_ROWS * 1024 - rows * columns_here),))
    return flat.reshape(1, 4, 2, 4, MOD_ROWS, 1024)


def after(value, *others):
    return lax.optimization_barrier((value,) + others)[0]


def weight_source(master, modulation, tile_slots):
    if not fast_layout(master):
        chunks, mod_all = fetch_generic(master, modulation, tile_slots)
        return (lambda number, mix, *others: (chunks[number], mix_generic(mix))), mod_all
    slots_here, row_count, width = master.shape
    dp_index = lax.axis_index("dp")
    narrow = master.astype(jnp.bfloat16).reshape(slots_here, 4, row_count // 4, width)
    index = ((tile_slots // slots_here) ^ dp_index) * slots_here + tile_slots % slots_here
    index = index[jnp.array([tile for chunk in CHUNKS for tile in chunk], jnp.int32)]
    mod_rows, mod_columns = modulation.shape
    mod_flat = modulation.astype(jnp.bfloat16).reshape(-1)
    mod_flat = jnp.pad(mod_flat, (0, MOD_ROWS * width - mod_flat.shape[0])).reshape(MOD_ROWS, width)
    first, mods, zoned, rest = first_gather(narrow, mod_flat, index)
    flat = mods.reshape(8, 4, MOD_ROWS * width)[:, :, : mod_rows * mod_columns]
    mod_all = flat.reshape(8, 4, mod_rows, mod_columns).transpose(2, 1, 0, 3).reshape(mod_rows, -1)

    def chunk(number, mix, *others):
        tiles = len(CHUNKS[number])
        if number == 0:
            return first.reshape(tiles, row_count * 8, width), None
        if number < 3:
            held = after(zoned, *others) if others else zoned
            return next_gather(held, tiles, (0, 3)[number - 1], True, mix, number)
        held = after(rest, *others) if others else rest
        return next_gather(held, tiles, (0, 4)[number - 3], False, mix, number)

    return chunk, mod_all


def exchange(pieces):
    return lax.all_to_all(pieces, "fsdp", split_axis=0, concat_axis=0, tiled=True)


def by_head(values, groups):
    blocks, objects, rows, width = values.shape
    moved = values.reshape(blocks, objects, rows, groups, width // groups)
    return moved.transpose(3, 0, 1, 2, 4)


def from_head(pieces):
    groups, blocks, objects, rows, share = pieces.shape
    return pieces.transpose(1, 2, 3, 0, 4).reshape(blocks, objects, rows, groups * share)


def mix_generic(mix):
    if mix is None:
        return None
    kind, sources = mix
    if kind == "heads":
        return exchange(by_head(sources[0], lax.axis_size("fsdp")))
    parts = [array if array.ndim == 5 else array[:, None] for array in sources]
    return from_head(exchange(jnp.concatenate(parts, axis=1)))


def adamw(weights, grads, first, second, rate):
    first_new = BETA_ONE * first + (1.0 - BETA_ONE) * grads
    second_new = BETA_TWO * second + (1.0 - BETA_TWO) * grads * grads
    first_hat = first_new / (1.0 - BETA_ONE**STEP)
    second_hat = second_new / (1.0 - BETA_TWO**STEP)
    weights_new = weights - rate * (
        first_hat / (jnp.sqrt(second_hat) + EPSILON) + WEIGHT_DECAY * weights
    )
    return (weights_new, first_new, second_new)


def shards(
    triplane,
    image_tokens,
    camera,
    view_tokens,
    master,
    moment1,
    moment2,
    tile_slots,
    modulation,
    mod_moment1,
    mod_moment2,
    cotangent,
):
    objects, tri_local, model_width = triplane.shape
    groups = lax.axis_size("fsdp")
    tri_total = tri_local * groups
    fast = fast_layout(master)
    partial_sums = tile_sums if fast else contract

    def reduced(grads, mods, mix, collective, *others):
        if not fast:
            return None, mix_generic(mix)
        grads = list(after(tuple(grads), *others)) if others else grads
        return reduce_tiles(grads, mods, mix, collective)

    chunk, mod_all = weight_source(master, modulation, tile_slots)
    mod_full = mod_all.astype(jnp.float32)
    modulations = (
        jnp.dot(camera, mod_full[:-1], precision=HIGHEST, preferred_element_type=jnp.float32)
        + mod_full[-1]
    )
    blocks = [
        modulations[:, position * model_width : (position + 1) * model_width][:, None, :]
        for position in range(9)
    ]
    tiles_pair, unused_mix = chunk(0, None)
    image_pairs = contract("oid,kde->koie", image_tokens, tiles_pair).astype(jnp.bfloat16)
    pair_sent = by_head(image_pairs, groups)
    pair_heads = exchange(pair_sent)
    tiles_qkv, unused_mix = chunk(1, None, pair_sent)
    residual_in = triplane.astype(jnp.float32)
    normed_one = modulate(residual_in, blocks[0], blocks[1]).astype(jnp.bfloat16)
    triples = contract("otd,kde->kote", normed_one, tiles_qkv).astype(jnp.bfloat16)
    tiles_mixed, triple_heads = chunk(2, ("heads", [triples]))
    tile_out_one, tile_query_two, tile_out_two = tiles_mixed[0], tiles_mixed[1], tiles_mixed[2]
    every_key = jnp.full((objects,), tri_total, jnp.int32)
    self_sources = [(triple_heads, index) for index in range(3)]
    self_result, self_logsum = attend_forward(every_key, *self_sources, tri_total, VIEW)
    tiles_up, merged_one = chunk(3, ("tokens", [self_result]))
    merged_one = merged_one[0]
    branch_one = contract("otd,de->ote", merged_one, tile_out_one)
    residual_mid = residual_in + blocks[2] * branch_one
    normed_two = modulate(residual_mid, blocks[3], blocks[4]).astype(jnp.bfloat16)
    cross_query = contract("otd,de->ote", normed_two, tile_query_two).astype(jnp.bfloat16)
    tiles_down, query_heads = chunk(4, ("heads", [cross_query[None]]))
    cross_sources = [(query_heads, 0), (pair_heads, 0), (pair_heads, 1)]
    cross_result, cross_logsum = attend_forward(view_tokens, *cross_sources, tri_total, VIEW)
    cross_mix = ("tokens", [cross_result])
    merged_two = (mix_alone(cross_mix, 11) if fast else mix_generic(cross_mix))[0]
    branch_two = contract("otd,de->ote", merged_two, tile_out_two)
    residual_late = residual_mid + blocks[5] * branch_two
    normed_three = modulate(residual_late, blocks[6], blocks[7]).astype(jnp.bfloat16)
    hidden_pre = contract("otd,kde->otke", normed_three, tiles_up)
    hidden = gelu_tanh(hidden_pre).astype(jnp.bfloat16)
    branch_three = contract("otkd,kde->ote", hidden, tiles_down)
    block_output = (residual_late + blocks[8] * branch_three).astype(jnp.bfloat16)
    grad_final = cotangent.astype(jnp.float32)
    grad_gate_three = jnp.sum(grad_final * branch_three, axis=1)
    grad_branch_three = (blocks[8] * grad_final).astype(jnp.bfloat16)
    grad_hidden = contract("ote,kde->otkd", grad_branch_three, tiles_down)
    unused_gelu, gelu_pull = jax.vjp(gelu_tanh, hidden_pre)
    grad_pre = gelu_pull(grad_hidden)[0].astype(jnp.bfloat16)
    grad_normed_three = contract("otke,kde->otd", grad_pre, tiles_up)
    grad_late_norm, grad_shift_three, grad_scale_three = modulate_back(
        residual_late, blocks[6], blocks[7], grad_normed_three
    )
    grad_late = grad_final + grad_late_norm
    grad_gate_two = jnp.sum(grad_late * branch_two, axis=1)
    grad_branch_two = (blocks[5] * grad_late).astype(jnp.bfloat16)
    grad_merged_two = contract("ote,de->otd", grad_branch_two, tile_out_two).astype(jnp.bfloat16)
    grad_down = partial_sums("otkd,ote->kde", hidden, grad_branch_three)
    grad_up = partial_sums("otd,otke->kde", normed_three, grad_pre)
    grad_out_two = partial_sums("otd,ote->de", merged_two, grad_branch_two)
    sums_down, grad_cross_heads = reduced([grad_down], None, ("heads", [grad_merged_two[None]]), 5)
    grad_query_heads, grad_pair_heads = attend_backward(
        view_tokens, *cross_sources, cross_result, cross_logsum, grad_cross_heads, VIEW
    )
    grad_pair_back = exchange(grad_pair_heads)
    sums_up, grad_query_two = reduced([grad_up], None, ("tokens", [grad_query_heads]), 6, grad_pair_heads)
    grad_query_two = grad_query_two[0]
    grad_tile_query = partial_sums("otd,ote->de", normed_two, grad_query_two)
    grad_normed_two = contract("ote,de->otd", grad_query_two, tile_query_two)
    grad_mid_norm, grad_shift_two, grad_scale_two = modulate_back(
        residual_mid, blocks[3], blocks[4], grad_normed_two
    )
    grad_mid = grad_late + grad_mid_norm
    grad_gate_one = jnp.sum(grad_mid * branch_one, axis=1)
    grad_branch_one = (blocks[2] * grad_mid).astype(jnp.bfloat16)
    grad_merged_one = contract("ote,de->otd", grad_branch_one, tile_out_one).astype(jnp.bfloat16)
    grad_out_one = partial_sums("otd,ote->de", merged_one, grad_branch_one)
    sums_mid, grad_self_heads = reduced(
        [grad_out_two, grad_tile_query], None, ("heads", [grad_merged_one[None]]), 7
    )
    grad_self_query, grad_self_pair = attend_backward(
        every_key, *self_sources, self_result, self_logsum, grad_self_heads, VIEW
    )
    grad_pairs = from_head(after(grad_pair_back, grad_self_query))
    grad_tiles_pair = partial_sums("oid,koie->kde", image_tokens, grad_pairs)
    grad_image = contract("koie,kde->oid", grad_pairs, tiles_pair)
    sums_late, grad_triples = reduced(
        [grad_tiles_pair, grad_out_one], None, ("tokens", [grad_self_query, grad_self_pair]), 8
    )
    grad_qkv = partial_sums("otd,kote->kde", normed_one, grad_triples)
    grad_normed_one = contract("kote,kde->otd", grad_triples, tiles_qkv)
    grad_in_norm, grad_shift_one, grad_scale_one = modulate_back(
        residual_in, blocks[0], blocks[1], grad_normed_one
    )
    grad_triplane = grad_mid + grad_in_norm
    grad_mods = jnp.concatenate(
        [
            grad_shift_one[:, 0],
            grad_scale_one[:, 0],
            grad_gate_one,
            grad_shift_two[:, 0],
            grad_scale_two[:, 0],
            grad_gate_two,
            grad_shift_three[:, 0],
            grad_scale_three[:, 0],
            grad_gate_three,
        ],
        axis=-1,
    )
    grad_mod_rows = jnp.dot(
        camera.T, grad_mods, precision=HIGHEST, preferred_element_type=jnp.float32
    )
    grad_modulation = jnp.concatenate(
        [grad_mod_rows, jnp.sum(grad_mods, axis=0, keepdims=True)], axis=0
    )
    if fast:
        sums_qkv, mod_sum = reduce_tiles([grad_qkv], mod_sums(grad_modulation), None, 9)
        sums = [sums_qkv, sums_late, sums_mid, sums_up, sums_down]
        order = (0, 1, 2, 5, 6, 3, 7, 4, 8, 9, 10, 11, 12, 13, 14, 15)
        tile_grad = to_owners(sums, order, tile_slots, 10).reshape(master.shape)
        mod_grad = mod_sum.reshape(-1)[: modulation.size].reshape(modulation.shape)
        tile_grad, mod_grad = tile_grad.astype(jnp.float32), mod_grad.astype(jnp.float32)
    else:
        logical = [grad_qkv[0], grad_qkv[1], grad_qkv[2], grad_out_one, grad_tile_query]
        logical = logical + [grad_tiles_pair[0], grad_tiles_pair[1], grad_out_two]
        logical = logical + [grad_up[tile] for tile in range(4)]
        logical = logical + [grad_down[tile] for tile in range(4)]
        tile_grad = sums_generic(logical, tile_slots).astype(jnp.float32)
        mod_grad = mod_generic(grad_modulation)
    new_master, new_moment1, new_moment2 = adamw(master, tile_grad, moment1, moment2, RATE_TILES)
    new_modulation, new_mod_moment1, new_mod_moment2 = adamw(
        modulation, mod_grad, mod_moment1, mod_moment2, RATE_MODULATION
    )
    return (
        block_output,
        grad_triplane,
        grad_image,
        new_master,
        new_moment1,
        new_moment2,
        new_master.astype(jnp.bfloat16),
        new_modulation,
        new_mod_moment1,
        new_mod_moment2,
    )


def solution(mesh):
    in_specs = (
        P("dp", "fsdp", None),
        P("dp", "fsdp", None),
        P("dp", None),
        P("dp"),
        P("dp", "fsdp", None),
        P("dp", "fsdp", None),
        P("dp", "fsdp", None),
        P(),
        P(None, ("dp", "fsdp")),
        P(None, ("dp", "fsdp")),
        P(None, ("dp", "fsdp")),
        P("dp", "fsdp", None),
    )
    out_specs = (
        P("dp", "fsdp", None),
        P("dp", "fsdp", None),
        P("dp", "fsdp", None),
        P("dp", "fsdp", None),
        P("dp", "fsdp", None),
        P("dp", "fsdp", None),
        P("dp", "fsdp", None),
        P(None, ("dp", "fsdp")),
        P(None, ("dp", "fsdp")),
        P(None, ("dp", "fsdp")),
    )
    return jax.shard_map(shards, mesh=mesh, in_specs=in_specs, out_specs=out_specs, check_vma=False)
```

```python
import functools

import jax
import jax.numpy as jnp
from jax import lax
from jax.experimental import pallas as pl
from jax.experimental.pallas import tpu as pltpu
from jax.sharding import PartitionSpec as P

HD = 64
STEP = 5
VIEW = 1024
LANES = 128


HIGHEST = lax.Precision.HIGHEST
NEGATIVE = -1e30
BETA_ONE = 0.5
BETA_TWO = 0.5
EPSILON = 1e-08
WEIGHT_DECAY = 0.01
RATE_TILES = 0.03
RATE_MODULATION = 0.15


def contract(form, left, right):
    return jnp.einsum(form, left, right, preferred_element_type=jnp.float32)


def layer_norm(values):
    center = values - jnp.mean(values, axis=-1, keepdims=True)
    spread = jnp.mean(center * center, axis=-1, keepdims=True)
    return center * lax.rsqrt(spread + 1e-06)


def modulate(values, shift, scale):
    return layer_norm(values) * (1.0 + scale) + shift


def modulate_back(values, shift, scale, grad_normed):
    unused, pull = jax.vjp(modulate, values, shift, scale)
    return pull(grad_normed)


def gelu_tanh(values):
    return jax.nn.gelu(values, approximate=True)


NT = (((1,), (1,)), ((), ()))
NN = (((1,), (0,)), ((), ()))
TN = (((0,), (0,)), ((), ()))


def dot(left, right, dims):
    return lax.dot_general(left, right, dims, preferred_element_type=jnp.float32)


def head_part(values, head, heads):
    if heads == 1:
        return values
    lanes = lax.broadcasted_iota(jnp.int32, values.shape, 1)
    return jnp.where(lanes // HD == head, values, jnp.zeros_like(values))


def rows_of(ref, start, amount):
    block = ref[pl.ds(start, amount), 0]
    return block.reshape(block.shape[0] * block.shape[1], block.shape[2])


def forward_body(step_rows, live_ref, q_ref, k_ref, v_ref, out_ref, lse_ref):
    key_groups, unused_one, key_rows, width = k_ref.shape
    heads = width // HD
    per_block = step_rows // key_rows
    blocks = live_ref[pl.program_id(0)] // step_rows
    queries = rows_of(q_ref, 0, q_ref.shape[0]) * jnp.bfloat16(0.125)
    result = jnp.zeros(queries.shape, jnp.float32)
    for head in range(heads):
        own = head_part(queries, head, heads)

        def step(position, carried, own=own):
            highest, total, acc = carried
            keys = rows_of(k_ref, position * per_block, per_block)
            values = rows_of(v_ref, position * per_block, per_block)
            scores = dot(own, keys, NT)
            new_highest = jnp.maximum(highest, jnp.max(scores, axis=1, keepdims=True))
            weights = jnp.exp(scores - new_highest)
            scale = jnp.exp(highest - new_highest)
            total = total * scale + jnp.sum(weights, axis=1, keepdims=True)
            acc = acc * scale + dot(weights.astype(jnp.bfloat16), values, NN)
            return (new_highest, total, acc)

        first = (
            jnp.full((own.shape[0], 1), -jnp.inf, jnp.float32),
            jnp.zeros((own.shape[0], 1), jnp.float32),
            jnp.zeros(own.shape, jnp.float32),
        )
        highest, total, acc = lax.fori_loop(0, blocks, step, first)
        result = result + head_part(acc / total, head, heads)
        level = jnp.broadcast_to(highest + jnp.log(total), (own.shape[0], 128))
        lse_ref[0, head] = jnp.transpose(level)[0:1]
    out_ref[...] = result.astype(jnp.bfloat16).reshape(out_ref.shape)


def attend_forward(live, query_source, key_source, value_source, query_block, step_rows):
    (q_array, q_at), (k_array, k_at), (v_array, v_at) = query_source, key_source, value_source
    groups, unused_blocks, objects, q_rows, width = q_array.shape
    k_rows = k_array.shape[3]
    heads = width // HD
    total_q = groups * q_rows
    per_q = query_block // q_rows
    grid = (objects, total_q // query_block)
    whole = lambda index: (lambda o, j, live: (0, index, o, 0, 0))
    part = lambda index: (lambda o, j, live: (j, index, o, 0, 0))
    return pl.pallas_call(
        functools.partial(forward_body, step_rows),
        grid_spec=pltpu.PrefetchScalarGridSpec(
            num_scalar_prefetch=1,
            grid=grid,
            in_specs=[
                pl.BlockSpec((per_q, None, 1, q_rows, width), part(q_at)),
                pl.BlockSpec((groups, None, 1, k_rows, width), whole(k_at)),
                pl.BlockSpec((groups, None, 1, k_rows, width), whole(v_at)),
            ],
            out_specs=[
                pl.BlockSpec((per_q, 1, q_rows, width), lambda o, j, live: (j, o, 0, 0)),
                pl.BlockSpec((1, heads, 1, query_block), lambda o, j, live: (o, 0, 0, j)),
            ],
        ),
        out_shape=[
            jax.ShapeDtypeStruct((groups, objects, q_rows, width), jnp.bfloat16),
            jax.ShapeDtypeStruct((objects, heads, 1, total_q), jnp.float32),
        ],
        cost_estimate=pl.CostEstimate(
            flops=4 * objects * total_q * groups * k_rows * width,
            bytes_accessed=4 * objects * groups * (q_rows + k_rows) * width,
            transcendentals=objects * heads * total_q * groups * k_rows,
        ),
    )(live, q_array, k_array, v_array)


def backward_prepare(q_ref, out_ref, grad_ref, qs, gs, delta):
    heads = qs.shape[0]
    queries = rows_of(q_ref, 0, q_ref.shape[0]) * jnp.bfloat16(0.125)
    grads = rows_of(grad_ref, 0, grad_ref.shape[0])
    outs = rows_of(out_ref, 0, out_ref.shape[0])
    product = jnp.transpose(grads.astype(jnp.float32) * outs.astype(jnp.float32))
    for head in range(heads):
        qs[head] = head_part(queries, head, heads)
        gs[head] = head_part(grads, head, heads)
        delta[head] = jnp.sum(product[head * HD : (head + 1) * HD], axis=0, keepdims=True)


def backward_block(keys, values, lse_ref, qs, gs, delta):
    heads = qs.shape[0]
    grad_q, grad_k, grad_v = None, None, None
    for head in range(heads):
        own, grads = qs[head], gs[head]
        weights = jnp.exp(dot(keys, own, NT) - lse_ref[0, head])
        grad_weights = dot(values, grads, NT)
        grad_scores = (weights * (grad_weights - delta[head])).astype(jnp.bfloat16)
        new_v = dot(weights.astype(jnp.bfloat16), grads, NN)
        new_k = dot(grad_scores, own, NN)
        new_q = dot(grad_scores, head_part(keys, head, heads), TN)
        grad_q = new_q if grad_q is None else grad_q + new_q
        grad_k = new_k if grad_k is None else grad_k + new_k
        grad_v = new_v if grad_v is None else grad_v + new_v
    return grad_q, grad_k, grad_v


def cross_backward_body(
    first_object, live_ref, q_ref, k_ref, v_ref, out_ref, lse_ref, grad_ref, dq_ref, dkv_ref, qs, gs, delta, dq_acc
):
    position = pl.program_id(1)
    width = q_ref.shape[3]
    rows = k_ref.shape[0] * k_ref.shape[2]

    @pl.when(position == 0)
    def _():
        backward_prepare(q_ref, out_ref, grad_ref, qs, gs, delta)
        dq_acc[...] = jnp.zeros_like(dq_acc)

    alive = position * rows < live_ref[pl.program_id(0) + first_object]

    @pl.when(alive)
    def _():
        keys = rows_of(k_ref, 0, k_ref.shape[0])
        values = rows_of(v_ref, 0, v_ref.shape[0])
        grad_q, grad_k, grad_v = backward_block(keys, values, lse_ref, qs, gs, delta)
        dq_acc[...] += grad_q
        shape = (k_ref.shape[0], 1, k_ref.shape[2], width)
        dkv_ref[:, 0] = grad_k.astype(jnp.bfloat16).reshape(shape)
        dkv_ref[:, 1] = grad_v.astype(jnp.bfloat16).reshape(shape)

    @pl.when(jnp.logical_not(alive))
    def _():
        dkv_ref[...] = jnp.zeros_like(dkv_ref)

    @pl.when(position == pl.num_programs(1) - 1)
    def _():
        dq_ref[...] = (dq_acc[...] * 0.125).astype(jnp.bfloat16).reshape(dq_ref.shape)


def attend_backward(live, query_source, key_source, value_source, outs, lse, grads, step_rows, span):
    (q_array, q_at), (k_array, k_at), (v_array, v_at) = query_source, key_source, value_source
    groups, unused_blocks, unused_objects, q_rows, width = q_array.shape
    first_object, objects = span
    k_rows = k_array.shape[3]
    heads = width // HD
    total_q = groups * q_rows
    per_k = max(step_rows // k_rows, 1)
    grid = (objects, groups // per_k)
    whole = lambda index: (lambda o, j, live: (0, index, o + first_object, 0, 0))
    part = lambda index: (lambda o, j, live: (j, index, o + first_object, 0, 0))
    tokens = pl.BlockSpec((groups, 1, q_rows, width), lambda o, j, live: (0, o + first_object, 0, 0))
    return pl.pallas_call(
        functools.partial(cross_backward_body, first_object),
        grid_spec=pltpu.PrefetchScalarGridSpec(
            num_scalar_prefetch=1,
            grid=grid,
            in_specs=[
                pl.BlockSpec((groups, None, 1, q_rows, width), whole(q_at)),
                pl.BlockSpec((per_k, None, 1, k_rows, width), part(k_at)),
                pl.BlockSpec((per_k, None, 1, k_rows, width), part(v_at)),
                tokens,
                pl.BlockSpec((1, heads, 1, total_q), lambda o, j, live: (o + first_object, 0, 0, 0)),
                pl.BlockSpec((groups, None, 1, q_rows, width), whole(0)),
            ],
            out_specs=[
                pl.BlockSpec((groups, 1, q_rows, width), lambda o, j, live: (0, o, 0, 0)),
                pl.BlockSpec((per_k, 2, 1, k_rows, width), lambda o, j, live: (j, 0, o, 0, 0)),
            ],
            scratch_shapes=[
                pltpu.VMEM((heads, total_q, width), jnp.bfloat16),
                pltpu.VMEM((heads, total_q, width), jnp.bfloat16),
                pltpu.VMEM((heads, 1, total_q), jnp.float32),
                pltpu.VMEM((total_q, width), jnp.float32),
            ],
        ),
        out_shape=[
            jax.ShapeDtypeStruct((groups, objects, q_rows, width), jnp.bfloat16),
            jax.ShapeDtypeStruct((groups, 2, objects, k_rows, width), jnp.bfloat16),
        ],
        cost_estimate=pl.CostEstimate(
            flops=10 * objects * total_q * groups * k_rows * width,
            bytes_accessed=8 * objects * groups * (q_rows + k_rows) * width,
            transcendentals=objects * heads * total_q * groups * k_rows,
        ),
    )(live, q_array, k_array, v_array, outs, lse, grads)

CHUNKS = ((5, 6), (0, 1, 2), (3, 4, 7), (8, 9, 10, 11), (12, 13, 14, 15))
EARLY = 8
MOD_ROWS = 16
MESH = pl.DeviceIdType.MESH


def places():
    dp_index, fsdp_index = lax.axis_index("dp"), lax.axis_index("fsdp")
    return dp_index, fsdp_index, fsdp_index // 2, fsdp_index % 2


def z_peer(fsdp_index, shift):
    return {"fsdp": (fsdp_index + 2 * shift) % 8}


def core_peer(fsdp_index):
    return {"fsdp": fsdp_index + 1 - 2 * (fsdp_index % 2)}


def dp_peer(dp_index, flip):
    return {"dp": dp_index ^ flip}


def greet(peers):
    barrier = pltpu.get_barrier_semaphore()
    for peer in peers:
        pl.semaphore_signal(barrier, inc=1, device_id=peer, device_id_type=MESH)
    pl.semaphore_wait(barrier, len(peers))


def remote(source, target, send_sem, recv_sem, peer):
    copy = pltpu.make_async_remote_copy(
        source, target, send_sem, recv_sem, device_id=peer, device_id_type=MESH
    )
    copy.start()
    return copy


def columns(index):
    return pl.ds(pl.multiple_of(index * LANES, LANES), LANES)


def fsdp_peers(fsdp_index):
    return [{"fsdp": (fsdp_index + shift) % 8} for shift in range(1, 8)]


def mix_begin(kind, sources, target, scratch, fsdp_index):
    sems, holds = scratch[0], scratch[1:]

    def ends(place, peer):
        if kind == "heads":
            return sources[0].at[:, :, :, columns(peer)], target.at[fsdp_index]
        mine = columns(fsdp_index)
        if kind == "objects":
            return sources[place].at[peer], target.at[0, place : place + 1, :, mine]
        if len(sources[place].shape) == 4:
            return sources[place].at[peer], target.at[place, :, :, mine]
        return sources[place].at[peer], target.at[place : place + 2, :, :, mine]

    copies, stays = [], []
    for shift in (4, 5, 3, 6, 2, 7, 1):
        peer = (fsdp_index + shift) % 8
        for place in range(len(sources)):
            theirs, there = ends(place, peer)
            copies.append(
                remote(theirs, there, sems.at[0, place, shift], sems.at[1, place, shift], {"fsdp": peer})
            )
    for place in range(len(sources)):
        ours, here = ends(place, fsdp_index)
        load = pltpu.make_async_copy(ours, holds[place], sems.at[0, place, 0])
        load.start()
        stays.append((load, pltpu.make_async_copy(holds[place], here, sems.at[1, place, 0])))
    return copies, stays


def mix_own(moving):
    for load, store in moving[1]:
        load.wait()
        store.start()


def mix_end(moving):
    for load, store in moving[1]:
        store.wait()
    for copy in moving[0]:
        copy.wait()


def mix_plan(mix):
    kind, sources = mix
    bf = jnp.bfloat16
    holds, blocks = [], 0
    for array in sources:
        if kind == "heads":
            holds.append(array.shape[:3] + (array.shape[3] // 8,))
            result = (8,) + holds[0]
        else:
            holds.append(array.shape[1:])
            blocks += 1 if len(array.shape) == 4 else array.shape[1]
            if kind == "objects":
                result = (1, len(sources), array.shape[2], 8 * array.shape[3])
                continue
            result = (blocks,) + array.shape[-3:-1] + (8 * array.shape[-1],)
    scratch = [pltpu.SemaphoreType.DMA((2, len(sources), 8))] + [pltpu.VMEM(hold, bf) for hold in holds]
    return scratch, jax.ShapeDtypeStruct(result, bf)


def mix_body(kind, amount, *refs):
    sources, target, scratch = refs[:amount], refs[amount], refs[amount + 1 :]
    fsdp_index = lax.axis_index("fsdp")
    greet(fsdp_peers(fsdp_index))
    moving = mix_begin(kind, sources, target, scratch, fsdp_index)
    mix_own(moving)
    mix_end(moving)


def mix_alone(mix, collective):
    kind, sources = mix
    scratch, result = mix_plan(mix)
    return pl.pallas_call(
        functools.partial(mix_body, kind, len(sources)),
        in_specs=[ANY] * len(sources),
        out_specs=ANY,
        scratch_shapes=scratch,
        out_shape=result,
        compiler_params=comm_params(collective),
        cost_estimate=pl.CostEstimate(flops=0, bytes_accessed=30_000_000, transcendentals=0),
    )(*sources)


def send_z(unit, full, fsdp_index, dp_index, z_index, sems):
    own = full.at[z_index, dp_index]
    return [
        remote(own, own, sems[0].at[unit, shift - 1], sems[1].at[unit, shift - 1], z_peer(fsdp_index, shift))
        for shift in (1, 2, 3)
    ]


def spread(units, fulls, outs, z_copies, z_local, sems, where):
    send_sems, recv_sems, out_sems = sems
    dp_index, fsdp_index, z_index, core = where
    near_x, near_y = dp_peer(dp_index, 1), dp_peer(dp_index, 2)
    first, second, last = {}, {}, []
    for step in range(units + 2):
        if step < units:
            unit, full = step, fulls[step]
            for copy in z_copies[unit]:
                copy.wait() if z_local else copy.wait_recv()
            low, high = full.at[0:2, dp_index], full.at[2:4, dp_index]
            pairs = [(low, near_x), (high, near_y), (low, near_y), (high, near_x)]
            first[unit] = [
                remote(ref, ref, send_sems.at[unit, 3 + n], recv_sems.at[unit, 3 + n], peer)
                for n, (ref, peer) in enumerate(pairs)
            ]
        if 0 <= step - 1 < units:
            unit, full = step - 1, fulls[step - 1]
            first[unit][0].wait_recv()
            first[unit][1].wait_recv()
            low, high = full.at[0:2, dp_index ^ 1], full.at[2:4, dp_index ^ 2]
            pairs = [(low, near_y), (high, near_x)]
            second[unit] = [
                remote(ref, ref, send_sems.at[unit, 7 + n], recv_sems.at[unit, 7 + n], peer)
                for n, (ref, peer) in enumerate(pairs)
            ]
        if 0 <= step - 2 < units:
            unit, full, out = step - 2, fulls[step - 2], outs[step - 2]
            for copy in first[unit][2:] + second[unit]:
                copy.wait_recv()
            target = out.at[:, core]
            last.append(
                remote(full, target, send_sems.at[unit, 9], recv_sems.at[unit, 9], core_peer(fsdp_index))
            )
            here = pltpu.make_async_copy(full, target, out_sems.at[unit])
            here.start()
            last.append(here)
    for unit in range(units):
        for copy in first[unit] + second[unit]:
            copy.wait_send()
    for copy in last:
        copy.wait()


def first_gather_body(tiles, rows, index_ref, narrow_ref, mod_ref, out_ref, mod_out_ref, wait_ref, rest_ref, stacked, mine, full, mod_full, zoned, swap_sems, load_sems, send_sems, recv_sems, out_sems, zone_sems):
    where = places()
    dp_index, fsdp_index, z_index, core = where
    peers = [z_peer(fsdp_index, shift) for shift in (1, 2, 3)]
    peers += [dp_peer(dp_index, flip) for flip in (1, 2, 3)] + [core_peer(fsdp_index)]
    greet(peers)
    swaps = [
        remote(narrow_ref.at[:, dp_index ^ flip], stacked.at[pl.ds(4 * flip, 4)], swap_sems.at[0, flip], swap_sems.at[1, flip], dp_peer(dp_index, flip))
        for flip in (1, 2, 3)
    ]
    own = pltpu.make_async_copy(narrow_ref.at[:, dp_index], stacked.at[pl.ds(0, 4)], load_sems.at[0])
    own.start()
    mod_load = pltpu.make_async_copy(mod_ref, mod_full.at[z_index, dp_index], load_sems.at[1])
    mod_load.start()
    mod_load.wait()
    z_copies = {tiles: send_z(tiles, mod_full, fsdp_index, dp_index, z_index, (send_sems, recv_sems))}
    own.wait()
    for swap in swaps:
        swap.wait()
    for tile in range(tiles):
        full[tile, z_index, dp_index] = stacked[index_ref[tile]]
        z_copies[tile] = send_z(tile, full.at[tile], fsdp_index, dp_index, z_index, (send_sems, recv_sems))

    def take(position, carried):
        mine[position] = stacked[index_ref[position + tiles]]
        return carried

    lax.fori_loop(0, 16 - tiles, take, 0)
    early = EARLY - tiles
    zone = [
        remote(mine.at[pl.ds(0, early)], zoned.at[z_index], zone_sems.at[0, shift - 1], zone_sems.at[1, shift - 1], z_peer(fsdp_index, shift))
        for shift in (1, 2, 3)
    ]
    zone_own = pltpu.make_async_copy(mine.at[pl.ds(0, early)], wait_ref.at[z_index], load_sems.at[2])
    zone_own.start()
    rest = pltpu.make_async_copy(mine.at[pl.ds(early, 16 - EARLY)], rest_ref, load_sems.at[3])
    rest.start()
    fulls = [full.at[tile] for tile in range(tiles)] + [mod_full]
    outs = [out_ref.at[tile] for tile in range(tiles)] + [mod_out_ref]
    spread(tiles + 1, fulls, outs, z_copies, False, (send_sems, recv_sems, out_sems), where)
    for unit in range(tiles + 1):
        for copy in z_copies[unit]:
            copy.wait_send()
    for copy in zone:
        copy.wait()
    zone_own.wait()
    rest.wait()
    stores = []
    for shift in (1, 2, 3):
        z_from = (z_index + shift) % 4
        store = pltpu.make_async_copy(zoned.at[z_from], wait_ref.at[z_from], load_sems.at[3 + shift])
        store.start()
        stores.append(store)
    for store in stores:
        store.wait()


ANY = pl.BlockSpec(memory_space=pl.ANY)


def comm_params(collective):
    return pltpu.CompilerParams(
        collective_id=collective, has_side_effects=True, vmem_limit_bytes=58 * 1024 * 1024
    )


def first_gather(narrow, mod_rows, index):
    tiles = len(CHUNKS[0])
    slots, owners, rows, width = narrow.shape
    bf = jnp.bfloat16
    return pl.pallas_call(
        functools.partial(first_gather_body, tiles, rows),
        grid_spec=pltpu.PrefetchScalarGridSpec(
            num_scalar_prefetch=1,
            grid=(),
            in_specs=[ANY, ANY],
            out_specs=[ANY] * 4,
            scratch_shapes=[
                pltpu.VMEM((16, rows, width), bf),
                pltpu.VMEM((16 - tiles, rows, width), bf),
                pltpu.VMEM((tiles, 4, 4, rows, width), bf),
                pltpu.VMEM((4, 4, MOD_ROWS, width), bf),
                pltpu.VMEM((4, EARLY - tiles, rows, width), bf),
                pltpu.SemaphoreType.DMA((2, 4)),
                pltpu.SemaphoreType.DMA((8,)),
                pltpu.SemaphoreType.DMA((tiles + 1, 10)),
                pltpu.SemaphoreType.DMA((tiles + 1, 10)),
                pltpu.SemaphoreType.DMA((tiles + 1,)),
                pltpu.SemaphoreType.DMA((2, 3)),
            ],
        ),
        out_shape=[
            jax.ShapeDtypeStruct((tiles, 4, 2, 4, rows, width), bf),
            jax.ShapeDtypeStruct((4, 2, 4, MOD_ROWS, width), bf),
            jax.ShapeDtypeStruct((4, EARLY - tiles, rows, width), bf),
            jax.ShapeDtypeStruct((16 - EARLY, rows, width), bf),
        ],
        compiler_params=comm_params(0),
        cost_estimate=pl.CostEstimate(flops=0, bytes_accessed=200_000_000, transcendentals=0),
    )(index, narrow, mod_rows)


def next_gather_body(tiles, start, zoned, kind, amount, ahead, source_ref, *refs):
    mix_sources, refs = refs[:amount], refs[amount:]
    out_ref, refs = refs[0], refs[1:]
    if amount:
        mixed_ref, refs = refs[0], refs[1:]
    if ahead:
        zone_ref, refs = refs[0], refs[1:]
        zone_hold, zone_sems, refs = refs[0], refs[1], refs[2:]
    full, load_sems, send_sems, recv_sems, out_sems = refs[:5]
    where = places()
    dp_index, fsdp_index, z_index, core = where
    loads = []
    for tile in range(tiles):
        if zoned:
            load = pltpu.make_async_copy(source_ref.at[:, start + tile], full.at[tile, :, dp_index], load_sems.at[tile])
        else:
            load = pltpu.make_async_copy(source_ref.at[start + tile], full.at[tile, z_index, dp_index], load_sems.at[tile])
        load.start()
        loads.append(load)
    peers = [dp_peer(dp_index, flip) for flip in (1, 2)]
    if amount:
        peers += fsdp_peers(fsdp_index)
    else:
        peers += [core_peer(fsdp_index)]
        peers += [] if zoned else [z_peer(fsdp_index, shift) for shift in (1, 2, 3)]
    greet(peers)
    z_copies = {}
    for tile in range(tiles):
        if zoned:
            z_copies[tile] = [loads[tile]]
        else:
            loads[tile].wait()
            z_copies[tile] = send_z(tile, full.at[tile], fsdp_index, dp_index, z_index, (send_sems, recv_sems))
    if amount:
        moving = mix_begin(kind, mix_sources, mixed_ref, refs[5:], fsdp_index)
        mix_own(moving)
    if ahead:
        later = source_ref.at[pl.ds(ahead[0], ahead[1])]
        zone = [
            remote(later, zone_ref.at[z_index], zone_sems.at[0, shift], zone_sems.at[1, shift], z_peer(fsdp_index, shift))
            for shift in (1, 2, 3)
        ]
        zone_load = pltpu.make_async_copy(later, zone_hold, zone_sems.at[0, 0])
        zone_load.start()
        zone_load.wait()
        zone_store = pltpu.make_async_copy(zone_hold, zone_ref.at[z_index], zone_sems.at[1, 0])
        zone_store.start()
    fulls = [full.at[tile] for tile in range(tiles)]
    outs = [out_ref.at[tile] for tile in range(tiles)]
    spread(tiles, fulls, outs, z_copies, zoned, (send_sems, recv_sems, out_sems), where)
    if not zoned:
        for tile in range(tiles):
            for copy in z_copies[tile]:
                copy.wait_send()
    if amount:
        mix_end(moving)
    if ahead:
        for copy in zone:
            copy.wait()
        zone_store.wait()


def next_gather(source, tiles, start, zoned, mix, ahead, collective):
    rows, width = source.shape[-2:]
    bf = jnp.bfloat16
    kind, mix_sources = mix if mix else (None, [])
    out_shape = [jax.ShapeDtypeStruct((tiles, 4, 2, 4, rows, width), bf)]
    scratch = [
        pltpu.VMEM((tiles, 4, 4, rows, width), bf),
        pltpu.SemaphoreType.DMA((tiles,)),
        pltpu.SemaphoreType.DMA((tiles, 10)),
        pltpu.SemaphoreType.DMA((tiles, 10)),
        pltpu.SemaphoreType.DMA((tiles,)),
    ]
    if mix:
        extra, result = mix_plan(mix)
        scratch, out_shape = scratch + extra, out_shape + [result]
    if ahead:
        scratch = [pltpu.VMEM((ahead[1], rows, width), bf), pltpu.SemaphoreType.DMA((2, 4))] + scratch
        out_shape = out_shape + [jax.ShapeDtypeStruct((4, ahead[1], rows, width), bf)]
    results = pl.pallas_call(
        functools.partial(next_gather_body, tiles, start, zoned, kind, len(mix_sources), ahead),
        in_specs=[ANY] * (1 + len(mix_sources)),
        out_specs=[ANY] * len(out_shape),
        scratch_shapes=scratch,
        out_shape=out_shape,
        compiler_params=comm_params(collective),
        cost_estimate=pl.CostEstimate(flops=0, bytes_accessed=tiles * 30_000_000, transcendentals=0),
    )(source, *mix_sources)
    mixed = results[1] if mix else None
    return results[0].reshape(tiles, 32 * rows, width), mixed, (results[-1] if ahead else None)


def fast_layout(master):
    owners, groups = lax.axis_size("dp"), lax.axis_size("fsdp")
    return owners == 4 and groups == 8 and master.shape[1:] == (128, 1024)


def fetch_generic(master, modulation, tile_slots):
    narrow = master.astype(jnp.bfloat16)
    mod_narrow = modulation.astype(jnp.bfloat16)[:, None, None, :]
    row_blocks = lax.all_gather(narrow, "fsdp", axis=1, tiled=True)
    mod_blocks = lax.all_gather(mod_narrow, "fsdp", axis=2, tiled=True)
    gathered = lax.all_gather(row_blocks, "dp", axis=0, tiled=True)
    mod_all = lax.all_gather(mod_blocks, "dp", axis=1, tiled=True)
    chunks = [
        jnp.stack(
            [lax.dynamic_index_in_dim(gathered, tile_slots[tile], 0, keepdims=False) for tile in chunk]
        )
        for chunk in CHUNKS
    ]
    return chunks, mod_all.reshape(mod_all.shape[0], -1)


def sums_generic(logical, tile_slots):
    slot_grads = jnp.zeros((len(logical),) + logical[0].shape, jnp.bfloat16)
    for position, grad in enumerate(logical):
        slot_grads = lax.dynamic_update_index_in_dim(
            slot_grads, grad.astype(jnp.bfloat16), tile_slots[position], 0
        )
    row_sums = lax.psum_scatter(slot_grads, "fsdp", scatter_dimension=1, tiled=True)
    return lax.psum_scatter(row_sums, "dp", scatter_dimension=0, tiled=True)


def mod_generic(grad_modulation):
    owners, groups = lax.axis_size("dp"), lax.axis_size("fsdp")
    rows, width = grad_modulation.shape
    blocks = grad_modulation.reshape(rows, owners, groups, width // (owners * groups))
    sums = lax.psum_scatter(blocks.astype(jnp.bfloat16), "fsdp", scatter_dimension=2, tiled=True)
    sums = lax.psum_scatter(sums, "dp", scatter_dimension=1, tiled=True)
    return sums.reshape(rows, -1).astype(jnp.float32)


def wide(value):
    return value.astype(jnp.float32)


def reduce_scratch(tiles, rows, width):
    bf, f32 = jnp.bfloat16, jnp.float32
    return [
        pltpu.VMEM((2, tiles, 4, 4, rows, width), bf),
        pltpu.VMEM((4, tiles, 2, 2, rows, width), bf),
        pltpu.VMEM((2, tiles, 2, 2, rows, width), f32),
        pltpu.VMEM((4, tiles, 2, rows, width), bf),
        pltpu.VMEM((tiles, 4, rows, width), f32),
        pltpu.VMEM((2, 3, tiles, rows, width), bf),
        pltpu.VMEM((tiles, rows, width), bf),
        pltpu.SemaphoreType.DMA((2, tiles)),
        pltpu.SemaphoreType.DMA((8, tiles)),
        pltpu.SemaphoreType.DMA((8, tiles)),
    ]


def reduce_stages(tiles, scratch, out_ref, where):
    core_buf, swap, kept, swap_two, whole, zbuf, out_buf, load_sems, send_sems, recv_sems = scratch
    dp_index, fsdp_index, z_index, core = where
    x_bit, y_bit = dp_index % 2, dp_index // 2
    near_x, near_y = dp_peer(dp_index, 1), dp_peer(dp_index, 2)

    def moved(stage, tile):
        if stage == 1:
            ends = (swap.at[0, tile], swap.at[1, tile], near_x)
        elif stage == 2:
            ends = (swap.at[2, tile], swap.at[3, tile], near_y)
        elif stage == 3:
            ends = (swap_two.at[0, tile], swap_two.at[1, tile], near_y)
        elif stage == 4:
            ends = (swap_two.at[2, tile], swap_two.at[3, tile], near_x)
        else:
            shift = stage - 4
            ends = (zbuf.at[0, shift - 1, tile], zbuf.at[1, shift - 1, tile], z_peer(fsdp_index, shift))
        return pltpu.make_async_remote_copy(
            ends[0], ends[1], send_sems.at[stage, tile], recv_sems.at[stage, tile], device_id=ends[2], device_id_type=MESH
        )

    def both(tile, z_place, quarter):
        return wide(core_buf[0, tile, z_place, quarter]) + wide(core_buf[1, tile, z_place, quarter])

    def add_core(tile):
        for side in range(2):
            for other in range(2):
                kept[0, tile, side, other] = both(tile, side, 2 * other + x_bit)
                swap[0, tile, side, other] = both(tile, side, 2 * other + 1 - x_bit).astype(jnp.bfloat16)
                kept[1, tile, side, other] = both(tile, 2 + side, 2 * y_bit + other)
                swap[2, tile, side, other] = both(tile, 2 + side, 2 * (1 - y_bit) + other).astype(jnp.bfloat16)
        moved(1, tile).start()
        moved(2, tile).start()

    def add_first(tile):
        moved(1, tile).wait_recv()
        moved(2, tile).wait_recv()
        for side in range(2):
            whole[tile, side] = kept[0, tile, side, y_bit] + wide(swap[1, tile, side, y_bit])
            away = kept[0, tile, side, 1 - y_bit] + wide(swap[1, tile, side, 1 - y_bit])
            swap_two[0, tile, side] = away.astype(jnp.bfloat16)
            whole[tile, 2 + side] = kept[1, tile, side, x_bit] + wide(swap[3, tile, side, x_bit])
            away = kept[1, tile, side, 1 - x_bit] + wide(swap[3, tile, side, 1 - x_bit])
            swap_two[2, tile, side] = away.astype(jnp.bfloat16)
        moved(3, tile).start()
        moved(4, tile).start()

    def add_second(tile):
        moved(3, tile).wait_recv()
        moved(4, tile).wait_recv()
        for side in range(2):
            whole[tile, side] = whole[tile, side] + wide(swap_two[1, tile, side])
            whole[tile, 2 + side] = whole[tile, 2 + side] + wide(swap_two[3, tile, side])
        for shift in (1, 2, 3):
            zbuf[0, shift - 1, tile] = whole[tile, (z_index + shift) % 4].astype(jnp.bfloat16)
            moved(4 + shift, tile).start()

    def add_z(tile):
        total = whole[tile, z_index]
        for shift in (1, 2, 3):
            moved(4 + shift, tile).wait_recv()
            total = total + wide(zbuf[1, shift - 1, tile])
        out_buf[tile] = total.astype(jnp.bfloat16)

    def finish(tile):
        for stage in range(1, 8):
            moved(stage, tile).wait_send()

    return add_core, add_first, add_second, add_z, finish


def core_copies(entries, scratch, where):
    core_buf, load_sems, send_sems, recv_sems = scratch[0], scratch[-3], scratch[-2], scratch[-1]
    copies = []
    for tile, (theirs, ours) in enumerate(entries):
        away = remote(theirs, core_buf.at[1, tile], send_sems.at[0, tile], recv_sems.at[0, tile], core_peer(where[1]))
        load = pltpu.make_async_copy(ours, core_buf.at[0, tile], load_sems.at[0, tile])
        load.start()
        copies.append((away, load))
    return copies


def reduce_body(counts, extra, plans, *refs):
    groups = len(counts)
    tiles = sum(counts)
    grads, refs = refs[:groups], refs[groups:]
    if extra:
        mod_grads, refs = refs[0], refs[1:]
    mix_sources = []
    for unused_kind, amount in plans:
        mix_sources.append(refs[:amount])
        refs = refs[amount:]
    out_ref, refs = refs[0], refs[1:]
    if extra:
        mod_out_ref, refs = refs[0], refs[1:]
    mixed_refs, refs = refs[: len(plans)], refs[len(plans) :]
    scratch, refs = refs[:10], refs[10:]
    if extra:
        mod_scratch, refs = refs[:10], refs[10:]
    where = places()
    dp_index, fsdp_index, core = where[0], where[1], where[3]
    peers = [dp_peer(dp_index, flip) for flip in (1, 2)]
    if plans:
        peers += fsdp_peers(fsdp_index)
    else:
        peers += [z_peer(fsdp_index, shift) for shift in (1, 2, 3)] + [core_peer(fsdp_index)]
    greet(peers)
    movings = []
    for place, (kind, amount) in enumerate(plans):
        mix_scratch, refs = refs[: 1 + amount], refs[1 + amount :]
        movings.append(mix_begin(kind, mix_sources[place], mixed_refs[place], mix_scratch, fsdp_index))
    entries = [
        (grads[group].at[tile, :, 1 - core], grads[group].at[tile, :, core])
        for group in range(groups)
        for tile in range(counts[group])
    ]
    mod_entry = [(mod_grads.at[0, :, 1 - core], mod_grads.at[0, :, core])] if extra else []
    mod_copies = core_copies(mod_entry, mod_scratch, where) if extra else []
    copies = core_copies(entries, scratch, where)
    for moving in movings:
        mix_own(moving)
    stages = reduce_stages(tiles, scratch, out_ref, where)
    if extra:
        mod_stages = reduce_stages(1, mod_scratch, mod_out_ref, where)
        mod_copies[0][0].wait()
        mod_copies[0][1].wait()
        mod_stages[0](0)

    def arrive(tile):
        pltpu.make_async_copy(scratch[0].at[0, tile], scratch[0].at[0, tile], scratch[-3].at[0, tile]).wait()
        pltpu.make_async_remote_copy(
            scratch[0].at[1, tile], scratch[0].at[1, tile], scratch[-2].at[0, tile], scratch[-1].at[0, tile],
            device_id=core_peer(fsdp_index), device_id_type=MESH,
        ).wait_recv()

    def step(position, carried):
        @pl.when(position < tiles)
        def _():
            arrive(position)
            stages[0](position)

        for place in (1, 2, 3):
            tile = position - place

            @pl.when((tile >= 0) & (tile < tiles))
            def _():
                stages[place](tile)

        return carried

    if extra:
        step(0, 0)
        mod_stages[1](0)
        step(1, 0)
        mod_stages[2](0)
        step(2, 0)
        mod_stages[3](0)
        lax.fori_loop(3, tiles + 3, step, 0)
        mod_stages[4](0)
    else:
        lax.fori_loop(0, tiles + 3, step, 0)

    store = pltpu.make_async_copy(scratch[6], out_ref, scratch[-3].at[1, 0])
    store.start()

    def close(tile, carried):
        stages[4](tile)
        return carried

    lax.fori_loop(0, tiles, close, 0)
    for away, load in copies:
        away.wait_send()
    if extra:
        mod_store = pltpu.make_async_copy(mod_scratch[6], mod_out_ref, mod_scratch[-3].at[1, 0])
        mod_store.start()
        mod_store.wait()
    store.wait()
    for moving in movings:
        mix_end(moving)


def reduce_tiles(grads, mods, mixes, collective):
    counts = tuple(part.shape[0] for part in grads)
    tiles = sum(counts)
    rows, width = grads[0].shape[-2:]
    bf = jnp.bfloat16
    operands = list(grads)
    out_shape = [jax.ShapeDtypeStruct((tiles, rows, width), bf)]
    scratch = reduce_scratch(tiles, rows, width)
    if mods is not None:
        operands.append(mods)
        out_shape.append(jax.ShapeDtypeStruct((1, MOD_ROWS, width), bf))
        scratch = scratch + reduce_scratch(1, MOD_ROWS, width)
    for mix in mixes:
        operands += list(mix[1])
        extra, result = mix_plan(mix)
        scratch, out_shape = scratch + extra, out_shape + [result]
    plans = tuple((kind, len(sources)) for kind, sources in mixes)
    return pl.pallas_call(
        functools.partial(reduce_body, counts, mods is not None, plans),
        in_specs=[ANY] * len(operands),
        out_specs=[ANY] * len(out_shape),
        scratch_shapes=scratch,
        out_shape=out_shape,
        compiler_params=comm_params(collective),
        cost_estimate=pl.CostEstimate(flops=0, bytes_accessed=tiles * 40_000_000, transcendentals=0),
    )(*operands)


def owner_body(counts, index_ref, *refs):
    sources, refs = refs[: len(counts)], refs[len(counts) :]
    out_ref, held, picked, load_sems, send_sems, recv_sems = refs
    dp_index = lax.axis_index("dp")
    loads, start = [], 0
    for place, count in enumerate(counts):
        load = pltpu.make_async_copy(sources[place], held.at[pl.ds(start, count)], load_sems.at[place])
        load.start()
        loads.append(load)
        start += count
    greet([dp_peer(dp_index, flip) for flip in (1, 2, 3)])
    for load in loads:
        load.wait()
    copies = []
    for flip in (3, 1, 2, 0):
        for slot in range(4):
            picked[flip, slot] = held[index_ref[4 * flip + slot]]
        target = out_ref.at[:, dp_index]
        if flip:
            copies.append(
                remote(picked.at[flip], target, send_sems.at[flip], recv_sems.at[flip], dp_peer(dp_index, flip))
            )
        else:
            here = pltpu.make_async_copy(picked.at[flip], target, load_sems.at[0])
            here.start()
            copies.append(here)
    for copy in copies:
        copy.wait()


def to_owners(sums, order, tile_slots, collective):
    rows, width = sums[0].shape[-2:]
    counts = tuple(part.shape[0] for part in sums)
    dp_index = lax.axis_index("dp")
    spots = jnp.arange(16, dtype=jnp.int32)
    wanted = ((spots // 4) ^ dp_index) * 4 + spots % 4
    slots = tile_slots[jnp.array(order, jnp.int32)]
    matches = slots[None, :] == wanted[:, None]
    index = jnp.sum(jnp.where(matches, spots[None, :], 0), axis=1).astype(jnp.int32)
    bf = jnp.bfloat16
    return pl.pallas_call(
        functools.partial(owner_body, counts),
        grid_spec=pltpu.PrefetchScalarGridSpec(
            num_scalar_prefetch=1,
            grid=(),
            in_specs=[ANY] * len(counts),
            out_specs=ANY,
            scratch_shapes=[
                pltpu.VMEM((16, rows, width), bf),
                pltpu.VMEM((4, 4, rows, width), bf),
                pltpu.SemaphoreType.DMA((len(counts),)),
                pltpu.SemaphoreType.DMA((4,)),
                pltpu.SemaphoreType.DMA((4,)),
            ],
        ),
        out_shape=jax.ShapeDtypeStruct((4, 4, rows, width), bf),
        compiler_params=comm_params(collective),
        cost_estimate=pl.CostEstimate(flops=0, bytes_accessed=50_000_000, transcendentals=0),
    )(index, *sums)


def tile_sums(form, left, right):
    total = contract(form, left, right).astype(jnp.bfloat16)
    return total.reshape(-1, 4, 2, 4, total.shape[-2] // 32, total.shape[-1])


def mod_sums(grad_modulation):
    rows, width = grad_modulation.shape
    columns_here = width // 32
    blocks = grad_modulation.reshape(rows, 4, 4, 2, columns_here).transpose(2, 3, 1, 0, 4)
    flat = blocks.astype(jnp.bfloat16).reshape(1, 4, 2, 4, rows * columns_here)
    flat = jnp.pad(flat, ((0, 0),) * 4 + ((0, MOD_ROWS * 1024 - rows * columns_here),))
    return flat.reshape(1, 4, 2, 4, MOD_ROWS, 1024)


def after(value, *others):
    return lax.optimization_barrier((value,) + others)[0]


def weight_source(master, modulation, tile_slots):
    if not fast_layout(master):
        chunks, mod_all = fetch_generic(master, modulation, tile_slots)
        return (lambda number, mix, *others: (chunks[number], mix_generic(mix))), mod_all
    slots_here, row_count, width = master.shape
    dp_index = lax.axis_index("dp")
    narrow = master.astype(jnp.bfloat16).reshape(slots_here, 4, row_count // 4, width)
    index = ((tile_slots // slots_here) ^ dp_index) * slots_here + tile_slots % slots_here
    index = index[jnp.array([tile for chunk in CHUNKS for tile in chunk], jnp.int32)]
    mod_rows, mod_columns = modulation.shape
    mod_flat = modulation.astype(jnp.bfloat16).reshape(-1)
    mod_flat = jnp.pad(mod_flat, (0, MOD_ROWS * width - mod_flat.shape[0])).reshape(MOD_ROWS, width)
    first, mods, zoned, rest = first_gather(narrow, mod_flat, index)
    flat = mods.reshape(8, 4, MOD_ROWS * width)[:, :, : mod_rows * mod_columns]
    mod_all = flat.reshape(8, 4, mod_rows, mod_columns).transpose(2, 1, 0, 3).reshape(mod_rows, -1)

    last_zone = []

    def chunk(number, mix, *others):
        tiles = len(CHUNKS[number])
        if number == 0:
            return first.reshape(tiles, row_count * 8, width), None
        if number < 3:
            held = after(zoned, *others) if others else zoned
            return next_gather(held, tiles, (0, 3)[number - 1], True, mix, None, number)[:2]
        if number == 3:
            full, mixed, zone = next_gather(rest, tiles, 0, False, mix, (tiles, 16 - EARLY - tiles), number)
            last_zone.append(zone)
            return full, mixed
        return next_gather(last_zone[0], tiles, 0, True, mix, None, number)[:2]

    return chunk, mod_all


def exchange(pieces):
    return lax.all_to_all(pieces, "fsdp", split_axis=0, concat_axis=0, tiled=True)


def by_head(values, groups):
    blocks, objects, rows, width = values.shape
    moved = values.reshape(blocks, objects, rows, groups, width // groups)
    return moved.transpose(3, 0, 1, 2, 4)


def from_head(pieces):
    groups, blocks, objects, rows, share = pieces.shape
    return pieces.transpose(1, 2, 3, 0, 4).reshape(blocks, objects, rows, groups * share)


def mix_generic(mix):
    if mix is None:
        return None
    kind, sources = mix
    if kind == "heads":
        return exchange(by_head(sources[0], lax.axis_size("fsdp")))
    if kind == "objects":
        sources = [jnp.concatenate(sources, axis=1)]
    parts = [array if array.ndim == 5 else array[:, None] for array in sources]
    return from_head(exchange(jnp.concatenate(parts, axis=1)))


def adamw(weights, grads, first, second, rate):
    first_new = BETA_ONE * first + (1.0 - BETA_ONE) * grads
    second_new = BETA_TWO * second + (1.0 - BETA_TWO) * grads * grads
    first_hat = first_new / (1.0 - BETA_ONE**STEP)
    second_hat = second_new / (1.0 - BETA_TWO**STEP)
    weights_new = weights - rate * (
        first_hat / (jnp.sqrt(second_hat) + EPSILON) + WEIGHT_DECAY * weights
    )
    return (weights_new, first_new, second_new)


def shards(
    triplane,
    image_tokens,
    camera,
    view_tokens,
    master,
    moment1,
    moment2,
    tile_slots,
    modulation,
    mod_moment1,
    mod_moment2,
    cotangent,
):
    objects, tri_local, model_width = triplane.shape
    groups = lax.axis_size("fsdp")
    tri_total = tri_local * groups
    fast = fast_layout(master)
    partial_sums = tile_sums if fast else contract

    def reduced(grads, mods, mixes, collective):
        if not fast:
            return [None] + [mix_generic(mix) for mix in mixes]
        return reduce_tiles(grads, mods, mixes, collective)

    chunk, mod_all = weight_source(master, modulation, tile_slots)
    mod_full = mod_all.astype(jnp.float32)
    modulations = (
        jnp.dot(camera, mod_full[:-1], precision=HIGHEST, preferred_element_type=jnp.float32)
        + mod_full[-1]
    )
    blocks = [
        modulations[:, position * model_width : (position + 1) * model_width][:, None, :]
        for position in range(9)
    ]
    tiles_pair, unused_mix = chunk(0, None)
    image_pairs = contract("oid,kde->koie", image_tokens, tiles_pair).astype(jnp.bfloat16)
    pair_sent = by_head(image_pairs, groups)
    pair_heads = exchange(pair_sent)
    tiles_qkv, unused_mix = chunk(1, None, pair_sent)
    residual_in = triplane.astype(jnp.float32)
    normed_one = modulate(residual_in, blocks[0], blocks[1]).astype(jnp.bfloat16)
    triples = contract("otd,kde->kote", normed_one, tiles_qkv).astype(jnp.bfloat16)
    tiles_mixed, triple_heads = chunk(2, ("heads", [triples]))
    tile_out_one, tile_query_two, tile_out_two = tiles_mixed[0], tiles_mixed[1], tiles_mixed[2]
    every_key = jnp.full((objects,), tri_total, jnp.int32)
    self_sources = [(triple_heads, index) for index in range(3)]
    self_result, self_logsum = attend_forward(every_key, *self_sources, tri_total, VIEW)
    tiles_up, merged_one = chunk(3, ("tokens", [self_result]))
    merged_one = merged_one[0]
    branch_one = contract("otd,de->ote", merged_one, tile_out_one)
    residual_mid = residual_in + blocks[2] * branch_one
    normed_two = modulate(residual_mid, blocks[3], blocks[4]).astype(jnp.bfloat16)
    cross_query = contract("otd,de->ote", normed_two, tile_query_two).astype(jnp.bfloat16)
    tiles_down, query_heads = chunk(4, ("heads", [cross_query[None]]))
    cross_sources = [(query_heads, 0), (pair_heads, 0), (pair_heads, 1)]
    cross_result, cross_logsum = attend_forward(view_tokens, *cross_sources, tri_total, VIEW)
    cross_mix = ("tokens", [cross_result])
    merged_two = (mix_alone(cross_mix, 11) if fast else mix_generic(cross_mix))[0]
    branch_two = contract("otd,de->ote", merged_two, tile_out_two)
    residual_late = residual_mid + blocks[5] * branch_two
    normed_three = modulate(residual_late, blocks[6], blocks[7]).astype(jnp.bfloat16)
    hidden_pre = contract("otd,kde->otke", normed_three, tiles_up)
    hidden = gelu_tanh(hidden_pre).astype(jnp.bfloat16)
    branch_three = contract("otkd,kde->ote", hidden, tiles_down)
    block_output = (residual_late + blocks[8] * branch_three).astype(jnp.bfloat16)
    grad_final = cotangent.astype(jnp.float32)
    grad_gate_three = jnp.sum(grad_final * branch_three, axis=1)
    grad_branch_three = (blocks[8] * grad_final).astype(jnp.bfloat16)
    grad_hidden = contract("ote,kde->otkd", grad_branch_three, tiles_down)
    unused_gelu, gelu_pull = jax.vjp(gelu_tanh, hidden_pre)
    grad_pre = gelu_pull(grad_hidden)[0].astype(jnp.bfloat16)
    grad_normed_three = contract("otke,kde->otd", grad_pre, tiles_up)
    grad_late_norm, grad_shift_three, grad_scale_three = modulate_back(
        residual_late, blocks[6], blocks[7], grad_normed_three
    )
    grad_late = grad_final + grad_late_norm
    grad_gate_two = jnp.sum(grad_late * branch_two, axis=1)
    grad_branch_two = (blocks[5] * grad_late).astype(jnp.bfloat16)
    grad_merged_two = contract("ote,de->otd", grad_branch_two, tile_out_two).astype(jnp.bfloat16)
    grad_down = partial_sums("otkd,ote->kde", hidden, grad_branch_three)
    grad_up = partial_sums("otd,otke->kde", normed_three, grad_pre)
    grad_out_two = partial_sums("otd,ote->de", merged_two, grad_branch_two)
    sums_down, grad_cross_heads = reduced([grad_down], None, [("heads", [grad_merged_two[None]])], 5)
    grad_query_heads, grad_pair_heads = [], []
    for place in range(objects):
        query_part, pair_part = attend_backward(
            view_tokens, *cross_sources, cross_result, cross_logsum, grad_cross_heads, VIEW, (place, 1)
        )
        grad_query_heads.append(query_part)
        grad_pair_heads.append(pair_part)
    half = objects // 2
    pair_mixes = [("tokens", [part]) for part in grad_pair_heads]
    sums_up, grad_query_two, *grad_pairs = reduced(
        [grad_up], None, [("objects", grad_query_heads)] + pair_mixes[:half], 6
    )
    grad_query_two = grad_query_two[0]
    grad_tile_query = partial_sums("otd,ote->de", normed_two, grad_query_two)
    grad_normed_two = contract("ote,de->otd", grad_query_two, tile_query_two)
    grad_mid_norm, grad_shift_two, grad_scale_two = modulate_back(
        residual_mid, blocks[3], blocks[4], grad_normed_two
    )
    grad_mid = grad_late + grad_mid_norm
    grad_gate_one = jnp.sum(grad_mid * branch_one, axis=1)
    grad_branch_one = (blocks[2] * grad_mid).astype(jnp.bfloat16)
    grad_merged_one = contract("ote,de->otd", grad_branch_one, tile_out_one).astype(jnp.bfloat16)
    grad_out_one = partial_sums("otd,ote->de", merged_one, grad_branch_one)
    sums_mid, grad_self_heads, *more_pairs = reduced(
        [grad_out_two, grad_tile_query], None, [("heads", [grad_merged_one[None]])] + pair_mixes[half:], 7
    )
    grad_self_query, grad_self_pair = attend_backward(
        every_key, *self_sources, self_result, self_logsum, grad_self_heads, VIEW, (0, objects)
    )
    grad_pairs = jnp.concatenate(grad_pairs + more_pairs, axis=1)
    grad_tiles_pair = partial_sums("oid,koie->kde", image_tokens, grad_pairs)
    grad_image = contract("koie,kde->oid", grad_pairs, tiles_pair)
    sums_late, grad_triples = reduced(
        [grad_tiles_pair, grad_out_one], None, [("tokens", [grad_self_query, grad_self_pair])], 8
    )
    grad_qkv = partial_sums("otd,kote->kde", normed_one, grad_triples)
    grad_normed_one = contract("kote,kde->otd", grad_triples, tiles_qkv)
    grad_in_norm, grad_shift_one, grad_scale_one = modulate_back(
        residual_in, blocks[0], blocks[1], grad_normed_one
    )
    grad_triplane = grad_mid + grad_in_norm
    grad_mods = jnp.concatenate(
        [
            grad_shift_one[:, 0],
            grad_scale_one[:, 0],
            grad_gate_one,
            grad_shift_two[:, 0],
            grad_scale_two[:, 0],
            grad_gate_two,
            grad_shift_three[:, 0],
            grad_scale_three[:, 0],
            grad_gate_three,
        ],
        axis=-1,
    )
    grad_mod_rows = jnp.dot(
        camera.T, grad_mods, precision=HIGHEST, preferred_element_type=jnp.float32
    )
    grad_modulation = jnp.concatenate(
        [grad_mod_rows, jnp.sum(grad_mods, axis=0, keepdims=True)], axis=0
    )
    if fast:
        sums_qkv, mod_sum = reduce_tiles([grad_qkv], mod_sums(grad_modulation), [], 9)
        sums = [sums_qkv, sums_late, sums_mid, sums_up, sums_down]
        order = (0, 1, 2, 5, 6, 3, 7, 4, 8, 9, 10, 11, 12, 13, 14, 15)
        tile_grad = to_owners(sums, order, tile_slots, 10).reshape(master.shape)
        mod_grad = mod_sum.reshape(-1)[: modulation.size].reshape(modulation.shape)
        tile_grad, mod_grad = tile_grad.astype(jnp.float32), mod_grad.astype(jnp.float32)
    else:
        logical = [grad_qkv[0], grad_qkv[1], grad_qkv[2], grad_out_one, grad_tile_query]
        logical = logical + [grad_tiles_pair[0], grad_tiles_pair[1], grad_out_two]
        logical = logical + [grad_up[tile] for tile in range(4)]
        logical = logical + [grad_down[tile] for tile in range(4)]
        tile_grad = sums_generic(logical, tile_slots).astype(jnp.float32)
        mod_grad = mod_generic(grad_modulation)
    new_master, new_moment1, new_moment2 = adamw(master, tile_grad, moment1, moment2, RATE_TILES)
    new_modulation, new_mod_moment1, new_mod_moment2 = adamw(
        modulation, mod_grad, mod_moment1, mod_moment2, RATE_MODULATION
    )
    return (
        block_output,
        grad_triplane,
        grad_image,
        new_master,
        new_moment1,
        new_moment2,
        new_master.astype(jnp.bfloat16),
        new_modulation,
        new_mod_moment1,
        new_mod_moment2,
    )


def solution(mesh):
    in_specs = (
        P("dp", "fsdp", None),
        P("dp", "fsdp", None),
        P("dp", None),
        P("dp"),
        P("dp", "fsdp", None),
        P("dp", "fsdp", None),
        P("dp", "fsdp", None),
        P(),
        P(None, ("dp", "fsdp")),
        P(None, ("dp", "fsdp")),
        P(None, ("dp", "fsdp")),
        P("dp", "fsdp", None),
    )
    out_specs = (
        P("dp", "fsdp", None),
        P("dp", "fsdp", None),
        P("dp", "fsdp", None),
        P("dp", "fsdp", None),
        P("dp", "fsdp", None),
        P("dp", "fsdp", None),
        P("dp", "fsdp", None),
        P(None, ("dp", "fsdp")),
        P(None, ("dp", "fsdp")),
        P(None, ("dp", "fsdp")),
    )
    return jax.shard_map(shards, mesh=mesh, in_specs=in_specs, out_specs=out_specs, check_vma=False)
```

```python
import functools

import jax
import jax.numpy as jnp
from jax import lax
from jax.experimental import pallas as pl
from jax.experimental.pallas import tpu as pltpu
from jax.sharding import PartitionSpec as P

HD = 64
STEP = 5
VIEW = 1024
LANES = 128


HIGHEST = lax.Precision.HIGHEST
NEGATIVE = -1e30
BETA_ONE = 0.5
BETA_TWO = 0.5
EPSILON = 1e-08
WEIGHT_DECAY = 0.01
RATE_TILES = 0.03
RATE_MODULATION = 0.15


def contract(form, left, right):
    return jnp.einsum(form, left, right, preferred_element_type=jnp.float32)


def layer_norm(values):
    center = values - jnp.mean(values, axis=-1, keepdims=True)
    spread = jnp.mean(center * center, axis=-1, keepdims=True)
    return center * lax.rsqrt(spread + 1e-06)


def modulate(values, shift, scale):
    return layer_norm(values) * (1.0 + scale) + shift


def modulate_back(values, shift, scale, grad_normed):
    unused, pull = jax.vjp(modulate, values, shift, scale)
    return pull(grad_normed)


def gelu_tanh(values):
    return jax.nn.gelu(values, approximate=True)


NT = (((1,), (1,)), ((), ()))
NN = (((1,), (0,)), ((), ()))
TN = (((0,), (0,)), ((), ()))


def dot(left, right, dims):
    return lax.dot_general(left, right, dims, preferred_element_type=jnp.float32)


def head_part(values, head, heads):
    if heads == 1:
        return values
    lanes = lax.broadcasted_iota(jnp.int32, values.shape, 1)
    return jnp.where(lanes // HD == head, values, jnp.zeros_like(values))


def rows_of(ref, start, amount):
    block = ref[pl.ds(start, amount), 0]
    return block.reshape(block.shape[0] * block.shape[1], block.shape[2])


def forward_body(step_rows, live_ref, q_ref, k_ref, v_ref, out_ref, lse_ref):
    key_groups, unused_one, key_rows, width = k_ref.shape
    heads = width // HD
    per_block = step_rows // key_rows
    blocks = live_ref[pl.program_id(0)] // step_rows
    queries = rows_of(q_ref, 0, q_ref.shape[0]) * jnp.bfloat16(0.125)
    result = jnp.zeros(queries.shape, jnp.float32)
    for head in range(heads):
        own = head_part(queries, head, heads)

        def step(position, carried, own=own):
            highest, total, acc = carried
            keys = rows_of(k_ref, position * per_block, per_block)
            values = rows_of(v_ref, position * per_block, per_block)
            scores = dot(own, keys, NT)
            new_highest = jnp.maximum(highest, jnp.max(scores, axis=1, keepdims=True))
            weights = jnp.exp(scores - new_highest)
            scale = jnp.exp(highest - new_highest)
            total = total * scale + jnp.sum(weights, axis=1, keepdims=True)
            acc = acc * scale + dot(weights.astype(jnp.bfloat16), values, NN)
            return (new_highest, total, acc)

        first = (
            jnp.full((own.shape[0], 1), -jnp.inf, jnp.float32),
            jnp.zeros((own.shape[0], 1), jnp.float32),
            jnp.zeros(own.shape, jnp.float32),
        )
        highest, total, acc = lax.fori_loop(0, blocks, step, first)
        result = result + head_part(acc / total, head, heads)
        level = jnp.broadcast_to(highest + jnp.log(total), (own.shape[0], 128))
        lse_ref[0, head] = jnp.transpose(level)[0:1]
    out_ref[...] = result.astype(jnp.bfloat16).reshape(out_ref.shape)


def attend_forward(live, query_source, key_source, value_source, query_block, step_rows):
    (q_array, q_at), (k_array, k_at), (v_array, v_at) = query_source, key_source, value_source
    groups, unused_blocks, objects, q_rows, width = q_array.shape
    k_rows = k_array.shape[3]
    heads = width // HD
    total_q = groups * q_rows
    per_q = query_block // q_rows
    grid = (objects, total_q // query_block)
    whole = lambda index: (lambda o, j, live: (0, index, o, 0, 0))
    part = lambda index: (lambda o, j, live: (j, index, o, 0, 0))
    return pl.pallas_call(
        functools.partial(forward_body, step_rows),
        grid_spec=pltpu.PrefetchScalarGridSpec(
            num_scalar_prefetch=1,
            grid=grid,
            in_specs=[
                pl.BlockSpec((per_q, None, 1, q_rows, width), part(q_at)),
                pl.BlockSpec((groups, None, 1, k_rows, width), whole(k_at)),
                pl.BlockSpec((groups, None, 1, k_rows, width), whole(v_at)),
            ],
            out_specs=[
                pl.BlockSpec((per_q, 1, q_rows, width), lambda o, j, live: (j, o, 0, 0)),
                pl.BlockSpec((1, heads, 1, query_block), lambda o, j, live: (o, 0, 0, j)),
            ],
        ),
        out_shape=[
            jax.ShapeDtypeStruct((groups, objects, q_rows, width), jnp.bfloat16),
            jax.ShapeDtypeStruct((objects, heads, 1, total_q), jnp.float32),
        ],
        cost_estimate=pl.CostEstimate(
            flops=4 * objects * total_q * groups * k_rows * width,
            bytes_accessed=4 * objects * groups * (q_rows + k_rows) * width,
            transcendentals=objects * heads * total_q * groups * k_rows,
        ),
    )(live, q_array, k_array, v_array)


def backward_prepare(q_ref, out_ref, grad_ref, qs, gs, delta):
    heads = qs.shape[0]
    queries = rows_of(q_ref, 0, q_ref.shape[0]) * jnp.bfloat16(0.125)
    grads = rows_of(grad_ref, 0, grad_ref.shape[0])
    outs = rows_of(out_ref, 0, out_ref.shape[0])
    product = jnp.transpose(grads.astype(jnp.float32) * outs.astype(jnp.float32))
    for head in range(heads):
        qs[head] = head_part(queries, head, heads)
        gs[head] = head_part(grads, head, heads)
        delta[head] = jnp.sum(product[head * HD : (head + 1) * HD], axis=0, keepdims=True)


def backward_block(keys, values, lse_ref, qs, gs, delta):
    heads = qs.shape[0]
    grad_q, grad_k, grad_v = None, None, None
    for head in range(heads):
        own, grads = qs[head], gs[head]
        weights = jnp.exp(dot(keys, own, NT) - lse_ref[0, head])
        grad_weights = dot(values, grads, NT)
        grad_scores = (weights * (grad_weights - delta[head])).astype(jnp.bfloat16)
        new_v = dot(weights.astype(jnp.bfloat16), grads, NN)
        new_k = dot(grad_scores, own, NN)
        new_q = dot(grad_scores, head_part(keys, head, heads), TN)
        grad_q = new_q if grad_q is None else grad_q + new_q
        grad_k = new_k if grad_k is None else grad_k + new_k
        grad_v = new_v if grad_v is None else grad_v + new_v
    return grad_q, grad_k, grad_v


def cross_backward_body(
    first_object, live_ref, q_ref, k_ref, v_ref, out_ref, lse_ref, grad_ref, dq_ref, dkv_ref, qs, gs, delta, dq_acc
):
    position = pl.program_id(1)
    width = q_ref.shape[3]
    rows = k_ref.shape[0] * k_ref.shape[2]

    @pl.when(position == 0)
    def _():
        backward_prepare(q_ref, out_ref, grad_ref, qs, gs, delta)
        dq_acc[...] = jnp.zeros_like(dq_acc)

    alive = position * rows < live_ref[pl.program_id(0) + first_object]

    @pl.when(alive)
    def _():
        keys = rows_of(k_ref, 0, k_ref.shape[0])
        values = rows_of(v_ref, 0, v_ref.shape[0])
        grad_q, grad_k, grad_v = backward_block(keys, values, lse_ref, qs, gs, delta)
        dq_acc[...] += grad_q
        shape = (k_ref.shape[0], 1, k_ref.shape[2], width)
        dkv_ref[:, 0] = grad_k.astype(jnp.bfloat16).reshape(shape)
        dkv_ref[:, 1] = grad_v.astype(jnp.bfloat16).reshape(shape)

    @pl.when(jnp.logical_not(alive))
    def _():
        dkv_ref[...] = jnp.zeros_like(dkv_ref)

    @pl.when(position == pl.num_programs(1) - 1)
    def _():
        dq_ref[...] = (dq_acc[...] * 0.125).astype(jnp.bfloat16).reshape(dq_ref.shape)


def attend_backward(live, query_source, key_source, value_source, outs, lse, grads, step_rows, span):
    (q_array, q_at), (k_array, k_at), (v_array, v_at) = query_source, key_source, value_source
    groups, unused_blocks, unused_objects, q_rows, width = q_array.shape
    first_object, objects = span
    k_rows = k_array.shape[3]
    heads = width // HD
    total_q = groups * q_rows
    per_k = max(step_rows // k_rows, 1)
    grid = (objects, groups // per_k)
    whole = lambda index: (lambda o, j, live: (0, index, o + first_object, 0, 0))
    part = lambda index: (lambda o, j, live: (j, index, o + first_object, 0, 0))
    tokens = pl.BlockSpec((groups, 1, q_rows, width), lambda o, j, live: (0, o + first_object, 0, 0))
    return pl.pallas_call(
        functools.partial(cross_backward_body, first_object),
        grid_spec=pltpu.PrefetchScalarGridSpec(
            num_scalar_prefetch=1,
            grid=grid,
            in_specs=[
                pl.BlockSpec((groups, None, 1, q_rows, width), whole(q_at)),
                pl.BlockSpec((per_k, None, 1, k_rows, width), part(k_at)),
                pl.BlockSpec((per_k, None, 1, k_rows, width), part(v_at)),
                tokens,
                pl.BlockSpec((1, heads, 1, total_q), lambda o, j, live: (o + first_object, 0, 0, 0)),
                pl.BlockSpec((groups, None, 1, q_rows, width), whole(0)),
            ],
            out_specs=[
                pl.BlockSpec((groups, 1, q_rows, width), lambda o, j, live: (0, o, 0, 0)),
                pl.BlockSpec((per_k, 2, 1, k_rows, width), lambda o, j, live: (j, 0, o, 0, 0)),
            ],
            scratch_shapes=[
                pltpu.VMEM((heads, total_q, width), jnp.bfloat16),
                pltpu.VMEM((heads, total_q, width), jnp.bfloat16),
                pltpu.VMEM((heads, 1, total_q), jnp.float32),
                pltpu.VMEM((total_q, width), jnp.float32),
            ],
        ),
        out_shape=[
            jax.ShapeDtypeStruct((groups, objects, q_rows, width), jnp.bfloat16),
            jax.ShapeDtypeStruct((groups, 2, objects, k_rows, width), jnp.bfloat16),
        ],
        cost_estimate=pl.CostEstimate(
            flops=10 * objects * total_q * groups * k_rows * width,
            bytes_accessed=8 * objects * groups * (q_rows + k_rows) * width,
            transcendentals=objects * heads * total_q * groups * k_rows,
        ),
    )(live, q_array, k_array, v_array, outs, lse, grads)

CHUNKS = ((5, 6), (0, 1, 2), (3, 4, 7), (8, 9, 10, 11), (12, 13, 14, 15))
EARLY = 8
GATHER_PARTS = 1
MOD_ROWS = 16
MESH = pl.DeviceIdType.MESH


def places():
    dp_index, fsdp_index = lax.axis_index("dp"), lax.axis_index("fsdp")
    return dp_index, fsdp_index, fsdp_index // 2, fsdp_index % 2


def z_peer(fsdp_index, shift):
    return {"fsdp": (fsdp_index + 2 * shift) % 8}


def core_peer(fsdp_index):
    return {"fsdp": fsdp_index + 1 - 2 * (fsdp_index % 2)}


def dp_peer(dp_index, flip):
    return {"dp": dp_index ^ flip}


def greet(peers):
    barrier = pltpu.get_barrier_semaphore()
    for peer in peers:
        pl.semaphore_signal(barrier, inc=1, device_id=peer, device_id_type=MESH)
    pl.semaphore_wait(barrier, len(peers))


def remote(source, target, send_sem, recv_sem, peer):
    copy = pltpu.make_async_remote_copy(
        source, target, send_sem, recv_sem, device_id=peer, device_id_type=MESH
    )
    copy.start()
    return copy


def columns(index):
    return pl.ds(pl.multiple_of(index * LANES, LANES), LANES)


def fsdp_peers(fsdp_index):
    return [{"fsdp": (fsdp_index + shift) % 8} for shift in range(1, 8)]


def mix_begin(kind, sources, target, scratch, fsdp_index):
    sems, holds = scratch[0], scratch[1:]

    def ends(place, peer):
        if kind == "heads":
            return sources[0].at[:, :, :, columns(peer)], target.at[fsdp_index]
        mine = columns(fsdp_index)
        if kind == "objects":
            return sources[place].at[peer], target.at[0, place : place + 1, :, mine]
        if len(sources[place].shape) == 4:
            return sources[place].at[peer], target.at[place, :, :, mine]
        return sources[place].at[peer], target.at[place : place + 2, :, :, mine]

    copies, stays = [], []
    for shift in (4, 5, 3, 6, 2, 7, 1):
        peer = (fsdp_index + shift) % 8
        for place in range(len(sources)):
            theirs, there = ends(place, peer)
            copies.append(
                remote(theirs, there, sems.at[0, place, shift], sems.at[1, place, shift], {"fsdp": peer})
            )
    for place in range(len(sources)):
        ours, here = ends(place, fsdp_index)
        load = pltpu.make_async_copy(ours, holds[place], sems.at[0, place, 0])
        load.start()
        stays.append((load, pltpu.make_async_copy(holds[place], here, sems.at[1, place, 0])))
    return copies, stays


def mix_own(moving):
    for load, store in moving[1]:
        load.wait()
        store.start()


def mix_end(moving):
    for load, store in moving[1]:
        store.wait()
    for copy in moving[0]:
        copy.wait()


def mix_plan(mix):
    kind, sources = mix
    bf = jnp.bfloat16
    holds, blocks = [], 0
    for array in sources:
        if kind == "heads":
            holds.append(array.shape[:3] + (array.shape[3] // 8,))
            result = (8,) + holds[0]
        else:
            holds.append(array.shape[1:])
            blocks += 1 if len(array.shape) == 4 else array.shape[1]
            if kind == "objects":
                result = (1, len(sources), array.shape[2], 8 * array.shape[3])
                continue
            result = (blocks,) + array.shape[-3:-1] + (8 * array.shape[-1],)
    scratch = [pltpu.SemaphoreType.DMA((2, len(sources), 8))] + [pltpu.VMEM(hold, bf) for hold in holds]
    return scratch, jax.ShapeDtypeStruct(result, bf)


def mix_body(kind, amount, *refs):
    sources, target, scratch = refs[:amount], refs[amount], refs[amount + 1 :]
    fsdp_index = lax.axis_index("fsdp")
    greet(fsdp_peers(fsdp_index))
    moving = mix_begin(kind, sources, target, scratch, fsdp_index)
    mix_own(moving)
    mix_end(moving)


def mix_alone(mix, collective):
    kind, sources = mix
    scratch, result = mix_plan(mix)
    return pl.pallas_call(
        functools.partial(mix_body, kind, len(sources)),
        in_specs=[ANY] * len(sources),
        out_specs=ANY,
        scratch_shapes=scratch,
        out_shape=result,
        compiler_params=comm_params(collective),
        cost_estimate=pl.CostEstimate(flops=0, bytes_accessed=30_000_000, transcendentals=0),
    )(*sources)


def part_of(ref, unit, dims):
    tile, part = unit // GATHER_PARTS, unit % GATHER_PARTS
    rows = ref.shape[-2] // GATHER_PARTS
    return ref.at[(tile,) + (slice(None),) * dims + (pl.ds(part * rows, rows),)]


def send_z(unit, full, fsdp_index, dp_index, z_index, sems):
    own = full.at[z_index, dp_index]
    return [
        remote(own, own, sems[0].at[unit, shift - 1], sems[1].at[unit, shift - 1], z_peer(fsdp_index, shift))
        for shift in (1, 2, 3)
    ]


def spread(units, fulls, outs, z_copies, z_local, sems, where):
    send_sems, recv_sems, out_sems = sems
    dp_index, fsdp_index, z_index, core = where
    near_x, near_y = dp_peer(dp_index, 1), dp_peer(dp_index, 2)
    first, second, last = {}, {}, []
    for step in range(units + 2):
        if step < units:
            unit, full = step, fulls[step]
            for copy in z_copies[unit]:
                copy.wait() if z_local else copy.wait_recv()
            low, high = full.at[0:2, dp_index], full.at[2:4, dp_index]
            pairs = [(low, near_x), (high, near_y), (low, near_y), (high, near_x)]
            first[unit] = [
                remote(ref, ref, send_sems.at[unit, 3 + n], recv_sems.at[unit, 3 + n], peer)
                for n, (ref, peer) in enumerate(pairs)
            ]
        if 0 <= step - 1 < units:
            unit, full = step - 1, fulls[step - 1]
            first[unit][0].wait_recv()
            first[unit][1].wait_recv()
            low, high = full.at[0:2, dp_index ^ 1], full.at[2:4, dp_index ^ 2]
            pairs = [(low, near_y), (high, near_x)]
            second[unit] = [
                remote(ref, ref, send_sems.at[unit, 7 + n], recv_sems.at[unit, 7 + n], peer)
                for n, (ref, peer) in enumerate(pairs)
            ]
        if 0 <= step - 2 < units:
            unit, full, out = step - 2, fulls[step - 2], outs[step - 2]
            for copy in first[unit][2:] + second[unit]:
                copy.wait_recv()
            target = out.at[:, core]
            last.append(
                remote(full, target, send_sems.at[unit, 9], recv_sems.at[unit, 9], core_peer(fsdp_index))
            )
            here = pltpu.make_async_copy(full, target, out_sems.at[unit])
            here.start()
            last.append(here)
    for unit in range(units):
        for copy in first[unit] + second[unit]:
            copy.wait_send()
    for copy in last:
        copy.wait()


def first_gather_body(tiles, rows, index_ref, narrow_ref, mod_ref, out_ref, mod_out_ref, wait_ref, rest_ref, stacked, mine, full, mod_full, zoned, swap_sems, load_sems, send_sems, recv_sems, out_sems, zone_sems):
    where = places()
    dp_index, fsdp_index, z_index, core = where
    peers = [z_peer(fsdp_index, shift) for shift in (1, 2, 3)]
    peers += [dp_peer(dp_index, flip) for flip in (1, 2, 3)] + [core_peer(fsdp_index)]
    greet(peers)
    swaps = [
        remote(narrow_ref.at[:, dp_index ^ flip], stacked.at[pl.ds(4 * flip, 4)], swap_sems.at[0, flip], swap_sems.at[1, flip], dp_peer(dp_index, flip))
        for flip in (1, 2, 3)
    ]
    own = pltpu.make_async_copy(narrow_ref.at[:, dp_index], stacked.at[pl.ds(0, 4)], load_sems.at[0])
    own.start()
    mod_load = pltpu.make_async_copy(mod_ref, mod_full.at[z_index, dp_index], load_sems.at[1])
    mod_load.start()
    mod_load.wait()
    units = tiles * GATHER_PARTS
    z_copies = {units: send_z(units, mod_full, fsdp_index, dp_index, z_index, (send_sems, recv_sems))}
    own.wait()
    for swap in swaps:
        swap.wait()
    for tile in range(tiles):
        full[tile, z_index, dp_index] = stacked[index_ref[tile]]
        for unit in range(tile * GATHER_PARTS, (tile + 1) * GATHER_PARTS):
            z_copies[unit] = send_z(unit, part_of(full, unit, 2), fsdp_index, dp_index, z_index, (send_sems, recv_sems))

    def take(position, carried):
        mine[position] = stacked[index_ref[position + tiles]]
        return carried

    lax.fori_loop(0, 16 - tiles, take, 0)
    early = EARLY - tiles
    zone = [
        remote(mine.at[pl.ds(0, early)], zoned.at[z_index], zone_sems.at[0, shift - 1], zone_sems.at[1, shift - 1], z_peer(fsdp_index, shift))
        for shift in (1, 2, 3)
    ]
    zone_own = pltpu.make_async_copy(mine.at[pl.ds(0, early)], wait_ref.at[z_index], load_sems.at[2])
    zone_own.start()
    rest = pltpu.make_async_copy(mine.at[pl.ds(early, 16 - EARLY)], rest_ref, load_sems.at[3])
    rest.start()
    fulls = [part_of(full, unit, 2) for unit in range(units)] + [mod_full]
    outs = [part_of(out_ref, unit, 3) for unit in range(units)] + [mod_out_ref]
    spread(units + 1, fulls, outs, z_copies, False, (send_sems, recv_sems, out_sems), where)
    for unit in range(units + 1):
        for copy in z_copies[unit]:
            copy.wait_send()
    for copy in zone:
        copy.wait()
    zone_own.wait()
    rest.wait()
    stores = []
    for shift in (1, 2, 3):
        z_from = (z_index + shift) % 4
        store = pltpu.make_async_copy(zoned.at[z_from], wait_ref.at[z_from], load_sems.at[3 + shift])
        store.start()
        stores.append(store)
    for store in stores:
        store.wait()


ANY = pl.BlockSpec(memory_space=pl.ANY)


def comm_params(collective):
    return pltpu.CompilerParams(
        collective_id=collective, has_side_effects=True, vmem_limit_bytes=58 * 1024 * 1024
    )


def first_gather(narrow, mod_rows, index):
    tiles = len(CHUNKS[0])
    slots, owners, rows, width = narrow.shape
    bf = jnp.bfloat16
    return pl.pallas_call(
        functools.partial(first_gather_body, tiles, rows),
        grid_spec=pltpu.PrefetchScalarGridSpec(
            num_scalar_prefetch=1,
            grid=(),
            in_specs=[ANY, ANY],
            out_specs=[ANY] * 4,
            scratch_shapes=[
                pltpu.VMEM((16, rows, width), bf),
                pltpu.VMEM((16 - tiles, rows, width), bf),
                pltpu.VMEM((tiles, 4, 4, rows, width), bf),
                pltpu.VMEM((4, 4, MOD_ROWS, width), bf),
                pltpu.VMEM((4, EARLY - tiles, rows, width), bf),
                pltpu.SemaphoreType.DMA((2, 4)),
                pltpu.SemaphoreType.DMA((8,)),
                pltpu.SemaphoreType.DMA((tiles * GATHER_PARTS + 1, 10)),
                pltpu.SemaphoreType.DMA((tiles * GATHER_PARTS + 1, 10)),
                pltpu.SemaphoreType.DMA((tiles * GATHER_PARTS + 1,)),
                pltpu.SemaphoreType.DMA((2, 3)),
            ],
        ),
        out_shape=[
            jax.ShapeDtypeStruct((tiles, 4, 2, 4, rows, width), bf),
            jax.ShapeDtypeStruct((4, 2, 4, MOD_ROWS, width), bf),
            jax.ShapeDtypeStruct((4, EARLY - tiles, rows, width), bf),
            jax.ShapeDtypeStruct((16 - EARLY, rows, width), bf),
        ],
        compiler_params=comm_params(0),
        cost_estimate=pl.CostEstimate(flops=0, bytes_accessed=200_000_000, transcendentals=0),
    )(index, narrow, mod_rows)


def next_gather_body(tiles, start, zoned, kind, amount, ahead, source_ref, *refs):
    mix_sources, refs = refs[:amount], refs[amount:]
    out_ref, refs = refs[0], refs[1:]
    if amount:
        mixed_ref, refs = refs[0], refs[1:]
    if ahead:
        zone_ref, refs = refs[0], refs[1:]
        zone_hold, zone_sems, refs = refs[0], refs[1], refs[2:]
    full, load_sems, send_sems, recv_sems, out_sems = refs[:5]
    where = places()
    dp_index, fsdp_index, z_index, core = where
    loads = []
    for tile in range(tiles):
        if zoned:
            load = pltpu.make_async_copy(source_ref.at[:, start + tile], full.at[tile, :, dp_index], load_sems.at[tile])
        else:
            load = pltpu.make_async_copy(source_ref.at[start + tile], full.at[tile, z_index, dp_index], load_sems.at[tile])
        load.start()
        loads.append(load)
    units = tiles * GATHER_PARTS
    peers = [dp_peer(dp_index, flip) for flip in (1, 2)]
    if amount:
        peers += fsdp_peers(fsdp_index)
    else:
        peers += [core_peer(fsdp_index)]
        peers += [] if zoned else [z_peer(fsdp_index, shift) for shift in (1, 2, 3)]
    greet(peers)
    z_copies = {}
    for tile in range(tiles):
        near = range(tile * GATHER_PARTS, (tile + 1) * GATHER_PARTS)
        if zoned:
            for unit in near:
                z_copies[unit] = [loads[tile]] if unit == near[0] else []
        else:
            loads[tile].wait()
            for unit in near:
                z_copies[unit] = send_z(unit, part_of(full, unit, 2), fsdp_index, dp_index, z_index, (send_sems, recv_sems))
    if amount:
        moving = mix_begin(kind, mix_sources, mixed_ref, refs[5:], fsdp_index)
        mix_own(moving)
    if ahead:
        later = source_ref.at[pl.ds(ahead[0], ahead[1])]
        zone = [
            remote(later, zone_ref.at[z_index], zone_sems.at[0, shift], zone_sems.at[1, shift], z_peer(fsdp_index, shift))
            for shift in (1, 2, 3)
        ]
        zone_load = pltpu.make_async_copy(later, zone_hold, zone_sems.at[0, 0])
        zone_load.start()
        zone_load.wait()
        zone_store = pltpu.make_async_copy(zone_hold, zone_ref.at[z_index], zone_sems.at[1, 0])
        zone_store.start()
    fulls = [part_of(full, unit, 2) for unit in range(units)]
    outs = [part_of(out_ref, unit, 3) for unit in range(units)]
    spread(units, fulls, outs, z_copies, zoned, (send_sems, recv_sems, out_sems), where)
    if not zoned:
        for unit in range(units):
            for copy in z_copies[unit]:
                copy.wait_send()
    if amount:
        mix_end(moving)
    if ahead:
        for copy in zone:
            copy.wait()
        zone_store.wait()


def next_gather(source, tiles, start, zoned, mix, ahead, collective):
    rows, width = source.shape[-2:]
    bf = jnp.bfloat16
    kind, mix_sources = mix if mix else (None, [])
    out_shape = [jax.ShapeDtypeStruct((tiles, 4, 2, 4, rows, width), bf)]
    scratch = [
        pltpu.VMEM((tiles, 4, 4, rows, width), bf),
        pltpu.SemaphoreType.DMA((tiles,)),
        pltpu.SemaphoreType.DMA((tiles * GATHER_PARTS, 10)),
        pltpu.SemaphoreType.DMA((tiles * GATHER_PARTS, 10)),
        pltpu.SemaphoreType.DMA((tiles * GATHER_PARTS,)),
    ]
    if mix:
        extra, result = mix_plan(mix)
        scratch, out_shape = scratch + extra, out_shape + [result]
    if ahead:
        scratch = [pltpu.VMEM((ahead[1], rows, width), bf), pltpu.SemaphoreType.DMA((2, 4))] + scratch
        out_shape = out_shape + [jax.ShapeDtypeStruct((4, ahead[1], rows, width), bf)]
    results = pl.pallas_call(
        functools.partial(next_gather_body, tiles, start, zoned, kind, len(mix_sources), ahead),
        in_specs=[ANY] * (1 + len(mix_sources)),
        out_specs=[ANY] * len(out_shape),
        scratch_shapes=scratch,
        out_shape=out_shape,
        compiler_params=comm_params(collective),
        cost_estimate=pl.CostEstimate(flops=0, bytes_accessed=tiles * 30_000_000, transcendentals=0),
    )(source, *mix_sources)
    mixed = results[1] if mix else None
    return results[0].reshape(tiles, 32 * rows, width), mixed, (results[-1] if ahead else None)


def fast_layout(master):
    owners, groups = lax.axis_size("dp"), lax.axis_size("fsdp")
    return owners == 4 and groups == 8 and master.shape[1:] == (128, 1024)


def fetch_generic(master, modulation, tile_slots):
    narrow = master.astype(jnp.bfloat16)
    mod_narrow = modulation.astype(jnp.bfloat16)[:, None, None, :]
    row_blocks = lax.all_gather(narrow, "fsdp", axis=1, tiled=True)
    mod_blocks = lax.all_gather(mod_narrow, "fsdp", axis=2, tiled=True)
    gathered = lax.all_gather(row_blocks, "dp", axis=0, tiled=True)
    mod_all = lax.all_gather(mod_blocks, "dp", axis=1, tiled=True)
    chunks = [
        jnp.stack(
            [lax.dynamic_index_in_dim(gathered, tile_slots[tile], 0, keepdims=False) for tile in chunk]
        )
        for chunk in CHUNKS
    ]
    return chunks, mod_all.reshape(mod_all.shape[0], -1)


def sums_generic(logical, tile_slots):
    slot_grads = jnp.zeros((len(logical),) + logical[0].shape, jnp.bfloat16)
    for position, grad in enumerate(logical):
        slot_grads = lax.dynamic_update_index_in_dim(
            slot_grads, grad.astype(jnp.bfloat16), tile_slots[position], 0
        )
    row_sums = lax.psum_scatter(slot_grads, "fsdp", scatter_dimension=1, tiled=True)
    return lax.psum_scatter(row_sums, "dp", scatter_dimension=0, tiled=True)


def mod_generic(grad_modulation):
    owners, groups = lax.axis_size("dp"), lax.axis_size("fsdp")
    rows, width = grad_modulation.shape
    blocks = grad_modulation.reshape(rows, owners, groups, width // (owners * groups))
    sums = lax.psum_scatter(blocks.astype(jnp.bfloat16), "fsdp", scatter_dimension=2, tiled=True)
    sums = lax.psum_scatter(sums, "dp", scatter_dimension=1, tiled=True)
    return sums.reshape(rows, -1).astype(jnp.float32)


def wide(value):
    return value.astype(jnp.float32)


def reduce_scratch(tiles, rows, width):
    bf, f32 = jnp.bfloat16, jnp.float32
    return [
        pltpu.VMEM((2, tiles, 4, 4, rows, width), bf),
        pltpu.VMEM((4, tiles, 2, 2, rows, width), bf),
        pltpu.VMEM((2, tiles, 2, 2, rows, width), f32),
        pltpu.VMEM((4, tiles, 2, rows, width), bf),
        pltpu.VMEM((tiles, 4, rows, width), f32),
        pltpu.VMEM((2, 3, tiles, rows, width), bf),
        pltpu.VMEM((tiles, rows, width), bf),
        pltpu.SemaphoreType.DMA((2, tiles)),
        pltpu.SemaphoreType.DMA((8, tiles)),
        pltpu.SemaphoreType.DMA((8, tiles)),
    ]


def reduce_stages(tiles, scratch, out_ref, where):
    core_buf, swap, kept, swap_two, whole, zbuf, out_buf, load_sems, send_sems, recv_sems = scratch
    dp_index, fsdp_index, z_index, core = where
    x_bit, y_bit = dp_index % 2, dp_index // 2
    near_x, near_y = dp_peer(dp_index, 1), dp_peer(dp_index, 2)

    def moved(stage, tile):
        if stage == 1:
            ends = (swap.at[0, tile], swap.at[1, tile], near_x)
        elif stage == 2:
            ends = (swap.at[2, tile], swap.at[3, tile], near_y)
        elif stage == 3:
            ends = (swap_two.at[0, tile], swap_two.at[1, tile], near_y)
        elif stage == 4:
            ends = (swap_two.at[2, tile], swap_two.at[3, tile], near_x)
        else:
            shift = stage - 4
            ends = (zbuf.at[0, shift - 1, tile], zbuf.at[1, shift - 1, tile], z_peer(fsdp_index, shift))
        return pltpu.make_async_remote_copy(
            ends[0], ends[1], send_sems.at[stage, tile], recv_sems.at[stage, tile], device_id=ends[2], device_id_type=MESH
        )

    def both(tile, z_place, quarter):
        return wide(core_buf[0, tile, z_place, quarter]) + wide(core_buf[1, tile, z_place, quarter])

    def add_core(tile):
        for side in range(2):
            for other in range(2):
                kept[0, tile, side, other] = both(tile, side, 2 * other + x_bit)
                swap[0, tile, side, other] = both(tile, side, 2 * other + 1 - x_bit).astype(jnp.bfloat16)
                kept[1, tile, side, other] = both(tile, 2 + side, 2 * y_bit + other)
                swap[2, tile, side, other] = both(tile, 2 + side, 2 * (1 - y_bit) + other).astype(jnp.bfloat16)
        moved(1, tile).start()
        moved(2, tile).start()

    def add_first(tile):
        moved(1, tile).wait_recv()
        moved(2, tile).wait_recv()
        for side in range(2):
            whole[tile, side] = kept[0, tile, side, y_bit] + wide(swap[1, tile, side, y_bit])
            away = kept[0, tile, side, 1 - y_bit] + wide(swap[1, tile, side, 1 - y_bit])
            swap_two[0, tile, side] = away.astype(jnp.bfloat16)
            whole[tile, 2 + side] = kept[1, tile, side, x_bit] + wide(swap[3, tile, side, x_bit])
            away = kept[1, tile, side, 1 - x_bit] + wide(swap[3, tile, side, 1 - x_bit])
            swap_two[2, tile, side] = away.astype(jnp.bfloat16)
        moved(3, tile).start()
        moved(4, tile).start()

    def add_second(tile):
        moved(3, tile).wait_recv()
        moved(4, tile).wait_recv()
        for side in range(2):
            whole[tile, side] = whole[tile, side] + wide(swap_two[1, tile, side])
            whole[tile, 2 + side] = whole[tile, 2 + side] + wide(swap_two[3, tile, side])
        for shift in (1, 2, 3):
            zbuf[0, shift - 1, tile] = whole[tile, (z_index + shift) % 4].astype(jnp.bfloat16)
            moved(4 + shift, tile).start()

    def add_z(tile):
        total = whole[tile, z_index]
        for shift in (1, 2, 3):
            moved(4 + shift, tile).wait_recv()
            total = total + wide(zbuf[1, shift - 1, tile])
        out_buf[tile] = total.astype(jnp.bfloat16)

    def finish(tile):
        for stage in range(1, 8):
            moved(stage, tile).wait_send()

    return add_core, add_first, add_second, add_z, finish


def core_copies(entries, scratch, where):
    core_buf, load_sems, send_sems, recv_sems = scratch[0], scratch[-3], scratch[-2], scratch[-1]
    copies = []
    for tile, (theirs, ours) in enumerate(entries):
        away = remote(theirs, core_buf.at[1, tile], send_sems.at[0, tile], recv_sems.at[0, tile], core_peer(where[1]))
        load = pltpu.make_async_copy(ours, core_buf.at[0, tile], load_sems.at[0, tile])
        load.start()
        copies.append((away, load))
    return copies


def reduce_body(counts, extra, plans, parts, *refs):
    groups = len(counts)
    tiles = sum(counts) * parts
    grads, refs = refs[:groups], refs[groups:]
    if extra:
        mod_grads, refs = refs[0], refs[1:]
    mix_sources = []
    for unused_kind, amount in plans:
        mix_sources.append(refs[:amount])
        refs = refs[amount:]
    out_ref, refs = refs[0], refs[1:]
    if extra:
        mod_out_ref, refs = refs[0], refs[1:]
    mixed_refs, refs = refs[: len(plans)], refs[len(plans) :]
    scratch, refs = refs[:10], refs[10:]
    if extra:
        mod_scratch, refs = refs[:10], refs[10:]
    where = places()
    dp_index, fsdp_index, core = where[0], where[1], where[3]
    peers = [dp_peer(dp_index, flip) for flip in (1, 2)]
    if plans:
        peers += fsdp_peers(fsdp_index)
    else:
        peers += [z_peer(fsdp_index, shift) for shift in (1, 2, 3)] + [core_peer(fsdp_index)]
    greet(peers)
    movings = []
    for place, (kind, amount) in enumerate(plans):
        mix_scratch, refs = refs[: 1 + amount], refs[1 + amount :]
        movings.append(mix_begin(kind, mix_sources[place], mixed_refs[place], mix_scratch, fsdp_index))
    rows = out_ref.shape[1]
    entries = [
        tuple(grads[group].at[tile, :, side, :, pl.ds(part * rows, rows)] for side in (1 - core, core))
        for group in range(groups)
        for tile in range(counts[group])
        for part in range(parts)
    ]
    mod_entry = [(mod_grads.at[0, :, 1 - core], mod_grads.at[0, :, core])] if extra else []
    mod_copies = core_copies(mod_entry, mod_scratch, where) if extra else []
    copies = core_copies(entries, scratch, where)
    for moving in movings:
        mix_own(moving)
    stages = reduce_stages(tiles, scratch, out_ref, where)
    if extra:
        mod_stages = reduce_stages(1, mod_scratch, mod_out_ref, where)
        mod_copies[0][0].wait()
        mod_copies[0][1].wait()
        mod_stages[0](0)

    def arrive(tile):
        pltpu.make_async_copy(scratch[0].at[0, tile], scratch[0].at[0, tile], scratch[-3].at[0, tile]).wait()
        pltpu.make_async_remote_copy(
            scratch[0].at[1, tile], scratch[0].at[1, tile], scratch[-2].at[0, tile], scratch[-1].at[0, tile],
            device_id=core_peer(fsdp_index), device_id_type=MESH,
        ).wait_recv()

    def step(position, carried):
        @pl.when(position < tiles)
        def _():
            arrive(position)
            stages[0](position)

        for place in (1, 2, 3):
            tile = position - place

            @pl.when((tile >= 0) & (tile < tiles))
            def _():
                stages[place](tile)

        return carried

    if extra:
        step(0, 0)
        mod_stages[1](0)
        step(1, 0)
        mod_stages[2](0)
        step(2, 0)
        mod_stages[3](0)
        lax.fori_loop(3, tiles + 3, step, 0)
        mod_stages[4](0)
    else:
        lax.fori_loop(0, tiles + 3, step, 0)

    store = pltpu.make_async_copy(scratch[6], out_ref, scratch[-3].at[1, 0])
    store.start()

    def close(tile, carried):
        stages[4](tile)
        return carried

    lax.fori_loop(0, tiles, close, 0)
    for away, load in copies:
        away.wait_send()
    if extra:
        mod_store = pltpu.make_async_copy(mod_scratch[6], mod_out_ref, mod_scratch[-3].at[1, 0])
        mod_store.start()
        mod_store.wait()
    store.wait()
    for moving in movings:
        mix_end(moving)


def reduce_tiles(grads, mods, mixes, collective, parts=1):
    counts = tuple(part.shape[0] for part in grads)
    tiles = sum(counts) * parts
    rows, width = grads[0].shape[-2:]
    rows = rows // parts
    bf = jnp.bfloat16
    operands = list(grads)
    out_shape = [jax.ShapeDtypeStruct((tiles, rows, width), bf)]
    scratch = reduce_scratch(tiles, rows, width)
    if mods is not None:
        operands.append(mods)
        out_shape.append(jax.ShapeDtypeStruct((1, MOD_ROWS, width), bf))
        scratch = scratch + reduce_scratch(1, MOD_ROWS, width)
    for mix in mixes:
        operands += list(mix[1])
        extra, result = mix_plan(mix)
        scratch, out_shape = scratch + extra, out_shape + [result]
    plans = tuple((kind, len(sources)) for kind, sources in mixes)
    results = pl.pallas_call(
        functools.partial(reduce_body, counts, mods is not None, plans, parts),
        in_specs=[ANY] * len(operands),
        out_specs=[ANY] * len(out_shape),
        scratch_shapes=scratch,
        out_shape=out_shape,
        compiler_params=comm_params(collective),
        cost_estimate=pl.CostEstimate(flops=0, bytes_accessed=tiles * 20_000_000, transcendentals=0),
    )(*operands)
    return [results[0].reshape(-1, rows * parts, width)] + list(results[1:])


def owner_body(counts, index_ref, *refs):
    sources, refs = refs[: len(counts)], refs[len(counts) :]
    out_ref, held, picked, load_sems, send_sems, recv_sems = refs
    dp_index = lax.axis_index("dp")
    loads, start = [], 0
    for place, count in enumerate(counts):
        load = pltpu.make_async_copy(sources[place], held.at[pl.ds(start, count)], load_sems.at[place])
        load.start()
        loads.append(load)
        start += count
    greet([dp_peer(dp_index, flip) for flip in (1, 2, 3)])
    for load in loads:
        load.wait()
    copies = []
    for flip in (3, 1, 2, 0):
        for slot in range(4):
            picked[flip, slot] = held[index_ref[4 * flip + slot]]
        target = out_ref.at[:, dp_index]
        if flip:
            copies.append(
                remote(picked.at[flip], target, send_sems.at[flip], recv_sems.at[flip], dp_peer(dp_index, flip))
            )
        else:
            here = pltpu.make_async_copy(picked.at[flip], target, load_sems.at[0])
            here.start()
            copies.append(here)
    for copy in copies:
        copy.wait()


def to_owners(sums, order, tile_slots, collective):
    rows, width = sums[0].shape[-2:]
    counts = tuple(part.shape[0] for part in sums)
    dp_index = lax.axis_index("dp")
    spots = jnp.arange(16, dtype=jnp.int32)
    wanted = ((spots // 4) ^ dp_index) * 4 + spots % 4
    slots = tile_slots[jnp.array(order, jnp.int32)]
    matches = slots[None, :] == wanted[:, None]
    index = jnp.sum(jnp.where(matches, spots[None, :], 0), axis=1).astype(jnp.int32)
    bf = jnp.bfloat16
    return pl.pallas_call(
        functools.partial(owner_body, counts),
        grid_spec=pltpu.PrefetchScalarGridSpec(
            num_scalar_prefetch=1,
            grid=(),
            in_specs=[ANY] * len(counts),
            out_specs=ANY,
            scratch_shapes=[
                pltpu.VMEM((16, rows, width), bf),
                pltpu.VMEM((4, 4, rows, width), bf),
                pltpu.SemaphoreType.DMA((len(counts),)),
                pltpu.SemaphoreType.DMA((4,)),
                pltpu.SemaphoreType.DMA((4,)),
            ],
        ),
        out_shape=jax.ShapeDtypeStruct((4, 4, rows, width), bf),
        compiler_params=comm_params(collective),
        cost_estimate=pl.CostEstimate(flops=0, bytes_accessed=50_000_000, transcendentals=0),
    )(index, *sums)


def tile_sums(form, left, right):
    total = contract(form, left, right).astype(jnp.bfloat16)
    return total.reshape(-1, 4, 2, 4, total.shape[-2] // 32, total.shape[-1])


def mod_sums(grad_modulation):
    rows, width = grad_modulation.shape
    columns_here = width // 32
    blocks = grad_modulation.reshape(rows, 4, 4, 2, columns_here).transpose(2, 3, 1, 0, 4)
    flat = blocks.astype(jnp.bfloat16).reshape(1, 4, 2, 4, rows * columns_here)
    flat = jnp.pad(flat, ((0, 0),) * 4 + ((0, MOD_ROWS * 1024 - rows * columns_here),))
    return flat.reshape(1, 4, 2, 4, MOD_ROWS, 1024)


def after(value, *others):
    return lax.optimization_barrier((value,) + others)[0]


def weight_source(master, modulation, tile_slots):
    if not fast_layout(master):
        chunks, mod_all = fetch_generic(master, modulation, tile_slots)
        return (lambda number, mix, *others: (chunks[number], mix_generic(mix))), mod_all
    slots_here, row_count, width = master.shape
    dp_index = lax.axis_index("dp")
    narrow = master.astype(jnp.bfloat16).reshape(slots_here, 4, row_count // 4, width)
    index = ((tile_slots // slots_here) ^ dp_index) * slots_here + tile_slots % slots_here
    index = index[jnp.array([tile for chunk in CHUNKS for tile in chunk], jnp.int32)]
    mod_rows, mod_columns = modulation.shape
    mod_flat = modulation.astype(jnp.bfloat16).reshape(-1)
    mod_flat = jnp.pad(mod_flat, (0, MOD_ROWS * width - mod_flat.shape[0])).reshape(MOD_ROWS, width)
    first, mods, zoned, rest = first_gather(narrow, mod_flat, index)
    flat = mods.reshape(8, 4, MOD_ROWS * width)[:, :, : mod_rows * mod_columns]
    mod_all = flat.reshape(8, 4, mod_rows, mod_columns).transpose(2, 1, 0, 3).reshape(mod_rows, -1)

    last_zone = []

    def chunk(number, mix, *others):
        tiles = len(CHUNKS[number])
        if number == 0:
            return first.reshape(tiles, row_count * 8, width), None
        if number < 3:
            held = after(zoned, *others) if others else zoned
            return next_gather(held, tiles, (0, 3)[number - 1], True, mix, None, number)[:2]
        if number == 3:
            full, mixed, zone = next_gather(rest, tiles, 0, False, mix, (tiles, 16 - EARLY - tiles), number)
            last_zone.append(zone)
            return full, mixed
        return next_gather(last_zone[0], tiles, 0, True, mix, None, number)[:2]

    return chunk, mod_all


def pair_body(x_ref, w_ref, out_ref):
    objects, rows, width = x_ref.shape
    values = dot(x_ref[...].reshape(objects * rows, width), w_ref[0], NN).astype(jnp.bfloat16)
    for side in range(2):
        part = values[:, side * LANES : (side + 1) * LANES]
        out_ref[side, 0] = part.reshape(objects, rows, LANES)


def project_pairs(tokens, tiles):
    objects, rows, width = tokens.shape
    blocks = tiles.shape[0]
    return pl.pallas_call(
        pair_body,
        grid=(blocks, 4),
        in_specs=[
            pl.BlockSpec((objects, rows, width), lambda k, g: (0, 0, 0)),
            pl.BlockSpec((1, width, 2 * LANES), lambda k, g: (k, 0, g)),
        ],
        out_specs=pl.BlockSpec((2, 1, objects, rows, LANES), lambda k, g: (g, k, 0, 0, 0)),
        out_shape=jax.ShapeDtypeStruct((8, blocks, objects, rows, LANES), jnp.bfloat16),
        cost_estimate=pl.CostEstimate(
            flops=2 * objects * rows * width * blocks * 8 * LANES,
            bytes_accessed=2 * objects * rows * (width + blocks * 8 * LANES),
            transcendentals=0,
        ),
    )(tokens, tiles)


def exchange(pieces):
    return lax.all_to_all(pieces, "fsdp", split_axis=0, concat_axis=0, tiled=True)


def by_head(values, groups):
    blocks, objects, rows, width = values.shape
    moved = values.reshape(blocks, objects, rows, groups, width // groups)
    return moved.transpose(3, 0, 1, 2, 4)


def from_head(pieces):
    groups, blocks, objects, rows, share = pieces.shape
    return pieces.transpose(1, 2, 3, 0, 4).reshape(blocks, objects, rows, groups * share)


def mix_generic(mix):
    if mix is None:
        return None
    kind, sources = mix
    if kind == "heads":
        return exchange(by_head(sources[0], lax.axis_size("fsdp")))
    if kind == "objects":
        sources = [jnp.concatenate(sources, axis=1)]
    parts = [array if array.ndim == 5 else array[:, None] for array in sources]
    return from_head(exchange(jnp.concatenate(parts, axis=1)))


def adamw(weights, grads, first, second, rate):
    first_new = BETA_ONE * first + (1.0 - BETA_ONE) * grads
    second_new = BETA_TWO * second + (1.0 - BETA_TWO) * grads * grads
    first_hat = first_new / (1.0 - BETA_ONE**STEP)
    second_hat = second_new / (1.0 - BETA_TWO**STEP)
    weights_new = weights - rate * (
        first_hat / (jnp.sqrt(second_hat) + EPSILON) + WEIGHT_DECAY * weights
    )
    return (weights_new, first_new, second_new)


def shards(
    triplane,
    image_tokens,
    camera,
    view_tokens,
    master,
    moment1,
    moment2,
    tile_slots,
    modulation,
    mod_moment1,
    mod_moment2,
    cotangent,
):
    objects, tri_local, model_width = triplane.shape
    groups = lax.axis_size("fsdp")
    tri_total = tri_local * groups
    fast = fast_layout(master)
    partial_sums = tile_sums if fast else contract

    def reduced(grads, mods, mixes, collective, parts=1):
        if not fast:
            return [None] + [mix_generic(mix) for mix in mixes]
        return reduce_tiles(grads, mods, mixes, collective, parts)

    chunk, mod_all = weight_source(master, modulation, tile_slots)
    mod_full = mod_all.astype(jnp.float32)
    modulations = (
        jnp.dot(camera, mod_full[:-1], precision=HIGHEST, preferred_element_type=jnp.float32)
        + mod_full[-1]
    )
    blocks = [
        modulations[:, position * model_width : (position + 1) * model_width][:, None, :]
        for position in range(9)
    ]
    tiles_pair, unused_mix = chunk(0, None)
    if fast:
        pair_sent = project_pairs(image_tokens, tiles_pair)
    else:
        image_pairs = contract("oid,kde->koie", image_tokens, tiles_pair).astype(jnp.bfloat16)
        pair_sent = by_head(image_pairs, groups)
    pair_heads = exchange(pair_sent)
    tiles_qkv, unused_mix = chunk(1, None, pair_sent)
    residual_in = triplane.astype(jnp.float32)
    normed_one = modulate(residual_in, blocks[0], blocks[1]).astype(jnp.bfloat16)
    triples = contract("otd,kde->kote", normed_one, tiles_qkv).astype(jnp.bfloat16)
    tiles_mixed, triple_heads = chunk(2, ("heads", [triples]))
    tile_out_one, tile_query_two, tile_out_two = tiles_mixed[0], tiles_mixed[1], tiles_mixed[2]
    every_key = jnp.full((objects,), tri_total, jnp.int32)
    self_sources = [(triple_heads, index) for index in range(3)]
    self_result, self_logsum = attend_forward(every_key, *self_sources, tri_total, VIEW)
    tiles_up, merged_one = chunk(3, ("tokens", [self_result]))
    merged_one = merged_one[0]
    branch_one = contract("otd,de->ote", merged_one, tile_out_one)
    residual_mid = residual_in + blocks[2] * branch_one
    normed_two = modulate(residual_mid, blocks[3], blocks[4]).astype(jnp.bfloat16)
    cross_query = contract("otd,de->ote", normed_two, tile_query_two).astype(jnp.bfloat16)
    tiles_down, query_heads = chunk(4, ("heads", [cross_query[None]]))
    cross_sources = [(query_heads, 0), (pair_heads, 0), (pair_heads, 1)]
    cross_result, cross_logsum = attend_forward(view_tokens, *cross_sources, tri_total, VIEW)
    cross_mix = ("tokens", [cross_result])
    merged_two = (mix_alone(cross_mix, 11) if fast else mix_generic(cross_mix))[0]
    branch_two = contract("otd,de->ote", merged_two, tile_out_two)
    residual_late = residual_mid + blocks[5] * branch_two
    normed_three = modulate(residual_late, blocks[6], blocks[7]).astype(jnp.bfloat16)
    hidden_pre = contract("otd,kde->otke", normed_three, tiles_up)
    hidden = gelu_tanh(hidden_pre).astype(jnp.bfloat16)
    branch_three = contract("otkd,kde->ote", hidden, tiles_down)
    block_output = (residual_late + blocks[8] * branch_three).astype(jnp.bfloat16)
    grad_final = cotangent.astype(jnp.float32)
    grad_gate_three = jnp.sum(grad_final * branch_three, axis=1)
    grad_branch_three = (blocks[8] * grad_final).astype(jnp.bfloat16)
    grad_hidden = contract("ote,kde->otkd", grad_branch_three, tiles_down)
    unused_gelu, gelu_pull = jax.vjp(gelu_tanh, hidden_pre)
    grad_pre = gelu_pull(grad_hidden)[0].astype(jnp.bfloat16)
    grad_normed_three = contract("otke,kde->otd", grad_pre, tiles_up)
    grad_late_norm, grad_shift_three, grad_scale_three = modulate_back(
        residual_late, blocks[6], blocks[7], grad_normed_three
    )
    grad_late = grad_final + grad_late_norm
    grad_gate_two = jnp.sum(grad_late * branch_two, axis=1)
    grad_branch_two = (blocks[5] * grad_late).astype(jnp.bfloat16)
    grad_merged_two = contract("ote,de->otd", grad_branch_two, tile_out_two).astype(jnp.bfloat16)
    grad_down = partial_sums("otkd,ote->kde", hidden, grad_branch_three)
    grad_up = partial_sums("otd,otke->kde", normed_three, grad_pre)
    grad_out_two = partial_sums("otd,ote->de", merged_two, grad_branch_two)
    sums_down, grad_cross_heads = reduced([grad_down], None, [("heads", [grad_merged_two[None]])], 5, 2)
    grad_query_heads, grad_pair_heads = [], []
    for place in range(objects):
        query_part, pair_part = attend_backward(
            view_tokens, *cross_sources, cross_result, cross_logsum, grad_cross_heads, VIEW, (place, 1)
        )
        grad_query_heads.append(query_part)
        grad_pair_heads.append(pair_part)
    half = objects // 2
    pair_mixes = [("tokens", [part]) for part in grad_pair_heads]
    sums_up, grad_query_two, *grad_pairs = reduced(
        [grad_up], None, [("objects", grad_query_heads)] + pair_mixes[:half], 6
    )
    grad_query_two = grad_query_two[0]
    grad_tile_query = partial_sums("otd,ote->de", normed_two, grad_query_two)
    grad_normed_two = contract("ote,de->otd", grad_query_two, tile_query_two)
    grad_mid_norm, grad_shift_two, grad_scale_two = modulate_back(
        residual_mid, blocks[3], blocks[4], grad_normed_two
    )
    grad_mid = grad_late + grad_mid_norm
    grad_gate_one = jnp.sum(grad_mid * branch_one, axis=1)
    grad_branch_one = (blocks[2] * grad_mid).astype(jnp.bfloat16)
    grad_merged_one = contract("ote,de->otd", grad_branch_one, tile_out_one).astype(jnp.bfloat16)
    grad_out_one = partial_sums("otd,ote->de", merged_one, grad_branch_one)
    sums_mid, grad_self_heads, *more_pairs = reduced(
        [grad_out_two, grad_tile_query], None, [("heads", [grad_merged_one[None]])] + pair_mixes[half:], 7
    )
    grad_self_query, grad_self_pair = attend_backward(
        every_key, *self_sources, self_result, self_logsum, grad_self_heads, VIEW, (0, objects)
    )
    grad_pairs = jnp.concatenate(grad_pairs + more_pairs, axis=1)
    grad_tiles_pair = partial_sums("oid,koie->kde", image_tokens, grad_pairs)
    grad_image = contract("koie,kde->oid", grad_pairs, tiles_pair)
    sums_late, grad_triples = reduced(
        [grad_tiles_pair, grad_out_one], None, [("tokens", [grad_self_query, grad_self_pair])], 8
    )
    grad_qkv = partial_sums("otd,kote->kde", normed_one, grad_triples)
    grad_normed_one = contract("kote,kde->otd", grad_triples, tiles_qkv)
    grad_in_norm, grad_shift_one, grad_scale_one = modulate_back(
        residual_in, blocks[0], blocks[1], grad_normed_one
    )
    grad_triplane = grad_mid + grad_in_norm
    grad_mods = jnp.concatenate(
        [
            grad_shift_one[:, 0],
            grad_scale_one[:, 0],
            grad_gate_one,
            grad_shift_two[:, 0],
            grad_scale_two[:, 0],
            grad_gate_two,
            grad_shift_three[:, 0],
            grad_scale_three[:, 0],
            grad_gate_three,
        ],
        axis=-1,
    )
    grad_mod_rows = jnp.dot(
        camera.T, grad_mods, precision=HIGHEST, preferred_element_type=jnp.float32
    )
    grad_modulation = jnp.concatenate(
        [grad_mod_rows, jnp.sum(grad_mods, axis=0, keepdims=True)], axis=0
    )
    if fast:
        sums_qkv, mod_sum = reduce_tiles([grad_qkv], mod_sums(grad_modulation), [], 9, 2)
        sums = [sums_qkv, sums_late, sums_mid, sums_up, sums_down]
        order = (0, 1, 2, 5, 6, 3, 7, 4, 8, 9, 10, 11, 12, 13, 14, 15)
        tile_grad = to_owners(sums, order, tile_slots, 10).reshape(master.shape)
        mod_grad = mod_sum.reshape(-1)[: modulation.size].reshape(modulation.shape)
        tile_grad, mod_grad = tile_grad.astype(jnp.float32), mod_grad.astype(jnp.float32)
    else:
        logical = [grad_qkv[0], grad_qkv[1], grad_qkv[2], grad_out_one, grad_tile_query]
        logical = logical + [grad_tiles_pair[0], grad_tiles_pair[1], grad_out_two]
        logical = logical + [grad_up[tile] for tile in range(4)]
        logical = logical + [grad_down[tile] for tile in range(4)]
        tile_grad = sums_generic(logical, tile_slots).astype(jnp.float32)
        mod_grad = mod_generic(grad_modulation)
    new_master, new_moment1, new_moment2 = adamw(master, tile_grad, moment1, moment2, RATE_TILES)
    new_modulation, new_mod_moment1, new_mod_moment2 = adamw(
        modulation, mod_grad, mod_moment1, mod_moment2, RATE_MODULATION
    )
    return (
        block_output,
        grad_triplane,
        grad_image,
        new_master,
        new_moment1,
        new_moment2,
        new_master.astype(jnp.bfloat16),
        new_modulation,
        new_mod_moment1,
        new_mod_moment2,
    )


def solution(mesh):
    in_specs = (
        P("dp", "fsdp", None),
        P("dp", "fsdp", None),
        P("dp", None),
        P("dp"),
        P("dp", "fsdp", None),
        P("dp", "fsdp", None),
        P("dp", "fsdp", None),
        P(),
        P(None, ("dp", "fsdp")),
        P(None, ("dp", "fsdp")),
        P(None, ("dp", "fsdp")),
        P("dp", "fsdp", None),
    )
    out_specs = (
        P("dp", "fsdp", None),
        P("dp", "fsdp", None),
        P("dp", "fsdp", None),
        P("dp", "fsdp", None),
        P("dp", "fsdp", None),
        P("dp", "fsdp", None),
        P("dp", "fsdp", None),
        P(None, ("dp", "fsdp")),
        P(None, ("dp", "fsdp")),
        P(None, ("dp", "fsdp")),
    )
    return jax.shard_map(shards, mesh=mesh, in_specs=in_specs, out_specs=out_specs, check_vma=False)
```

```python
import functools

import jax
import jax.numpy as jnp
from jax import lax
from jax.experimental import pallas as pl
from jax.experimental.pallas import tpu as pltpu
from jax.sharding import PartitionSpec as P

HD = 64
STEP = 5
VIEW = 1024
LANES = 128


HIGHEST = lax.Precision.HIGHEST
NEGATIVE = -1e30
BETA_ONE = 0.5
BETA_TWO = 0.5
EPSILON = 1e-08
WEIGHT_DECAY = 0.01
RATE_TILES = 0.03
RATE_MODULATION = 0.15


def contract(form, left, right):
    return jnp.einsum(form, left, right, preferred_element_type=jnp.float32)


def layer_norm(values):
    center = values - jnp.mean(values, axis=-1, keepdims=True)
    spread = jnp.mean(center * center, axis=-1, keepdims=True)
    return center * lax.rsqrt(spread + 1e-06)


def modulate(values, shift, scale):
    return layer_norm(values) * (1.0 + scale) + shift


def modulate_back(values, shift, scale, grad_normed):
    unused, pull = jax.vjp(modulate, values, shift, scale)
    return pull(grad_normed)


def gelu_tanh(values):
    return jax.nn.gelu(values, approximate=True)


NT = (((1,), (1,)), ((), ()))
NN = (((1,), (0,)), ((), ()))
TN = (((0,), (0,)), ((), ()))


def dot(left, right, dims):
    return lax.dot_general(left, right, dims, preferred_element_type=jnp.float32)


def head_part(values, head, heads):
    if heads == 1:
        return values
    lanes = lax.broadcasted_iota(jnp.int32, values.shape, 1)
    return jnp.where(lanes // HD == head, values, jnp.zeros_like(values))


def rows_of(ref, start, amount):
    block = ref[pl.ds(start, amount), 0]
    return block.reshape(block.shape[0] * block.shape[1], block.shape[2])


def forward_body(step_rows, first_object, live_ref, q_ref, k_ref, v_ref, out_ref, lse_ref):
    key_groups, unused_one, key_rows, width = k_ref.shape
    heads = width // HD
    per_block = step_rows // key_rows
    blocks = live_ref[pl.program_id(0) + first_object] // step_rows
    queries = rows_of(q_ref, 0, q_ref.shape[0]) * jnp.bfloat16(0.125)
    result = jnp.zeros(queries.shape, jnp.float32)
    for head in range(heads):
        own = head_part(queries, head, heads)

        def step(position, carried, own=own):
            highest, total, acc = carried
            keys = rows_of(k_ref, position * per_block, per_block)
            values = rows_of(v_ref, position * per_block, per_block)
            scores = dot(own, keys, NT)
            new_highest = jnp.maximum(highest, jnp.max(scores, axis=1, keepdims=True))
            weights = jnp.exp(scores - new_highest)
            scale = jnp.exp(highest - new_highest)
            total = total * scale + jnp.sum(weights, axis=1, keepdims=True)
            acc = acc * scale + dot(weights.astype(jnp.bfloat16), values, NN)
            return (new_highest, total, acc)

        first = (
            jnp.full((own.shape[0], 1), -jnp.inf, jnp.float32),
            jnp.zeros((own.shape[0], 1), jnp.float32),
            jnp.zeros(own.shape, jnp.float32),
        )
        highest, total, acc = lax.fori_loop(0, blocks, step, first)
        result = result + head_part(acc / total, head, heads)
        level = jnp.broadcast_to(highest + jnp.log(total), (own.shape[0], 128))
        lse_ref[0, head] = jnp.transpose(level)[0:1]
    out_ref[...] = result.astype(jnp.bfloat16).reshape(out_ref.shape)


def attend_forward(live, query_source, key_source, value_source, query_block, step_rows, span):
    (q_array, *q_at), (k_array, *k_at), (v_array, *v_at) = query_source, key_source, value_source
    groups, unused_blocks, unused_objects, q_rows, width = q_array.shape
    first_object, objects = span
    k_rows = k_array.shape[3]
    heads = width // HD
    total_q = groups * q_rows
    per_q = query_block // q_rows
    grid = (objects, total_q // query_block)
    whole = lambda at: (lambda o, j, live: (0, at[0], o + at[1], 0, 0))
    part = lambda at: (lambda o, j, live: (j, at[0], o + at[1], 0, 0))
    return pl.pallas_call(
        functools.partial(forward_body, step_rows, first_object),
        grid_spec=pltpu.PrefetchScalarGridSpec(
            num_scalar_prefetch=1,
            grid=grid,
            in_specs=[
                pl.BlockSpec((per_q, None, 1, q_rows, width), part(q_at)),
                pl.BlockSpec((groups, None, 1, k_rows, width), whole(k_at)),
                pl.BlockSpec((groups, None, 1, k_rows, width), whole(v_at)),
            ],
            out_specs=[
                pl.BlockSpec((per_q, 1, q_rows, width), lambda o, j, live: (j, o, 0, 0)),
                pl.BlockSpec((1, heads, 1, query_block), lambda o, j, live: (o, 0, 0, j)),
            ],
        ),
        out_shape=[
            jax.ShapeDtypeStruct((groups, objects, q_rows, width), jnp.bfloat16),
            jax.ShapeDtypeStruct((objects, heads, 1, total_q), jnp.float32),
        ],
        cost_estimate=pl.CostEstimate(
            flops=4 * objects * total_q * groups * k_rows * width,
            bytes_accessed=4 * objects * groups * (q_rows + k_rows) * width,
            transcendentals=objects * heads * total_q * groups * k_rows,
        ),
    )(live, q_array, k_array, v_array)


def backward_prepare(q_ref, out_ref, grad_ref, qs, gs, delta):
    heads = qs.shape[0]
    queries = rows_of(q_ref, 0, q_ref.shape[0]) * jnp.bfloat16(0.125)
    grads = rows_of(grad_ref, 0, grad_ref.shape[0])
    outs = rows_of(out_ref, 0, out_ref.shape[0])
    product = jnp.transpose(grads.astype(jnp.float32) * outs.astype(jnp.float32))
    for head in range(heads):
        qs[head] = head_part(queries, head, heads)
        gs[head] = head_part(grads, head, heads)
        delta[head] = jnp.sum(product[head * HD : (head + 1) * HD], axis=0, keepdims=True)


def backward_block(keys, values, lse_ref, qs, gs, delta):
    heads = qs.shape[0]
    grad_q, grad_k, grad_v = None, None, None
    for head in range(heads):
        own, grads = qs[head], gs[head]
        weights = jnp.exp(dot(keys, own, NT) - lse_ref[0, head])
        grad_weights = dot(values, grads, NT)
        grad_scores = (weights * (grad_weights - delta[head])).astype(jnp.bfloat16)
        new_v = dot(weights.astype(jnp.bfloat16), grads, NN)
        new_k = dot(grad_scores, own, NN)
        new_q = dot(grad_scores, head_part(keys, head, heads), TN)
        grad_q = new_q if grad_q is None else grad_q + new_q
        grad_k = new_k if grad_k is None else grad_k + new_k
        grad_v = new_v if grad_v is None else grad_v + new_v
    return grad_q, grad_k, grad_v


def cross_backward_body(
    first_object, live_ref, q_ref, k_ref, v_ref, out_ref, lse_ref, grad_ref, dq_ref, dkv_ref, qs, gs, delta, dq_acc
):
    position = pl.program_id(1)
    width = q_ref.shape[3]
    rows = k_ref.shape[0] * k_ref.shape[2]

    @pl.when(position == 0)
    def _():
        backward_prepare(q_ref, out_ref, grad_ref, qs, gs, delta)
        dq_acc[...] = jnp.zeros_like(dq_acc)

    alive = position * rows < live_ref[pl.program_id(0) + first_object]

    @pl.when(alive)
    def _():
        keys = rows_of(k_ref, 0, k_ref.shape[0])
        values = rows_of(v_ref, 0, v_ref.shape[0])
        grad_q, grad_k, grad_v = backward_block(keys, values, lse_ref, qs, gs, delta)
        dq_acc[...] += grad_q
        shape = (k_ref.shape[0], 1, k_ref.shape[2], width)
        dkv_ref[:, 0] = grad_k.astype(jnp.bfloat16).reshape(shape)
        dkv_ref[:, 1] = grad_v.astype(jnp.bfloat16).reshape(shape)

    @pl.when(jnp.logical_not(alive))
    def _():
        dkv_ref[...] = jnp.zeros_like(dkv_ref)

    @pl.when(position == pl.num_programs(1) - 1)
    def _():
        dq_ref[...] = (dq_acc[...] * 0.125).astype(jnp.bfloat16).reshape(dq_ref.shape)


def attend_backward(live, query_source, key_source, value_source, outs, lse, grads, step_rows, span):
    (q_array, *q_at), (k_array, *k_at), (v_array, *v_at) = query_source, key_source, value_source
    groups, unused_blocks, unused_objects, q_rows, width = q_array.shape
    first_object, objects = span
    k_rows = k_array.shape[3]
    heads = width // HD
    total_q = groups * q_rows
    per_k = max(step_rows // k_rows, 1)
    grid = (objects, groups // per_k)
    whole = lambda at: (lambda o, j, live: (0, at[0], o + at[1], 0, 0))
    part = lambda at: (lambda o, j, live: (j, at[0], o + at[1], 0, 0))
    tokens = pl.BlockSpec((groups, 1, q_rows, width), lambda o, j, live: (0, o, 0, 0))
    return pl.pallas_call(
        functools.partial(cross_backward_body, first_object),
        grid_spec=pltpu.PrefetchScalarGridSpec(
            num_scalar_prefetch=1,
            grid=grid,
            in_specs=[
                pl.BlockSpec((groups, None, 1, q_rows, width), whole(q_at)),
                pl.BlockSpec((per_k, None, 1, k_rows, width), part(k_at)),
                pl.BlockSpec((per_k, None, 1, k_rows, width), part(v_at)),
                tokens,
                pl.BlockSpec((1, heads, 1, total_q), lambda o, j, live: (o, 0, 0, 0)),
                pl.BlockSpec((groups, None, 1, q_rows, width), whole((0, first_object))),
            ],
            out_specs=[
                pl.BlockSpec((groups, 1, q_rows, width), lambda o, j, live: (0, o, 0, 0)),
                pl.BlockSpec((per_k, 2, 1, k_rows, width), lambda o, j, live: (j, 0, o, 0, 0)),
            ],
            scratch_shapes=[
                pltpu.VMEM((heads, total_q, width), jnp.bfloat16),
                pltpu.VMEM((heads, total_q, width), jnp.bfloat16),
                pltpu.VMEM((heads, 1, total_q), jnp.float32),
                pltpu.VMEM((total_q, width), jnp.float32),
            ],
        ),
        out_shape=[
            jax.ShapeDtypeStruct((groups, objects, q_rows, width), jnp.bfloat16),
            jax.ShapeDtypeStruct((groups, 2, objects, k_rows, width), jnp.bfloat16),
        ],
        cost_estimate=pl.CostEstimate(
            flops=10 * objects * total_q * groups * k_rows * width,
            bytes_accessed=8 * objects * groups * (q_rows + k_rows) * width,
            transcendentals=objects * heads * total_q * groups * k_rows,
        ),
    )(live, q_array, k_array, v_array, outs, lse, grads)

CHUNKS = ((5, 6), (0, 1, 2), (3, 4, 7), (8, 9, 10, 11), (12, 13, 14, 15))
EARLY = 8
GATHER_PARTS = 1
MOD_ROWS = 16
MESH = pl.DeviceIdType.MESH


def places():
    dp_index, fsdp_index = lax.axis_index("dp"), lax.axis_index("fsdp")
    return dp_index, fsdp_index, fsdp_index // 2, fsdp_index % 2


def z_peer(fsdp_index, shift):
    return {"fsdp": (fsdp_index + 2 * shift) % 8}


def core_peer(fsdp_index):
    return {"fsdp": fsdp_index + 1 - 2 * (fsdp_index % 2)}


def dp_peer(dp_index, flip):
    return {"dp": dp_index ^ flip}


def greet(peers):
    barrier = pltpu.get_barrier_semaphore()
    for peer in peers:
        pl.semaphore_signal(barrier, inc=1, device_id=peer, device_id_type=MESH)
    pl.semaphore_wait(barrier, len(peers))


def remote(source, target, send_sem, recv_sem, peer):
    copy = pltpu.make_async_remote_copy(
        source, target, send_sem, recv_sem, device_id=peer, device_id_type=MESH
    )
    copy.start()
    return copy


def columns(index):
    return pl.ds(pl.multiple_of(index * LANES, LANES), LANES)


def fsdp_peers(fsdp_index):
    return [{"fsdp": (fsdp_index + shift) % 8} for shift in range(1, 8)]


def mix_begin(kind, sources, target, scratch, fsdp_index):
    sems, holds = scratch[0], scratch[1:]

    def ends(place, peer):
        if kind == "heads":
            return sources[0].at[:, :, :, columns(peer)], target.at[fsdp_index]
        mine = columns(fsdp_index)
        if kind == "objects":
            return sources[place].at[peer], target.at[0, place : place + 1, :, mine]
        if len(sources[place].shape) == 4:
            return sources[place].at[peer], target.at[place, :, :, mine]
        return sources[place].at[peer], target.at[place : place + 2, :, :, mine]

    copies, stays = [], []
    for shift in (4, 5, 3, 6, 2, 7, 1):
        peer = (fsdp_index + shift) % 8
        for place in range(len(sources)):
            theirs, there = ends(place, peer)
            copies.append(
                remote(theirs, there, sems.at[0, place, shift], sems.at[1, place, shift], {"fsdp": peer})
            )
    for place in range(len(sources)):
        ours, here = ends(place, fsdp_index)
        load = pltpu.make_async_copy(ours, holds[place], sems.at[0, place, 0])
        load.start()
        stays.append((load, pltpu.make_async_copy(holds[place], here, sems.at[1, place, 0])))
    return copies, stays


def mix_own(moving):
    for load, store in moving[1]:
        load.wait()
        store.start()


def mix_end(moving):
    for load, store in moving[1]:
        store.wait()
    for copy in moving[0]:
        copy.wait()


def mix_plan(mix):
    kind, sources = mix
    bf = jnp.bfloat16
    holds, blocks = [], 0
    for array in sources:
        if kind == "heads":
            holds.append(array.shape[:3] + (array.shape[3] // 8,))
            result = (8,) + holds[0]
        else:
            holds.append(array.shape[1:])
            blocks += 1 if len(array.shape) == 4 else array.shape[1]
            if kind == "objects":
                result = (1, len(sources), array.shape[2], 8 * array.shape[3])
                continue
            result = (blocks,) + array.shape[-3:-1] + (8 * array.shape[-1],)
    scratch = [pltpu.SemaphoreType.DMA((2, len(sources), 8))] + [pltpu.VMEM(hold, bf) for hold in holds]
    return scratch, jax.ShapeDtypeStruct(result, bf)


def mix_body(kind, amount, *refs):
    sources, target, scratch = refs[:amount], refs[amount], refs[amount + 1 :]
    fsdp_index = lax.axis_index("fsdp")
    greet(fsdp_peers(fsdp_index))
    moving = mix_begin(kind, sources, target, scratch, fsdp_index)
    mix_own(moving)
    mix_end(moving)


def mix_alone(mix, collective):
    kind, sources = mix
    scratch, result = mix_plan(mix)
    return pl.pallas_call(
        functools.partial(mix_body, kind, len(sources)),
        in_specs=[ANY] * len(sources),
        out_specs=ANY,
        scratch_shapes=scratch,
        out_shape=result,
        compiler_params=comm_params(collective),
        cost_estimate=pl.CostEstimate(flops=0, bytes_accessed=30_000_000, transcendentals=0),
    )(*sources)


def part_of(ref, unit, dims):
    tile, part = unit // GATHER_PARTS, unit % GATHER_PARTS
    rows = ref.shape[-2] // GATHER_PARTS
    return ref.at[(tile,) + (slice(None),) * dims + (pl.ds(part * rows, rows),)]


def send_z(unit, full, fsdp_index, dp_index, z_index, sems):
    own = full.at[z_index, dp_index]
    return [
        remote(own, own, sems[0].at[unit, shift - 1], sems[1].at[unit, shift - 1], z_peer(fsdp_index, shift))
        for shift in (1, 2, 3)
    ]


def spread(units, fulls, outs, z_copies, z_local, sems, where):
    send_sems, recv_sems, out_sems = sems
    dp_index, fsdp_index, z_index, core = where
    near_x, near_y = dp_peer(dp_index, 1), dp_peer(dp_index, 2)
    first, second, last = {}, {}, []
    for step in range(units + 2):
        if step < units:
            unit, full = step, fulls[step]
            for copy in z_copies[unit]:
                copy.wait() if z_local else copy.wait_recv()
            low, high = full.at[0:2, dp_index], full.at[2:4, dp_index]
            pairs = [(low, near_x), (high, near_y), (low, near_y), (high, near_x)]
            first[unit] = [
                remote(ref, ref, send_sems.at[unit, 3 + n], recv_sems.at[unit, 3 + n], peer)
                for n, (ref, peer) in enumerate(pairs)
            ]
        if 0 <= step - 1 < units:
            unit, full = step - 1, fulls[step - 1]
            first[unit][0].wait_recv()
            first[unit][1].wait_recv()
            low, high = full.at[0:2, dp_index ^ 1], full.at[2:4, dp_index ^ 2]
            pairs = [(low, near_y), (high, near_x)]
            second[unit] = [
                remote(ref, ref, send_sems.at[unit, 7 + n], recv_sems.at[unit, 7 + n], peer)
                for n, (ref, peer) in enumerate(pairs)
            ]
        if 0 <= step - 2 < units:
            unit, full, out = step - 2, fulls[step - 2], outs[step - 2]
            for copy in first[unit][2:] + second[unit]:
                copy.wait_recv()
            target = out.at[:, core]
            last.append(
                remote(full, target, send_sems.at[unit, 9], recv_sems.at[unit, 9], core_peer(fsdp_index))
            )
            here = pltpu.make_async_copy(full, target, out_sems.at[unit])
            here.start()
            last.append(here)
    for unit in range(units):
        for copy in first[unit] + second[unit]:
            copy.wait_send()
    for copy in last:
        copy.wait()


def first_gather_body(tiles, rows, index_ref, narrow_ref, mod_ref, out_ref, mod_out_ref, wait_ref, rest_ref, stacked, mine, full, mod_full, zoned, swap_sems, load_sems, send_sems, recv_sems, out_sems, zone_sems):
    where = places()
    dp_index, fsdp_index, z_index, core = where
    peers = [z_peer(fsdp_index, shift) for shift in (1, 2, 3)]
    peers += [dp_peer(dp_index, flip) for flip in (1, 2, 3)] + [core_peer(fsdp_index)]
    greet(peers)
    swaps = [
        remote(narrow_ref.at[:, dp_index ^ flip], stacked.at[pl.ds(4 * flip, 4)], swap_sems.at[0, flip], swap_sems.at[1, flip], dp_peer(dp_index, flip))
        for flip in (1, 2, 3)
    ]
    own = pltpu.make_async_copy(narrow_ref.at[:, dp_index], stacked.at[pl.ds(0, 4)], load_sems.at[0])
    own.start()
    mod_load = pltpu.make_async_copy(mod_ref, mod_full.at[z_index, dp_index], load_sems.at[1])
    mod_load.start()
    mod_load.wait()
    units = tiles * GATHER_PARTS
    z_copies = {units: send_z(units, mod_full, fsdp_index, dp_index, z_index, (send_sems, recv_sems))}
    own.wait()
    for swap in swaps:
        swap.wait()
    for tile in range(tiles):
        full[tile, z_index, dp_index] = stacked[index_ref[tile]]
        for unit in range(tile * GATHER_PARTS, (tile + 1) * GATHER_PARTS):
            z_copies[unit] = send_z(unit, part_of(full, unit, 2), fsdp_index, dp_index, z_index, (send_sems, recv_sems))

    def take(position, carried):
        mine[position] = stacked[index_ref[position + tiles]]
        return carried

    lax.fori_loop(0, 16 - tiles, take, 0)
    early = EARLY - tiles
    zone = [
        remote(mine.at[pl.ds(0, early)], zoned.at[z_index], zone_sems.at[0, shift - 1], zone_sems.at[1, shift - 1], z_peer(fsdp_index, shift))
        for shift in (1, 2, 3)
    ]
    zone_own = pltpu.make_async_copy(mine.at[pl.ds(0, early)], wait_ref.at[z_index], load_sems.at[2])
    zone_own.start()
    rest = pltpu.make_async_copy(mine.at[pl.ds(early, 16 - EARLY)], rest_ref, load_sems.at[3])
    rest.start()
    fulls = [part_of(full, unit, 2) for unit in range(units)] + [mod_full]
    outs = [part_of(out_ref, unit, 3) for unit in range(units)] + [mod_out_ref]
    spread(units + 1, fulls, outs, z_copies, False, (send_sems, recv_sems, out_sems), where)
    for unit in range(units + 1):
        for copy in z_copies[unit]:
            copy.wait_send()
    for copy in zone:
        copy.wait()
    zone_own.wait()
    rest.wait()
    stores = []
    for shift in (1, 2, 3):
        z_from = (z_index + shift) % 4
        store = pltpu.make_async_copy(zoned.at[z_from], wait_ref.at[z_from], load_sems.at[3 + shift])
        store.start()
        stores.append(store)
    for store in stores:
        store.wait()


ANY = pl.BlockSpec(memory_space=pl.ANY)


def comm_params(collective):
    return pltpu.CompilerParams(
        collective_id=collective, has_side_effects=True, vmem_limit_bytes=58 * 1024 * 1024
    )


def first_gather(narrow, mod_rows, index):
    tiles = len(CHUNKS[0])
    slots, owners, rows, width = narrow.shape
    bf = jnp.bfloat16
    return pl.pallas_call(
        functools.partial(first_gather_body, tiles, rows),
        grid_spec=pltpu.PrefetchScalarGridSpec(
            num_scalar_prefetch=1,
            grid=(),
            in_specs=[ANY, ANY],
            out_specs=[ANY] * 4,
            scratch_shapes=[
                pltpu.VMEM((16, rows, width), bf),
                pltpu.VMEM((16 - tiles, rows, width), bf),
                pltpu.VMEM((tiles, 4, 4, rows, width), bf),
                pltpu.VMEM((4, 4, MOD_ROWS, width), bf),
                pltpu.VMEM((4, EARLY - tiles, rows, width), bf),
                pltpu.SemaphoreType.DMA((2, 4)),
                pltpu.SemaphoreType.DMA((8,)),
                pltpu.SemaphoreType.DMA((tiles * GATHER_PARTS + 1, 10)),
                pltpu.SemaphoreType.DMA((tiles * GATHER_PARTS + 1, 10)),
                pltpu.SemaphoreType.DMA((tiles * GATHER_PARTS + 1,)),
                pltpu.SemaphoreType.DMA((2, 3)),
            ],
        ),
        out_shape=[
            jax.ShapeDtypeStruct((tiles, 4, 2, 4, rows, width), bf),
            jax.ShapeDtypeStruct((4, 2, 4, MOD_ROWS, width), bf),
            jax.ShapeDtypeStruct((4, EARLY - tiles, rows, width), bf),
            jax.ShapeDtypeStruct((16 - EARLY, rows, width), bf),
        ],
        compiler_params=comm_params(0),
        cost_estimate=pl.CostEstimate(flops=0, bytes_accessed=200_000_000, transcendentals=0),
    )(index, narrow, mod_rows)


def next_gather_body(tiles, start, zoned, plans, ahead, source_ref, *refs):
    mix_sources = []
    for unused_kind, amount in plans:
        mix_sources.append(refs[:amount])
        refs = refs[amount:]
    out_ref, refs = refs[0], refs[1:]
    mixed_refs, refs = refs[: len(plans)], refs[len(plans) :]
    if ahead:
        zone_ref, refs = refs[0], refs[1:]
        zone_hold, zone_sems, refs = refs[0], refs[1], refs[2:]
    (full, load_sems, send_sems, recv_sems, out_sems), refs = refs[:5], refs[5:]
    where = places()
    dp_index, fsdp_index, z_index, core = where
    loads = []
    for tile in range(tiles):
        if zoned:
            load = pltpu.make_async_copy(source_ref.at[:, start + tile], full.at[tile, :, dp_index], load_sems.at[tile])
        else:
            load = pltpu.make_async_copy(source_ref.at[start + tile], full.at[tile, z_index, dp_index], load_sems.at[tile])
        load.start()
        loads.append(load)
    units = tiles * GATHER_PARTS
    peers = [dp_peer(dp_index, flip) for flip in (1, 2)]
    if plans:
        peers += fsdp_peers(fsdp_index)
    else:
        peers += [core_peer(fsdp_index)]
        peers += [] if zoned else [z_peer(fsdp_index, shift) for shift in (1, 2, 3)]
    greet(peers)
    z_copies = {}
    for tile in range(tiles):
        near = range(tile * GATHER_PARTS, (tile + 1) * GATHER_PARTS)
        if zoned:
            for unit in near:
                z_copies[unit] = [loads[tile]] if unit == near[0] else []
        else:
            loads[tile].wait()
            for unit in near:
                z_copies[unit] = send_z(unit, part_of(full, unit, 2), fsdp_index, dp_index, z_index, (send_sems, recv_sems))
    movings = []
    for place, (kind, amount) in enumerate(plans):
        mix_scratch, refs = refs[: 1 + amount], refs[1 + amount :]
        movings.append(mix_begin(kind, mix_sources[place], mixed_refs[place], mix_scratch, fsdp_index))
    for moving in movings:
        mix_own(moving)
    if ahead:
        later = source_ref.at[pl.ds(ahead[0], ahead[1])]
        zone = [
            remote(later, zone_ref.at[z_index], zone_sems.at[0, shift], zone_sems.at[1, shift], z_peer(fsdp_index, shift))
            for shift in (1, 2, 3)
        ]
        zone_load = pltpu.make_async_copy(later, zone_hold, zone_sems.at[0, 0])
        zone_load.start()
        zone_load.wait()
        zone_store = pltpu.make_async_copy(zone_hold, zone_ref.at[z_index], zone_sems.at[1, 0])
        zone_store.start()
    fulls = [part_of(full, unit, 2) for unit in range(units)]
    outs = [part_of(out_ref, unit, 3) for unit in range(units)]
    spread(units, fulls, outs, z_copies, zoned, (send_sems, recv_sems, out_sems), where)
    if not zoned:
        for unit in range(units):
            for copy in z_copies[unit]:
                copy.wait_send()
    for moving in movings:
        mix_end(moving)
    if ahead:
        for copy in zone:
            copy.wait()
        zone_store.wait()


def next_gather(source, tiles, start, zoned, mixes, ahead, collective):
    rows, width = source.shape[-2:]
    bf = jnp.bfloat16
    operands = [source]
    out_shape = [jax.ShapeDtypeStruct((tiles, 4, 2, 4, rows, width), bf)]
    scratch = [
        pltpu.VMEM((tiles, 4, 4, rows, width), bf),
        pltpu.SemaphoreType.DMA((tiles,)),
        pltpu.SemaphoreType.DMA((tiles * GATHER_PARTS, 10)),
        pltpu.SemaphoreType.DMA((tiles * GATHER_PARTS, 10)),
        pltpu.SemaphoreType.DMA((tiles * GATHER_PARTS,)),
    ]
    for mix in mixes:
        operands += list(mix[1])
        extra, result = mix_plan(mix)
        scratch, out_shape = scratch + extra, out_shape + [result]
    plans = tuple((kind, len(sources)) for kind, sources in mixes)
    if ahead:
        scratch = [pltpu.VMEM((ahead[1], rows, width), bf), pltpu.SemaphoreType.DMA((2, 4))] + scratch
        out_shape = out_shape + [jax.ShapeDtypeStruct((4, ahead[1], rows, width), bf)]
    results = pl.pallas_call(
        functools.partial(next_gather_body, tiles, start, zoned, plans, ahead),
        in_specs=[ANY] * len(operands),
        out_specs=[ANY] * len(out_shape),
        scratch_shapes=scratch,
        out_shape=out_shape,
        compiler_params=comm_params(collective),
        cost_estimate=pl.CostEstimate(flops=0, bytes_accessed=tiles * 30_000_000, transcendentals=0),
    )(*operands)
    return [results[0].reshape(tiles, 32 * rows, width)] + list(results[1:])


def fast_layout(master):
    owners, groups = lax.axis_size("dp"), lax.axis_size("fsdp")
    return owners == 4 and groups == 8 and master.shape[1:] == (128, 1024)


def fetch_generic(master, modulation, tile_slots):
    narrow = master.astype(jnp.bfloat16)
    mod_narrow = modulation.astype(jnp.bfloat16)[:, None, None, :]
    row_blocks = lax.all_gather(narrow, "fsdp", axis=1, tiled=True)
    mod_blocks = lax.all_gather(mod_narrow, "fsdp", axis=2, tiled=True)
    gathered = lax.all_gather(row_blocks, "dp", axis=0, tiled=True)
    mod_all = lax.all_gather(mod_blocks, "dp", axis=1, tiled=True)
    chunks = [
        jnp.stack(
            [lax.dynamic_index_in_dim(gathered, tile_slots[tile], 0, keepdims=False) for tile in chunk]
        )
        for chunk in CHUNKS
    ]
    return chunks, mod_all.reshape(mod_all.shape[0], -1)


def sums_generic(logical, tile_slots):
    slot_grads = jnp.zeros((len(logical),) + logical[0].shape, jnp.bfloat16)
    for position, grad in enumerate(logical):
        slot_grads = lax.dynamic_update_index_in_dim(
            slot_grads, grad.astype(jnp.bfloat16), tile_slots[position], 0
        )
    row_sums = lax.psum_scatter(slot_grads, "fsdp", scatter_dimension=1, tiled=True)
    return lax.psum_scatter(row_sums, "dp", scatter_dimension=0, tiled=True)


def mod_generic(grad_modulation):
    owners, groups = lax.axis_size("dp"), lax.axis_size("fsdp")
    rows, width = grad_modulation.shape
    blocks = grad_modulation.reshape(rows, owners, groups, width // (owners * groups))
    sums = lax.psum_scatter(blocks.astype(jnp.bfloat16), "fsdp", scatter_dimension=2, tiled=True)
    sums = lax.psum_scatter(sums, "dp", scatter_dimension=1, tiled=True)
    return sums.reshape(rows, -1).astype(jnp.float32)


def wide(value):
    return value.astype(jnp.float32)


def reduce_scratch(tiles, rows, width):
    bf, f32 = jnp.bfloat16, jnp.float32
    return [
        pltpu.VMEM((2, tiles, 4, 4, rows, width), bf),
        pltpu.VMEM((4, tiles, 2, 2, rows, width), bf),
        pltpu.VMEM((2, tiles, 2, 2, rows, width), f32),
        pltpu.VMEM((4, tiles, 2, rows, width), bf),
        pltpu.VMEM((tiles, 4, rows, width), f32),
        pltpu.VMEM((2, 3, tiles, rows, width), bf),
        pltpu.VMEM((tiles, rows, width), bf),
        pltpu.SemaphoreType.DMA((2, tiles)),
        pltpu.SemaphoreType.DMA((8, tiles)),
        pltpu.SemaphoreType.DMA((8, tiles)),
    ]


def reduce_stages(tiles, scratch, out_ref, where):
    core_buf, swap, kept, swap_two, whole, zbuf, out_buf, load_sems, send_sems, recv_sems = scratch
    dp_index, fsdp_index, z_index, core = where
    x_bit, y_bit = dp_index % 2, dp_index // 2
    near_x, near_y = dp_peer(dp_index, 1), dp_peer(dp_index, 2)

    def moved(stage, tile):
        if stage == 1:
            ends = (swap.at[0, tile], swap.at[1, tile], near_x)
        elif stage == 2:
            ends = (swap.at[2, tile], swap.at[3, tile], near_y)
        elif stage == 3:
            ends = (swap_two.at[0, tile], swap_two.at[1, tile], near_y)
        elif stage == 4:
            ends = (swap_two.at[2, tile], swap_two.at[3, tile], near_x)
        else:
            shift = stage - 4
            ends = (zbuf.at[0, shift - 1, tile], zbuf.at[1, shift - 1, tile], z_peer(fsdp_index, shift))
        return pltpu.make_async_remote_copy(
            ends[0], ends[1], send_sems.at[stage, tile], recv_sems.at[stage, tile], device_id=ends[2], device_id_type=MESH
        )

    def both(tile, z_place, quarter):
        return wide(core_buf[0, tile, z_place, quarter]) + wide(core_buf[1, tile, z_place, quarter])

    def add_core(tile):
        for side in range(2):
            for other in range(2):
                kept[0, tile, side, other] = both(tile, side, 2 * other + x_bit)
                swap[0, tile, side, other] = both(tile, side, 2 * other + 1 - x_bit).astype(jnp.bfloat16)
                kept[1, tile, side, other] = both(tile, 2 + side, 2 * y_bit + other)
                swap[2, tile, side, other] = both(tile, 2 + side, 2 * (1 - y_bit) + other).astype(jnp.bfloat16)
        moved(1, tile).start()
        moved(2, tile).start()

    def add_first(tile):
        moved(1, tile).wait_recv()
        moved(2, tile).wait_recv()
        for side in range(2):
            whole[tile, side] = kept[0, tile, side, y_bit] + wide(swap[1, tile, side, y_bit])
            away = kept[0, tile, side, 1 - y_bit] + wide(swap[1, tile, side, 1 - y_bit])
            swap_two[0, tile, side] = away.astype(jnp.bfloat16)
            whole[tile, 2 + side] = kept[1, tile, side, x_bit] + wide(swap[3, tile, side, x_bit])
            away = kept[1, tile, side, 1 - x_bit] + wide(swap[3, tile, side, 1 - x_bit])
            swap_two[2, tile, side] = away.astype(jnp.bfloat16)
        moved(3, tile).start()
        moved(4, tile).start()

    def add_second(tile):
        moved(3, tile).wait_recv()
        moved(4, tile).wait_recv()
        for side in range(2):
            whole[tile, side] = whole[tile, side] + wide(swap_two[1, tile, side])
            whole[tile, 2 + side] = whole[tile, 2 + side] + wide(swap_two[3, tile, side])
        for shift in (1, 2, 3):
            zbuf[0, shift - 1, tile] = whole[tile, (z_index + shift) % 4].astype(jnp.bfloat16)
            moved(4 + shift, tile).start()

    def add_z(tile):
        total = whole[tile, z_index]
        for shift in (1, 2, 3):
            moved(4 + shift, tile).wait_recv()
            total = total + wide(zbuf[1, shift - 1, tile])
        out_buf[tile] = total.astype(jnp.bfloat16)

    def finish(tile):
        for stage in range(1, 8):
            moved(stage, tile).wait_send()

    return add_core, add_first, add_second, add_z, finish


def core_copies(entries, scratch, where):
    core_buf, load_sems, send_sems, recv_sems = scratch[0], scratch[-3], scratch[-2], scratch[-1]
    copies = []
    for tile, (theirs, ours) in enumerate(entries):
        away = remote(theirs, core_buf.at[1, tile], send_sems.at[0, tile], recv_sems.at[0, tile], core_peer(where[1]))
        load = pltpu.make_async_copy(ours, core_buf.at[0, tile], load_sems.at[0, tile])
        load.start()
        copies.append((away, load))
    return copies


def reduce_body(counts, extra, plans, parts, *refs):
    groups = len(counts)
    tiles = sum(counts) * parts
    grads, refs = refs[:groups], refs[groups:]
    if extra:
        mod_grads, refs = refs[0], refs[1:]
    mix_sources = []
    for unused_kind, amount in plans:
        mix_sources.append(refs[:amount])
        refs = refs[amount:]
    out_ref, refs = refs[0], refs[1:]
    if extra:
        mod_out_ref, refs = refs[0], refs[1:]
    mixed_refs, refs = refs[: len(plans)], refs[len(plans) :]
    scratch, refs = refs[:10], refs[10:]
    if extra:
        mod_scratch, refs = refs[:10], refs[10:]
    where = places()
    dp_index, fsdp_index, core = where[0], where[1], where[3]
    peers = [dp_peer(dp_index, flip) for flip in (1, 2)]
    if plans:
        peers += fsdp_peers(fsdp_index)
    else:
        peers += [z_peer(fsdp_index, shift) for shift in (1, 2, 3)] + [core_peer(fsdp_index)]
    greet(peers)
    movings = []
    for place, (kind, amount) in enumerate(plans):
        mix_scratch, refs = refs[: 1 + amount], refs[1 + amount :]
        movings.append(mix_begin(kind, mix_sources[place], mixed_refs[place], mix_scratch, fsdp_index))
    rows = out_ref.shape[1]
    entries = [
        tuple(grads[group].at[tile, :, side, :, pl.ds(part * rows, rows)] for side in (1 - core, core))
        for group in range(groups)
        for tile in range(counts[group])
        for part in range(parts)
    ]
    mod_entry = [(mod_grads.at[0, :, 1 - core], mod_grads.at[0, :, core])] if extra else []
    mod_copies = core_copies(mod_entry, mod_scratch, where) if extra else []
    copies = core_copies(entries, scratch, where)
    for moving in movings:
        mix_own(moving)
    stages = reduce_stages(tiles, scratch, out_ref, where)
    if extra:
        mod_stages = reduce_stages(1, mod_scratch, mod_out_ref, where)
        mod_copies[0][0].wait()
        mod_copies[0][1].wait()
        mod_stages[0](0)

    def arrive(tile):
        pltpu.make_async_copy(scratch[0].at[0, tile], scratch[0].at[0, tile], scratch[-3].at[0, tile]).wait()
        pltpu.make_async_remote_copy(
            scratch[0].at[1, tile], scratch[0].at[1, tile], scratch[-2].at[0, tile], scratch[-1].at[0, tile],
            device_id=core_peer(fsdp_index), device_id_type=MESH,
        ).wait_recv()

    def step(position, carried):
        @pl.when(position < tiles)
        def _():
            arrive(position)
            stages[0](position)

        for place in (1, 2, 3):
            tile = position - place

            @pl.when((tile >= 0) & (tile < tiles))
            def _():
                stages[place](tile)

        return carried

    if extra:
        step(0, 0)
        mod_stages[1](0)
        step(1, 0)
        mod_stages[2](0)
        step(2, 0)
        mod_stages[3](0)
        lax.fori_loop(3, tiles + 3, step, 0)
        mod_stages[4](0)
    else:
        lax.fori_loop(0, tiles + 3, step, 0)

    store = pltpu.make_async_copy(scratch[6], out_ref, scratch[-3].at[1, 0])
    store.start()

    def close(tile, carried):
        stages[4](tile)
        return carried

    lax.fori_loop(0, tiles, close, 0)
    for away, load in copies:
        away.wait_send()
    if extra:
        mod_store = pltpu.make_async_copy(mod_scratch[6], mod_out_ref, mod_scratch[-3].at[1, 0])
        mod_store.start()
        mod_store.wait()
    store.wait()
    for moving in movings:
        mix_end(moving)


def reduce_tiles(grads, mods, mixes, collective, parts=1):
    counts = tuple(part.shape[0] for part in grads)
    tiles = sum(counts) * parts
    rows, width = grads[0].shape[-2:]
    rows = rows // parts
    bf = jnp.bfloat16
    operands = list(grads)
    out_shape = [jax.ShapeDtypeStruct((tiles, rows, width), bf)]
    scratch = reduce_scratch(tiles, rows, width)
    if mods is not None:
        operands.append(mods)
        out_shape.append(jax.ShapeDtypeStruct((1, MOD_ROWS, width), bf))
        scratch = scratch + reduce_scratch(1, MOD_ROWS, width)
    for mix in mixes:
        operands += list(mix[1])
        extra, result = mix_plan(mix)
        scratch, out_shape = scratch + extra, out_shape + [result]
    plans = tuple((kind, len(sources)) for kind, sources in mixes)
    results = pl.pallas_call(
        functools.partial(reduce_body, counts, mods is not None, plans, parts),
        in_specs=[ANY] * len(operands),
        out_specs=[ANY] * len(out_shape),
        scratch_shapes=scratch,
        out_shape=out_shape,
        compiler_params=comm_params(collective),
        cost_estimate=pl.CostEstimate(flops=0, bytes_accessed=tiles * 20_000_000, transcendentals=0),
    )(*operands)
    return [results[0].reshape(-1, rows * parts, width)] + list(results[1:])


def owner_body(counts, index_ref, *refs):
    sources, refs = refs[: len(counts)], refs[len(counts) :]
    out_ref, held, picked, load_sems, send_sems, recv_sems = refs
    dp_index = lax.axis_index("dp")
    loads, start = [], 0
    for place, count in enumerate(counts):
        load = pltpu.make_async_copy(sources[place], held.at[pl.ds(start, count)], load_sems.at[place])
        load.start()
        loads.append(load)
        start += count
    greet([dp_peer(dp_index, flip) for flip in (1, 2, 3)])
    for load in loads:
        load.wait()
    copies = []
    for flip in (3, 1, 2, 0):
        for slot in range(4):
            picked[flip, slot] = held[index_ref[4 * flip + slot]]
        target = out_ref.at[:, dp_index]
        if flip:
            copies.append(
                remote(picked.at[flip], target, send_sems.at[flip], recv_sems.at[flip], dp_peer(dp_index, flip))
            )
        else:
            here = pltpu.make_async_copy(picked.at[flip], target, load_sems.at[0])
            here.start()
            copies.append(here)
    for copy in copies:
        copy.wait()


def to_owners(sums, order, tile_slots, collective):
    rows, width = sums[0].shape[-2:]
    counts = tuple(part.shape[0] for part in sums)
    dp_index = lax.axis_index("dp")
    spots = jnp.arange(16, dtype=jnp.int32)
    wanted = ((spots // 4) ^ dp_index) * 4 + spots % 4
    slots = tile_slots[jnp.array(order, jnp.int32)]
    matches = slots[None, :] == wanted[:, None]
    index = jnp.sum(jnp.where(matches, spots[None, :], 0), axis=1).astype(jnp.int32)
    bf = jnp.bfloat16
    return pl.pallas_call(
        functools.partial(owner_body, counts),
        grid_spec=pltpu.PrefetchScalarGridSpec(
            num_scalar_prefetch=1,
            grid=(),
            in_specs=[ANY] * len(counts),
            out_specs=ANY,
            scratch_shapes=[
                pltpu.VMEM((16, rows, width), bf),
                pltpu.VMEM((4, 4, rows, width), bf),
                pltpu.SemaphoreType.DMA((len(counts),)),
                pltpu.SemaphoreType.DMA((4,)),
                pltpu.SemaphoreType.DMA((4,)),
            ],
        ),
        out_shape=jax.ShapeDtypeStruct((4, 4, rows, width), bf),
        compiler_params=comm_params(collective),
        cost_estimate=pl.CostEstimate(flops=0, bytes_accessed=50_000_000, transcendentals=0),
    )(index, *sums)


def tile_sums(form, left, right):
    total = contract(form, left, right).astype(jnp.bfloat16)
    return total.reshape(-1, 4, 2, 4, total.shape[-2] // 32, total.shape[-1])


def mod_sums(grad_modulation):
    rows, width = grad_modulation.shape
    columns_here = width // 32
    blocks = grad_modulation.reshape(rows, 4, 4, 2, columns_here).transpose(2, 3, 1, 0, 4)
    flat = blocks.astype(jnp.bfloat16).reshape(1, 4, 2, 4, rows * columns_here)
    flat = jnp.pad(flat, ((0, 0),) * 4 + ((0, MOD_ROWS * 1024 - rows * columns_here),))
    return flat.reshape(1, 4, 2, 4, MOD_ROWS, 1024)


def after(value, *others):
    return lax.optimization_barrier((value,) + others)[0]


def weight_source(master, modulation, tile_slots):
    if not fast_layout(master):
        chunks, mod_all = fetch_generic(master, modulation, tile_slots)
        generic = lambda number, mixes, *others: [chunks[number]] + [mix_generic(mix) for mix in mixes]
        return generic, mod_all
    slots_here, row_count, width = master.shape
    dp_index = lax.axis_index("dp")
    narrow = master.astype(jnp.bfloat16).reshape(slots_here, 4, row_count // 4, width)
    index = ((tile_slots // slots_here) ^ dp_index) * slots_here + tile_slots % slots_here
    index = index[jnp.array([tile for chunk in CHUNKS for tile in chunk], jnp.int32)]
    mod_rows, mod_columns = modulation.shape
    mod_flat = modulation.astype(jnp.bfloat16).reshape(-1)
    mod_flat = jnp.pad(mod_flat, (0, MOD_ROWS * width - mod_flat.shape[0])).reshape(MOD_ROWS, width)
    first, mods, zoned, rest = first_gather(narrow, mod_flat, index)
    flat = mods.reshape(8, 4, MOD_ROWS * width)[:, :, : mod_rows * mod_columns]
    mod_all = flat.reshape(8, 4, mod_rows, mod_columns).transpose(2, 1, 0, 3).reshape(mod_rows, -1)

    last_zone = []

    def chunk(number, mixes, *others):
        tiles = len(CHUNKS[number])
        if number == 0:
            return [first.reshape(tiles, row_count * 8, width)]
        if number < 3:
            held = after(zoned, *others) if others else zoned
            return next_gather(held, tiles, (0, 3)[number - 1], True, mixes, None, number)
        if number == 3:
            *results, zone = next_gather(rest, tiles, 0, False, mixes, (tiles, 16 - EARLY - tiles), number)
            last_zone.append(zone)
            return results
        return next_gather(last_zone[0], tiles, 0, True, mixes, None, number)

    return chunk, mod_all


def pair_body(x_ref, w_ref, out_ref):
    objects, rows, width = x_ref.shape
    values = dot(x_ref[...].reshape(objects * rows, width), w_ref[0], NN).astype(jnp.bfloat16)
    for side in range(2):
        part = values[:, side * LANES : (side + 1) * LANES]
        out_ref[side, 0] = part.reshape(objects, rows, LANES)


def project_pairs(tokens, objects, tiles):
    unused_objects, rows, width = tokens.shape
    blocks = tiles.shape[0]
    return pl.pallas_call(
        pair_body,
        grid=(blocks, 4),
        in_specs=[
            pl.BlockSpec((objects, rows, width), lambda k, g: (0, 0, 0)),
            pl.BlockSpec((1, width, 2 * LANES), lambda k, g: (k, 0, g)),
        ],
        out_specs=pl.BlockSpec((2, 1, objects, rows, LANES), lambda k, g: (g, k, 0, 0, 0)),
        out_shape=jax.ShapeDtypeStruct((8, blocks, objects, rows, LANES), jnp.bfloat16),
        cost_estimate=pl.CostEstimate(
            flops=2 * objects * rows * width * blocks * 8 * LANES,
            bytes_accessed=2 * objects * rows * (width + blocks * 8 * LANES),
            transcendentals=0,
        ),
    )(tokens, tiles)


def exchange(pieces):
    return lax.all_to_all(pieces, "fsdp", split_axis=0, concat_axis=0, tiled=True)


def by_head(values, groups):
    blocks, objects, rows, width = values.shape
    moved = values.reshape(blocks, objects, rows, groups, width // groups)
    return moved.transpose(3, 0, 1, 2, 4)


def from_head(pieces):
    groups, blocks, objects, rows, share = pieces.shape
    return pieces.transpose(1, 2, 3, 0, 4).reshape(blocks, objects, rows, groups * share)


def mix_generic(mix):
    if mix is None:
        return None
    kind, sources = mix
    if kind == "heads":
        return exchange(by_head(sources[0], lax.axis_size("fsdp")))
    if kind == "objects":
        sources = [jnp.concatenate(sources, axis=1)]
    parts = [array if array.ndim == 5 else array[:, None] for array in sources]
    return from_head(exchange(jnp.concatenate(parts, axis=1)))


def adamw(weights, grads, first, second, rate):
    first_new = BETA_ONE * first + (1.0 - BETA_ONE) * grads
    second_new = BETA_TWO * second + (1.0 - BETA_TWO) * grads * grads
    first_hat = first_new / (1.0 - BETA_ONE**STEP)
    second_hat = second_new / (1.0 - BETA_TWO**STEP)
    weights_new = weights - rate * (
        first_hat / (jnp.sqrt(second_hat) + EPSILON) + WEIGHT_DECAY * weights
    )
    return (weights_new, first_new, second_new)


def shards(
    triplane,
    image_tokens,
    camera,
    view_tokens,
    master,
    moment1,
    moment2,
    tile_slots,
    modulation,
    mod_moment1,
    mod_moment2,
    cotangent,
):
    objects, tri_local, model_width = triplane.shape
    groups = lax.axis_size("fsdp")
    tri_total = tri_local * groups
    fast = fast_layout(master)
    partial_sums = tile_sums if fast else contract

    def reduced(grads, mods, mixes, collective, parts=1):
        if not fast:
            return [None] + [mix_generic(mix) for mix in mixes]
        return reduce_tiles(grads, mods, mixes, collective, parts)

    chunk, mod_all = weight_source(master, modulation, tile_slots)
    mod_full = mod_all.astype(jnp.float32)
    modulations = (
        jnp.dot(camera, mod_full[:-1], precision=HIGHEST, preferred_element_type=jnp.float32)
        + mod_full[-1]
    )
    blocks = [
        modulations[:, position * model_width : (position + 1) * model_width][:, None, :]
        for position in range(9)
    ]
    half = objects // 2
    (tiles_pair,) = chunk(0, [])
    if fast:
        pair_sent = project_pairs(image_tokens, half, tiles_pair)
    else:
        image_pairs = contract("oid,kde->koie", image_tokens[:half], tiles_pair).astype(jnp.bfloat16)
        pair_sent = by_head(image_pairs, groups)
    pair_early = exchange(pair_sent)
    (tiles_qkv,) = chunk(1, [], pair_sent)
    pairs_late = contract("oid,kde->koie", image_tokens[half:], tiles_pair).astype(jnp.bfloat16)
    residual_in = triplane.astype(jnp.float32)
    normed_one = modulate(residual_in, blocks[0], blocks[1]).astype(jnp.bfloat16)
    triples = contract("otd,kde->kote", normed_one, tiles_qkv).astype(jnp.bfloat16)
    tiles_mixed, triple_heads = chunk(2, [("heads", [triples])])
    tile_out_one, tile_query_two, tile_out_two = tiles_mixed[0], tiles_mixed[1], tiles_mixed[2]
    every_key = jnp.full((objects,), tri_total, jnp.int32)
    self_sources = [(triple_heads, index, 0) for index in range(3)]
    self_result, self_logsum = attend_forward(every_key, *self_sources, tri_total, VIEW, (0, objects))
    tiles_up, merged_one = chunk(3, [("tokens", [self_result])])
    merged_one = merged_one[0]
    branch_one = contract("otd,de->ote", merged_one, tile_out_one)
    residual_mid = residual_in + blocks[2] * branch_one
    normed_two = modulate(residual_mid, blocks[3], blocks[4]).astype(jnp.bfloat16)
    cross_query = contract("otd,de->ote", normed_two, tile_query_two).astype(jnp.bfloat16)
    tiles_down, query_heads, pair_late = chunk(4, [("heads", [cross_query[None]]), ("heads", [pairs_late])])
    cross_sources, cross_result, cross_logsum = [], [], []
    for place in range(objects):
        pair_heads, shift = (pair_early, place) if place < half else (pair_late, place - half)
        sources = [(query_heads, 0, place), (pair_heads, 0, shift), (pair_heads, 1, shift)]
        result, logsum = attend_forward(view_tokens, *sources, tri_total, VIEW, (place, 1))
        cross_sources.append(sources)
        cross_result.append(result)
        cross_logsum.append(logsum)
    cross_mix = ("objects", cross_result)
    merged_two = (mix_alone(cross_mix, 11) if fast else mix_generic(cross_mix))[0]
    branch_two = contract("otd,de->ote", merged_two, tile_out_two)
    residual_late = residual_mid + blocks[5] * branch_two
    normed_three = modulate(residual_late, blocks[6], blocks[7]).astype(jnp.bfloat16)
    hidden_pre = contract("otd,kde->otke", normed_three, tiles_up)
    hidden = gelu_tanh(hidden_pre).astype(jnp.bfloat16)
    branch_three = contract("otkd,kde->ote", hidden, tiles_down)
    block_output = (residual_late + blocks[8] * branch_three).astype(jnp.bfloat16)
    grad_final = cotangent.astype(jnp.float32)
    grad_gate_three = jnp.sum(grad_final * branch_three, axis=1)
    grad_branch_three = (blocks[8] * grad_final).astype(jnp.bfloat16)
    grad_hidden = contract("ote,kde->otkd", grad_branch_three, tiles_down)
    unused_gelu, gelu_pull = jax.vjp(gelu_tanh, hidden_pre)
    grad_pre = gelu_pull(grad_hidden)[0].astype(jnp.bfloat16)
    grad_normed_three = contract("otke,kde->otd", grad_pre, tiles_up)
    grad_late_norm, grad_shift_three, grad_scale_three = modulate_back(
        residual_late, blocks[6], blocks[7], grad_normed_three
    )
    grad_late = grad_final + grad_late_norm
    grad_gate_two = jnp.sum(grad_late * branch_two, axis=1)
    grad_branch_two = (blocks[5] * grad_late).astype(jnp.bfloat16)
    grad_merged_two = contract("ote,de->otd", grad_branch_two, tile_out_two).astype(jnp.bfloat16)
    grad_down = partial_sums("otkd,ote->kde", hidden, grad_branch_three)
    grad_up = partial_sums("otd,otke->kde", normed_three, grad_pre)
    grad_out_two = partial_sums("otd,ote->de", merged_two, grad_branch_two)
    sums_down, grad_cross_heads = reduced([grad_down], None, [("heads", [grad_merged_two[None]])], 5, 2)
    grad_query_heads, grad_pair_heads = [], []
    for place in range(objects):
        query_part, pair_part = attend_backward(
            view_tokens, *cross_sources[place], cross_result[place], cross_logsum[place], grad_cross_heads, VIEW, (place, 1)
        )
        grad_query_heads.append(query_part)
        grad_pair_heads.append(pair_part)
    pair_mixes = [("tokens", [part]) for part in grad_pair_heads]
    sums_up, grad_query_two, *grad_pairs = reduced(
        [grad_up], None, [("objects", grad_query_heads)] + pair_mixes[:half], 6
    )
    grad_query_two = grad_query_two[0]
    grad_tile_query = partial_sums("otd,ote->de", normed_two, grad_query_two)
    grad_normed_two = contract("ote,de->otd", grad_query_two, tile_query_two)
    grad_mid_norm, grad_shift_two, grad_scale_two = modulate_back(
        residual_mid, blocks[3], blocks[4], grad_normed_two
    )
    grad_mid = grad_late + grad_mid_norm
    grad_gate_one = jnp.sum(grad_mid * branch_one, axis=1)
    grad_branch_one = (blocks[2] * grad_mid).astype(jnp.bfloat16)
    grad_merged_one = contract("ote,de->otd", grad_branch_one, tile_out_one).astype(jnp.bfloat16)
    grad_out_one = partial_sums("otd,ote->de", merged_one, grad_branch_one)
    sums_mid, grad_self_heads, *more_pairs = reduced(
        [grad_out_two, grad_tile_query], None, [("heads", [grad_merged_one[None]])] + pair_mixes[half:], 7
    )
    grad_self_query, grad_self_pair = attend_backward(
        every_key, *self_sources, self_result, self_logsum, grad_self_heads, VIEW, (0, objects)
    )
    grad_pairs = jnp.concatenate(grad_pairs + more_pairs, axis=1)
    grad_tiles_pair = partial_sums("oid,koie->kde", image_tokens, grad_pairs)
    grad_image = contract("koie,kde->oid", grad_pairs, tiles_pair)
    sums_late, grad_triples = reduced(
        [grad_tiles_pair, grad_out_one], None, [("tokens", [grad_self_query, grad_self_pair])], 8
    )
    grad_qkv = partial_sums("otd,kote->kde", normed_one, grad_triples)
    grad_normed_one = contract("kote,kde->otd", grad_triples, tiles_qkv)
    grad_in_norm, grad_shift_one, grad_scale_one = modulate_back(
        residual_in, blocks[0], blocks[1], grad_normed_one
    )
    grad_triplane = grad_mid + grad_in_norm
    grad_mods = jnp.concatenate(
        [
            grad_shift_one[:, 0],
            grad_scale_one[:, 0],
            grad_gate_one,
            grad_shift_two[:, 0],
            grad_scale_two[:, 0],
            grad_gate_two,
            grad_shift_three[:, 0],
            grad_scale_three[:, 0],
            grad_gate_three,
        ],
        axis=-1,
    )
    grad_mod_rows = jnp.dot(
        camera.T, grad_mods, precision=HIGHEST, preferred_element_type=jnp.float32
    )
    grad_modulation = jnp.concatenate(
        [grad_mod_rows, jnp.sum(grad_mods, axis=0, keepdims=True)], axis=0
    )
    if fast:
        sums_qkv, mod_sum = reduce_tiles([grad_qkv], mod_sums(grad_modulation), [], 9, 2)
        sums = [sums_qkv, sums_late, sums_mid, sums_up, sums_down]
        order = (0, 1, 2, 5, 6, 3, 7, 4, 8, 9, 10, 11, 12, 13, 14, 15)
        tile_grad = to_owners(sums, order, tile_slots, 10).reshape(master.shape)
        mod_grad = mod_sum.reshape(-1)[: modulation.size].reshape(modulation.shape)
        tile_grad, mod_grad = tile_grad.astype(jnp.float32), mod_grad.astype(jnp.float32)
    else:
        logical = [grad_qkv[0], grad_qkv[1], grad_qkv[2], grad_out_one, grad_tile_query]
        logical = logical + [grad_tiles_pair[0], grad_tiles_pair[1], grad_out_two]
        logical = logical + [grad_up[tile] for tile in range(4)]
        logical = logical + [grad_down[tile] for tile in range(4)]
        tile_grad = sums_generic(logical, tile_slots).astype(jnp.float32)
        mod_grad = mod_generic(grad_modulation)
    new_master, new_moment1, new_moment2 = adamw(master, tile_grad, moment1, moment2, RATE_TILES)
    new_modulation, new_mod_moment1, new_mod_moment2 = adamw(
        modulation, mod_grad, mod_moment1, mod_moment2, RATE_MODULATION
    )
    return (
        block_output,
        grad_triplane,
        grad_image,
        new_master,
        new_moment1,
        new_moment2,
        new_master.astype(jnp.bfloat16),
        new_modulation,
        new_mod_moment1,
        new_mod_moment2,
    )


def solution(mesh):
    in_specs = (
        P("dp", "fsdp", None),
        P("dp", "fsdp", None),
        P("dp", None),
        P("dp"),
        P("dp", "fsdp", None),
        P("dp", "fsdp", None),
        P("dp", "fsdp", None),
        P(),
        P(None, ("dp", "fsdp")),
        P(None, ("dp", "fsdp")),
        P(None, ("dp", "fsdp")),
        P("dp", "fsdp", None),
    )
    out_specs = (
        P("dp", "fsdp", None),
        P("dp", "fsdp", None),
        P("dp", "fsdp", None),
        P("dp", "fsdp", None),
        P("dp", "fsdp", None),
        P("dp", "fsdp", None),
        P("dp", "fsdp", None),
        P(None, ("dp", "fsdp")),
        P(None, ("dp", "fsdp")),
        P(None, ("dp", "fsdp")),
    )
    return jax.shard_map(shards, mesh=mesh, in_specs=in_specs, out_specs=out_specs, check_vma=False)
```

```python
import functools

import jax
import jax.numpy as jnp
from jax import lax
from jax.experimental import pallas as pl
from jax.experimental.pallas import tpu as pltpu
from jax.sharding import PartitionSpec as P

HD = 64
STEP = 5
VIEW = 1024
LANES = 128


HIGHEST = lax.Precision.HIGHEST
NEGATIVE = -1e30
BETA_ONE = 0.5
BETA_TWO = 0.5
EPSILON = 1e-08
WEIGHT_DECAY = 0.01
RATE_TILES = 0.03
RATE_MODULATION = 0.15


def contract(form, left, right):
    return jnp.einsum(form, left, right, preferred_element_type=jnp.float32)


def layer_norm(values):
    center = values - jnp.mean(values, axis=-1, keepdims=True)
    spread = jnp.mean(center * center, axis=-1, keepdims=True)
    return center * lax.rsqrt(spread + 1e-06)


def modulate(values, shift, scale):
    return layer_norm(values) * (1.0 + scale) + shift


def modulate_back(values, shift, scale, grad_normed):
    unused, pull = jax.vjp(modulate, values, shift, scale)
    return pull(grad_normed)


def gelu_tanh(values):
    return jax.nn.gelu(values, approximate=True)


NT = (((1,), (1,)), ((), ()))
NN = (((1,), (0,)), ((), ()))
TN = (((0,), (0,)), ((), ()))


def dot(left, right, dims):
    return lax.dot_general(left, right, dims, preferred_element_type=jnp.float32)


def head_part(values, head, heads):
    if heads == 1:
        return values
    lanes = lax.broadcasted_iota(jnp.int32, values.shape, 1)
    return jnp.where(lanes // HD == head, values, jnp.zeros_like(values))


def rows_of(ref, start, amount):
    block = ref[pl.ds(start, amount), 0]
    return block.reshape(block.shape[0] * block.shape[1], block.shape[2])


def forward_body(step_rows, first_object, live_ref, q_ref, k_ref, v_ref, out_ref, lse_ref):
    key_groups, unused_one, key_rows, width = k_ref.shape
    heads = width // HD
    per_block = step_rows // key_rows
    blocks = live_ref[pl.program_id(0) + first_object] // step_rows
    queries = rows_of(q_ref, 0, q_ref.shape[0]) * jnp.bfloat16(0.125)
    result = jnp.zeros(queries.shape, jnp.float32)
    for head in range(heads):
        own = head_part(queries, head, heads)

        def step(position, carried, own=own):
            highest, total, acc = carried
            keys = rows_of(k_ref, position * per_block, per_block)
            values = rows_of(v_ref, position * per_block, per_block)
            scores = dot(own, keys, NT)
            new_highest = jnp.maximum(highest, jnp.max(scores, axis=1, keepdims=True))
            weights = jnp.exp(scores - new_highest)
            scale = jnp.exp(highest - new_highest)
            total = total * scale + jnp.sum(weights, axis=1, keepdims=True)
            acc = acc * scale + dot(weights.astype(jnp.bfloat16), values, NN)
            return (new_highest, total, acc)

        first = (
            jnp.full((own.shape[0], 1), -jnp.inf, jnp.float32),
            jnp.zeros((own.shape[0], 1), jnp.float32),
            jnp.zeros(own.shape, jnp.float32),
        )
        highest, total, acc = lax.fori_loop(0, blocks, step, first)
        result = result + head_part(acc / total, head, heads)
        level = jnp.broadcast_to(highest + jnp.log(total), (own.shape[0], 128))
        lse_ref[0, head] = jnp.transpose(level)[0:1]
    out_ref[...] = result.astype(jnp.bfloat16).reshape(out_ref.shape)


def attend_forward(live, query_source, key_source, value_source, query_block, step_rows, span):
    (q_array, *q_at), (k_array, *k_at), (v_array, *v_at) = query_source, key_source, value_source
    groups, unused_blocks, unused_objects, q_rows, width = q_array.shape
    first_object, objects = span
    k_rows = k_array.shape[3]
    heads = width // HD
    total_q = groups * q_rows
    per_q = query_block // q_rows
    grid = (objects, total_q // query_block)
    whole = lambda at: (lambda o, j, live: (0, at[0], o + at[1], 0, 0))
    part = lambda at: (lambda o, j, live: (j, at[0], o + at[1], 0, 0))
    return pl.pallas_call(
        functools.partial(forward_body, step_rows, first_object),
        grid_spec=pltpu.PrefetchScalarGridSpec(
            num_scalar_prefetch=1,
            grid=grid,
            in_specs=[
                pl.BlockSpec((per_q, None, 1, q_rows, width), part(q_at)),
                pl.BlockSpec((groups, None, 1, k_rows, width), whole(k_at)),
                pl.BlockSpec((groups, None, 1, k_rows, width), whole(v_at)),
            ],
            out_specs=[
                pl.BlockSpec((per_q, 1, q_rows, width), lambda o, j, live: (j, o, 0, 0)),
                pl.BlockSpec((1, heads, 1, query_block), lambda o, j, live: (o, 0, 0, j)),
            ],
        ),
        out_shape=[
            jax.ShapeDtypeStruct((groups, objects, q_rows, width), jnp.bfloat16),
            jax.ShapeDtypeStruct((objects, heads, 1, total_q), jnp.float32),
        ],
        cost_estimate=pl.CostEstimate(
            flops=4 * objects * total_q * groups * k_rows * width,
            bytes_accessed=4 * objects * groups * (q_rows + k_rows) * width,
            transcendentals=objects * heads * total_q * groups * k_rows,
        ),
    )(live, q_array, k_array, v_array)


def backward_prepare(q_ref, out_ref, grad_ref, qs, gs, delta):
    heads = qs.shape[0]
    queries = rows_of(q_ref, 0, q_ref.shape[0]) * jnp.bfloat16(0.125)
    grads = rows_of(grad_ref, 0, grad_ref.shape[0])
    outs = rows_of(out_ref, 0, out_ref.shape[0])
    product = jnp.transpose(grads.astype(jnp.float32) * outs.astype(jnp.float32))
    for head in range(heads):
        qs[head] = head_part(queries, head, heads)
        gs[head] = head_part(grads, head, heads)
        delta[head] = jnp.sum(product[head * HD : (head + 1) * HD], axis=0, keepdims=True)


def backward_block(keys, values, lse_ref, qs, gs, delta):
    heads = qs.shape[0]
    grad_q, grad_k, grad_v = None, None, None
    for head in range(heads):
        own, grads = qs[head], gs[head]
        weights = jnp.exp(dot(keys, own, NT) - lse_ref[0, head])
        grad_weights = dot(values, grads, NT)
        grad_scores = (weights * (grad_weights - delta[head])).astype(jnp.bfloat16)
        new_v = dot(weights.astype(jnp.bfloat16), grads, NN)
        new_k = dot(grad_scores, own, NN)
        new_q = dot(grad_scores, head_part(keys, head, heads), TN)
        grad_q = new_q if grad_q is None else grad_q + new_q
        grad_k = new_k if grad_k is None else grad_k + new_k
        grad_v = new_v if grad_v is None else grad_v + new_v
    return grad_q, grad_k, grad_v


def cross_backward_body(
    first_object, live_ref, q_ref, k_ref, v_ref, out_ref, lse_ref, grad_ref, dq_ref, dkv_ref, qs, gs, delta, dq_acc
):
    position = pl.program_id(1)
    width = q_ref.shape[3]
    rows = k_ref.shape[0] * k_ref.shape[2]

    @pl.when(position == 0)
    def _():
        backward_prepare(q_ref, out_ref, grad_ref, qs, gs, delta)
        dq_acc[...] = jnp.zeros_like(dq_acc)

    alive = position * rows < live_ref[pl.program_id(0) + first_object]

    @pl.when(alive)
    def _():
        keys = rows_of(k_ref, 0, k_ref.shape[0])
        values = rows_of(v_ref, 0, v_ref.shape[0])
        grad_q, grad_k, grad_v = backward_block(keys, values, lse_ref, qs, gs, delta)
        dq_acc[...] += grad_q
        shape = (k_ref.shape[0], 1, k_ref.shape[2], width)
        dkv_ref[:, 0] = grad_k.astype(jnp.bfloat16).reshape(shape)
        dkv_ref[:, 1] = grad_v.astype(jnp.bfloat16).reshape(shape)

    @pl.when(jnp.logical_not(alive))
    def _():
        dkv_ref[...] = jnp.zeros_like(dkv_ref)

    @pl.when(position == pl.num_programs(1) - 1)
    def _():
        dq_ref[...] = (dq_acc[...] * 0.125).astype(jnp.bfloat16).reshape(dq_ref.shape)


def attend_backward(live, query_source, key_source, value_source, outs, lse, grads, step_rows, span):
    (q_array, *q_at), (k_array, *k_at), (v_array, *v_at) = query_source, key_source, value_source
    groups, unused_blocks, unused_objects, q_rows, width = q_array.shape
    first_object, objects = span
    k_rows = k_array.shape[3]
    heads = width // HD
    total_q = groups * q_rows
    per_k = max(step_rows // k_rows, 1)
    grid = (objects, groups // per_k)
    whole = lambda at: (lambda o, j, live: (0, at[0], o + at[1], 0, 0))
    part = lambda at: (lambda o, j, live: (j, at[0], o + at[1], 0, 0))
    tokens = pl.BlockSpec((groups, 1, q_rows, width), lambda o, j, live: (0, o, 0, 0))
    return pl.pallas_call(
        functools.partial(cross_backward_body, first_object),
        grid_spec=pltpu.PrefetchScalarGridSpec(
            num_scalar_prefetch=1,
            grid=grid,
            in_specs=[
                pl.BlockSpec((groups, None, 1, q_rows, width), whole(q_at)),
                pl.BlockSpec((per_k, None, 1, k_rows, width), part(k_at)),
                pl.BlockSpec((per_k, None, 1, k_rows, width), part(v_at)),
                tokens,
                pl.BlockSpec((1, heads, 1, total_q), lambda o, j, live: (o, 0, 0, 0)),
                pl.BlockSpec((groups, None, 1, q_rows, width), whole((0, first_object))),
            ],
            out_specs=[
                pl.BlockSpec((groups, 1, q_rows, width), lambda o, j, live: (0, o, 0, 0)),
                pl.BlockSpec((per_k, 2, 1, k_rows, width), lambda o, j, live: (j, 0, o, 0, 0)),
            ],
            scratch_shapes=[
                pltpu.VMEM((heads, total_q, width), jnp.bfloat16),
                pltpu.VMEM((heads, total_q, width), jnp.bfloat16),
                pltpu.VMEM((heads, 1, total_q), jnp.float32),
                pltpu.VMEM((total_q, width), jnp.float32),
            ],
        ),
        out_shape=[
            jax.ShapeDtypeStruct((groups, objects, q_rows, width), jnp.bfloat16),
            jax.ShapeDtypeStruct((groups, 2, objects, k_rows, width), jnp.bfloat16),
        ],
        cost_estimate=pl.CostEstimate(
            flops=10 * objects * total_q * groups * k_rows * width,
            bytes_accessed=8 * objects * groups * (q_rows + k_rows) * width,
            transcendentals=objects * heads * total_q * groups * k_rows,
        ),
    )(live, q_array, k_array, v_array, outs, lse, grads)

CHUNKS = ((5, 6), (0, 1, 2), (3, 4, 7), (8, 9, 10, 11), (12, 13, 14, 15))
EARLY = 8
GATHER_PARTS = 1
MOD_ROWS = 16
MESH = pl.DeviceIdType.MESH


def places():
    dp_index, fsdp_index = lax.axis_index("dp"), lax.axis_index("fsdp")
    return dp_index, fsdp_index, fsdp_index // 2, fsdp_index % 2


def z_peer(fsdp_index, shift):
    return {"fsdp": (fsdp_index + 2 * shift) % 8}


def core_peer(fsdp_index):
    return {"fsdp": fsdp_index + 1 - 2 * (fsdp_index % 2)}


def dp_peer(dp_index, flip):
    return {"dp": dp_index ^ flip}


def greet(peers):
    barrier = pltpu.get_barrier_semaphore()
    for peer in peers:
        pl.semaphore_signal(barrier, inc=1, device_id=peer, device_id_type=MESH)
    pl.semaphore_wait(barrier, len(peers))


def remote(source, target, send_sem, recv_sem, peer):
    copy = pltpu.make_async_remote_copy(
        source, target, send_sem, recv_sem, device_id=peer, device_id_type=MESH
    )
    copy.start()
    return copy


def columns(index):
    return pl.ds(pl.multiple_of(index * LANES, LANES), LANES)


def fsdp_peers(fsdp_index):
    return [{"fsdp": (fsdp_index + shift) % 8} for shift in range(1, 8)]


def mix_begin(kind, sources, target, scratch, fsdp_index):
    sems, holds = scratch[0], scratch[1:]

    def ends(place, peer):
        if kind == "heads":
            return sources[0].at[:, :, :, columns(peer)], target.at[fsdp_index]
        mine = columns(fsdp_index)
        if kind == "objects":
            return sources[place].at[peer], target.at[0, place : place + 1, :, mine]
        if len(sources[place].shape) == 4:
            return sources[place].at[peer], target.at[place, :, :, mine]
        return sources[place].at[peer], target.at[place : place + 2, :, :, mine]

    copies, stays = [], []
    for shift in (4, 5, 3, 6, 2, 7, 1):
        peer = (fsdp_index + shift) % 8
        for place in range(len(sources)):
            theirs, there = ends(place, peer)
            copies.append(
                remote(theirs, there, sems.at[0, place, shift], sems.at[1, place, shift], {"fsdp": peer})
            )
    for place in range(len(sources)):
        ours, here = ends(place, fsdp_index)
        load = pltpu.make_async_copy(ours, holds[place], sems.at[0, place, 0])
        load.start()
        stays.append((load, pltpu.make_async_copy(holds[place], here, sems.at[1, place, 0])))
    return copies, stays


def mix_own(moving):
    for load, store in moving[1]:
        load.wait()
        store.start()


def mix_end(moving):
    for load, store in moving[1]:
        store.wait()
    for copy in moving[0]:
        copy.wait()


def mix_plan(mix):
    kind, sources = mix
    bf = jnp.bfloat16
    holds, blocks = [], 0
    for array in sources:
        if kind == "heads":
            holds.append(array.shape[:3] + (array.shape[3] // 8,))
            result = (8,) + holds[0]
        else:
            holds.append(array.shape[1:])
            blocks += 1 if len(array.shape) == 4 else array.shape[1]
            if kind == "objects":
                result = (1, len(sources), array.shape[2], 8 * array.shape[3])
                continue
            result = (blocks,) + array.shape[-3:-1] + (8 * array.shape[-1],)
    scratch = [pltpu.SemaphoreType.DMA((2, len(sources), 8))] + [pltpu.VMEM(hold, bf) for hold in holds]
    return scratch, jax.ShapeDtypeStruct(result, bf)


def mix_body(kind, amount, *refs):
    sources, target, scratch = refs[:amount], refs[amount], refs[amount + 1 :]
    fsdp_index = lax.axis_index("fsdp")
    greet(fsdp_peers(fsdp_index))
    moving = mix_begin(kind, sources, target, scratch, fsdp_index)
    mix_own(moving)
    mix_end(moving)


def mix_alone(mix, collective):
    kind, sources = mix
    scratch, result = mix_plan(mix)
    return pl.pallas_call(
        functools.partial(mix_body, kind, len(sources)),
        in_specs=[ANY] * len(sources),
        out_specs=ANY,
        scratch_shapes=scratch,
        out_shape=result,
        compiler_params=comm_params(collective),
        cost_estimate=pl.CostEstimate(flops=0, bytes_accessed=30_000_000, transcendentals=0),
    )(*sources)


def part_of(ref, unit, dims):
    tile, part = unit // GATHER_PARTS, unit % GATHER_PARTS
    rows = ref.shape[-2] // GATHER_PARTS
    return ref.at[(tile,) + (slice(None),) * dims + (pl.ds(part * rows, rows),)]


def send_z(unit, full, fsdp_index, dp_index, z_index, sems):
    own = full.at[z_index, dp_index]
    return [
        remote(own, own, sems[0].at[unit, shift - 1], sems[1].at[unit, shift - 1], z_peer(fsdp_index, shift))
        for shift in (1, 2, 3)
    ]


def spread(units, fulls, outs, z_copies, z_local, sems, where):
    send_sems, recv_sems, out_sems = sems
    dp_index, fsdp_index, z_index, core = where
    near_x, near_y = dp_peer(dp_index, 1), dp_peer(dp_index, 2)
    first, second, last = {}, {}, []
    for step in range(units + 2):
        if step < units:
            unit, full = step, fulls[step]
            for copy in z_copies[unit]:
                copy.wait() if z_local else copy.wait_recv()
            low, high = full.at[0:2, dp_index], full.at[2:4, dp_index]
            pairs = [(low, near_x), (high, near_y), (low, near_y), (high, near_x)]
            first[unit] = [
                remote(ref, ref, send_sems.at[unit, 3 + n], recv_sems.at[unit, 3 + n], peer)
                for n, (ref, peer) in enumerate(pairs)
            ]
        if 0 <= step - 1 < units:
            unit, full = step - 1, fulls[step - 1]
            first[unit][0].wait_recv()
            first[unit][1].wait_recv()
            low, high = full.at[0:2, dp_index ^ 1], full.at[2:4, dp_index ^ 2]
            pairs = [(low, near_y), (high, near_x)]
            second[unit] = [
                remote(ref, ref, send_sems.at[unit, 7 + n], recv_sems.at[unit, 7 + n], peer)
                for n, (ref, peer) in enumerate(pairs)
            ]
        if 0 <= step - 2 < units:
            unit, full, out = step - 2, fulls[step - 2], outs[step - 2]
            for copy in first[unit][2:] + second[unit]:
                copy.wait_recv()
            target = out.at[:, core]
            last.append(
                remote(full, target, send_sems.at[unit, 9], recv_sems.at[unit, 9], core_peer(fsdp_index))
            )
            here = pltpu.make_async_copy(full, target, out_sems.at[unit])
            here.start()
            last.append(here)
    for unit in range(units):
        for copy in first[unit] + second[unit]:
            copy.wait_send()
    for copy in last:
        copy.wait()


def first_gather_body(tiles, rows, index_ref, narrow_ref, mod_ref, out_ref, mod_out_ref, wait_ref, rest_ref, stacked, mine, full, mod_full, zoned, swap_sems, load_sems, send_sems, recv_sems, out_sems, zone_sems):
    where = places()
    dp_index, fsdp_index, z_index, core = where
    peers = [z_peer(fsdp_index, shift) for shift in (1, 2, 3)]
    peers += [dp_peer(dp_index, flip) for flip in (1, 2, 3)] + [core_peer(fsdp_index)]
    greet(peers)
    swaps = [
        remote(narrow_ref.at[:, dp_index ^ flip], stacked.at[pl.ds(4 * flip, 4)], swap_sems.at[0, flip], swap_sems.at[1, flip], dp_peer(dp_index, flip))
        for flip in (1, 2, 3)
    ]
    own = pltpu.make_async_copy(narrow_ref.at[:, dp_index], stacked.at[pl.ds(0, 4)], load_sems.at[0])
    own.start()
    mod_load = pltpu.make_async_copy(mod_ref, mod_full.at[z_index, dp_index], load_sems.at[1])
    mod_load.start()
    mod_load.wait()
    units = tiles * GATHER_PARTS
    z_copies = {units: send_z(units, mod_full, fsdp_index, dp_index, z_index, (send_sems, recv_sems))}
    own.wait()
    for swap in swaps:
        swap.wait()
    for tile in range(tiles):
        full[tile, z_index, dp_index] = stacked[index_ref[tile]]
        for unit in range(tile * GATHER_PARTS, (tile + 1) * GATHER_PARTS):
            z_copies[unit] = send_z(unit, part_of(full, unit, 2), fsdp_index, dp_index, z_index, (send_sems, recv_sems))

    def take(position, carried):
        mine[position] = stacked[index_ref[position + tiles]]
        return carried

    lax.fori_loop(0, 16 - tiles, take, 0)
    early = EARLY - tiles
    zone = [
        remote(mine.at[pl.ds(0, early)], zoned.at[z_index], zone_sems.at[0, shift - 1], zone_sems.at[1, shift - 1], z_peer(fsdp_index, shift))
        for shift in (1, 2, 3)
    ]
    zone_own = pltpu.make_async_copy(mine.at[pl.ds(0, early)], wait_ref.at[z_index], load_sems.at[2])
    zone_own.start()
    rest = pltpu.make_async_copy(mine.at[pl.ds(early, 16 - EARLY)], rest_ref, load_sems.at[3])
    rest.start()
    fulls = [part_of(full, unit, 2) for unit in range(units)] + [mod_full]
    outs = [part_of(out_ref, unit, 3) for unit in range(units)] + [mod_out_ref]
    spread(units + 1, fulls, outs, z_copies, False, (send_sems, recv_sems, out_sems), where)
    for unit in range(units + 1):
        for copy in z_copies[unit]:
            copy.wait_send()
    for copy in zone:
        copy.wait()
    zone_own.wait()
    rest.wait()
    stores = []
    for shift in (1, 2, 3):
        z_from = (z_index + shift) % 4
        store = pltpu.make_async_copy(zoned.at[z_from], wait_ref.at[z_from], load_sems.at[3 + shift])
        store.start()
        stores.append(store)
    for store in stores:
        store.wait()


ANY = pl.BlockSpec(memory_space=pl.ANY)


def comm_params(collective):
    return pltpu.CompilerParams(
        collective_id=collective, has_side_effects=True, vmem_limit_bytes=58 * 1024 * 1024
    )


def reorder(values, order):
    runs = []
    for spot in order:
        if runs and runs[-1][1] == spot:
            runs[-1][1] = spot + 1
        else:
            runs.append([spot, spot + 1])
    return jnp.concatenate([values[start:end] for start, end in runs])


def first_gather(narrow, mod_rows, index):
    tiles = len(CHUNKS[0])
    slots, owners, rows, width = narrow.shape
    bf = jnp.bfloat16
    return pl.pallas_call(
        functools.partial(first_gather_body, tiles, rows),
        grid_spec=pltpu.PrefetchScalarGridSpec(
            num_scalar_prefetch=1,
            grid=(),
            in_specs=[ANY, ANY],
            out_specs=[ANY] * 4,
            scratch_shapes=[
                pltpu.VMEM((16, rows, width), bf),
                pltpu.VMEM((16 - tiles, rows, width), bf),
                pltpu.VMEM((tiles, 4, 4, rows, width), bf),
                pltpu.VMEM((4, 4, MOD_ROWS, width), bf),
                pltpu.VMEM((4, EARLY - tiles, rows, width), bf),
                pltpu.SemaphoreType.DMA((2, 4)),
                pltpu.SemaphoreType.DMA((8,)),
                pltpu.SemaphoreType.DMA((tiles * GATHER_PARTS + 1, 10)),
                pltpu.SemaphoreType.DMA((tiles * GATHER_PARTS + 1, 10)),
                pltpu.SemaphoreType.DMA((tiles * GATHER_PARTS + 1,)),
                pltpu.SemaphoreType.DMA((2, 3)),
            ],
        ),
        out_shape=[
            jax.ShapeDtypeStruct((tiles, 4, 2, 4, rows, width), bf),
            jax.ShapeDtypeStruct((4, 2, 4, MOD_ROWS, width), bf),
            jax.ShapeDtypeStruct((4, EARLY - tiles, rows, width), bf),
            jax.ShapeDtypeStruct((16 - EARLY, rows, width), bf),
        ],
        compiler_params=comm_params(0),
        cost_estimate=pl.CostEstimate(flops=0, bytes_accessed=200_000_000, transcendentals=0),
    )(index, narrow, mod_rows)


def next_gather_body(tiles, start, zoned, plans, ahead, source_ref, *refs):
    mix_sources = []
    for unused_kind, amount in plans:
        mix_sources.append(refs[:amount])
        refs = refs[amount:]
    out_ref, refs = refs[0], refs[1:]
    mixed_refs, refs = refs[: len(plans)], refs[len(plans) :]
    if ahead:
        zone_ref, refs = refs[0], refs[1:]
        zone_hold, zone_sems, refs = refs[0], refs[1], refs[2:]
    (full, load_sems, send_sems, recv_sems, out_sems), refs = refs[:5], refs[5:]
    where = places()
    dp_index, fsdp_index, z_index, core = where
    loads = []
    for tile in range(tiles):
        if zoned:
            load = pltpu.make_async_copy(source_ref.at[:, start + tile], full.at[tile, :, dp_index], load_sems.at[tile])
        else:
            load = pltpu.make_async_copy(source_ref.at[start + tile], full.at[tile, z_index, dp_index], load_sems.at[tile])
        load.start()
        loads.append(load)
    units = tiles * GATHER_PARTS
    peers = [dp_peer(dp_index, flip) for flip in (1, 2)]
    if plans:
        peers += fsdp_peers(fsdp_index)
    else:
        peers += [core_peer(fsdp_index)]
        peers += [] if zoned else [z_peer(fsdp_index, shift) for shift in (1, 2, 3)]
    greet(peers)
    z_copies = {}
    for tile in range(tiles):
        near = range(tile * GATHER_PARTS, (tile + 1) * GATHER_PARTS)
        if zoned:
            for unit in near:
                z_copies[unit] = [loads[tile]] if unit == near[0] else []
        else:
            loads[tile].wait()
            for unit in near:
                z_copies[unit] = send_z(unit, part_of(full, unit, 2), fsdp_index, dp_index, z_index, (send_sems, recv_sems))
    movings = []
    for place, (kind, amount) in enumerate(plans):
        mix_scratch, refs = refs[: 1 + amount], refs[1 + amount :]
        movings.append(mix_begin(kind, mix_sources[place], mixed_refs[place], mix_scratch, fsdp_index))
    for moving in movings:
        mix_own(moving)
    if ahead:
        later = source_ref.at[pl.ds(ahead[0], ahead[1])]
        zone = [
            remote(later, zone_ref.at[z_index], zone_sems.at[0, shift], zone_sems.at[1, shift], z_peer(fsdp_index, shift))
            for shift in (1, 2, 3)
        ]
        zone_load = pltpu.make_async_copy(later, zone_hold, zone_sems.at[0, 0])
        zone_load.start()
        zone_load.wait()
        zone_store = pltpu.make_async_copy(zone_hold, zone_ref.at[z_index], zone_sems.at[1, 0])
        zone_store.start()
    fulls = [part_of(full, unit, 2) for unit in range(units)]
    outs = [part_of(out_ref, unit, 3) for unit in range(units)]
    spread(units, fulls, outs, z_copies, zoned, (send_sems, recv_sems, out_sems), where)
    if not zoned:
        for unit in range(units):
            for copy in z_copies[unit]:
                copy.wait_send()
    for moving in movings:
        mix_end(moving)
    if ahead:
        for copy in zone:
            copy.wait()
        zone_store.wait()


def next_gather(source, tiles, start, zoned, mixes, ahead, collective):
    rows, width = source.shape[-2:]
    bf = jnp.bfloat16
    operands = [source]
    out_shape = [jax.ShapeDtypeStruct((tiles, 4, 2, 4, rows, width), bf)]
    scratch = [
        pltpu.VMEM((tiles, 4, 4, rows, width), bf),
        pltpu.SemaphoreType.DMA((tiles,)),
        pltpu.SemaphoreType.DMA((tiles * GATHER_PARTS, 10)),
        pltpu.SemaphoreType.DMA((tiles * GATHER_PARTS, 10)),
        pltpu.SemaphoreType.DMA((tiles * GATHER_PARTS,)),
    ]
    for mix in mixes:
        operands += list(mix[1])
        extra, result = mix_plan(mix)
        scratch, out_shape = scratch + extra, out_shape + [result]
    plans = tuple((kind, len(sources)) for kind, sources in mixes)
    if ahead:
        scratch = [pltpu.VMEM((ahead[1], rows, width), bf), pltpu.SemaphoreType.DMA((2, 4))] + scratch
        out_shape = out_shape + [jax.ShapeDtypeStruct((4, ahead[1], rows, width), bf)]
    results = pl.pallas_call(
        functools.partial(next_gather_body, tiles, start, zoned, plans, ahead),
        in_specs=[ANY] * len(operands),
        out_specs=[ANY] * len(out_shape),
        scratch_shapes=scratch,
        out_shape=out_shape,
        compiler_params=comm_params(collective),
        cost_estimate=pl.CostEstimate(flops=0, bytes_accessed=tiles * 30_000_000, transcendentals=0),
    )(*operands)
    return [results[0].reshape(tiles, 32 * rows, width)] + list(results[1:])


def fast_layout(master):
    owners, groups = lax.axis_size("dp"), lax.axis_size("fsdp")
    return owners == 4 and groups == 8 and master.shape[1:] == (128, 1024)


def fetch_generic(master, modulation, tile_slots):
    narrow = master.astype(jnp.bfloat16)
    mod_narrow = modulation.astype(jnp.bfloat16)[:, None, None, :]
    row_blocks = lax.all_gather(narrow, "fsdp", axis=1, tiled=True)
    mod_blocks = lax.all_gather(mod_narrow, "fsdp", axis=2, tiled=True)
    gathered = lax.all_gather(row_blocks, "dp", axis=0, tiled=True)
    mod_all = lax.all_gather(mod_blocks, "dp", axis=1, tiled=True)
    chunks = [
        jnp.stack(
            [lax.dynamic_index_in_dim(gathered, tile_slots[tile], 0, keepdims=False) for tile in chunk]
        )
        for chunk in CHUNKS
    ]
    return chunks, mod_all.reshape(mod_all.shape[0], -1)


def sums_generic(logical, tile_slots):
    slot_grads = jnp.zeros((len(logical),) + logical[0].shape, jnp.bfloat16)
    for position, grad in enumerate(logical):
        slot_grads = lax.dynamic_update_index_in_dim(
            slot_grads, grad.astype(jnp.bfloat16), tile_slots[position], 0
        )
    row_sums = lax.psum_scatter(slot_grads, "fsdp", scatter_dimension=1, tiled=True)
    return lax.psum_scatter(row_sums, "dp", scatter_dimension=0, tiled=True)


def mod_generic(grad_modulation):
    owners, groups = lax.axis_size("dp"), lax.axis_size("fsdp")
    rows, width = grad_modulation.shape
    blocks = grad_modulation.reshape(rows, owners, groups, width // (owners * groups))
    sums = lax.psum_scatter(blocks.astype(jnp.bfloat16), "fsdp", scatter_dimension=2, tiled=True)
    sums = lax.psum_scatter(sums, "dp", scatter_dimension=1, tiled=True)
    return sums.reshape(rows, -1).astype(jnp.float32)


def wide(value):
    return value.astype(jnp.float32)


def reduce_scratch(tiles, rows, width):
    bf, f32 = jnp.bfloat16, jnp.float32
    return [
        pltpu.VMEM((2, tiles, 4, 4, rows, width), bf),
        pltpu.VMEM((4, tiles, 2, 2, rows, width), bf),
        pltpu.VMEM((2, tiles, 2, 2, rows, width), f32),
        pltpu.VMEM((4, tiles, 2, rows, width), bf),
        pltpu.VMEM((tiles, 4, rows, width), f32),
        pltpu.VMEM((2, 3, tiles, rows, width), bf),
        pltpu.VMEM((tiles, rows, width), bf),
        pltpu.SemaphoreType.DMA((2, tiles)),
        pltpu.SemaphoreType.DMA((8, tiles)),
        pltpu.SemaphoreType.DMA((8, tiles)),
    ]


def reduce_stages(tiles, scratch, out_ref, where):
    core_buf, swap, kept, swap_two, whole, zbuf, out_buf, load_sems, send_sems, recv_sems = scratch
    dp_index, fsdp_index, z_index, core = where
    x_bit, y_bit = dp_index % 2, dp_index // 2
    near_x, near_y = dp_peer(dp_index, 1), dp_peer(dp_index, 2)

    def moved(stage, tile):
        if stage == 1:
            ends = (swap.at[0, tile], swap.at[1, tile], near_x)
        elif stage == 2:
            ends = (swap.at[2, tile], swap.at[3, tile], near_y)
        elif stage == 3:
            ends = (swap_two.at[0, tile], swap_two.at[1, tile], near_y)
        elif stage == 4:
            ends = (swap_two.at[2, tile], swap_two.at[3, tile], near_x)
        else:
            shift = stage - 4
            ends = (zbuf.at[0, shift - 1, tile], zbuf.at[1, shift - 1, tile], z_peer(fsdp_index, shift))
        return pltpu.make_async_remote_copy(
            ends[0], ends[1], send_sems.at[stage, tile], recv_sems.at[stage, tile], device_id=ends[2], device_id_type=MESH
        )

    def both(tile, z_place, quarter):
        return wide(core_buf[0, tile, z_place, quarter]) + wide(core_buf[1, tile, z_place, quarter])

    def add_core(tile):
        for side in range(2):
            for other in range(2):
                kept[0, tile, side, other] = both(tile, side, 2 * other + x_bit)
                swap[0, tile, side, other] = both(tile, side, 2 * other + 1 - x_bit).astype(jnp.bfloat16)
                kept[1, tile, side, other] = both(tile, 2 + side, 2 * y_bit + other)
                swap[2, tile, side, other] = both(tile, 2 + side, 2 * (1 - y_bit) + other).astype(jnp.bfloat16)
        moved(1, tile).start()
        moved(2, tile).start()

    def add_first(tile):
        moved(1, tile).wait_recv()
        moved(2, tile).wait_recv()
        for side in range(2):
            whole[tile, side] = kept[0, tile, side, y_bit] + wide(swap[1, tile, side, y_bit])
            away = kept[0, tile, side, 1 - y_bit] + wide(swap[1, tile, side, 1 - y_bit])
            swap_two[0, tile, side] = away.astype(jnp.bfloat16)
            whole[tile, 2 + side] = kept[1, tile, side, x_bit] + wide(swap[3, tile, side, x_bit])
            away = kept[1, tile, side, 1 - x_bit] + wide(swap[3, tile, side, 1 - x_bit])
            swap_two[2, tile, side] = away.astype(jnp.bfloat16)
        moved(3, tile).start()
        moved(4, tile).start()

    def add_second(tile):
        moved(3, tile).wait_recv()
        moved(4, tile).wait_recv()
        for side in range(2):
            whole[tile, side] = whole[tile, side] + wide(swap_two[1, tile, side])
            whole[tile, 2 + side] = whole[tile, 2 + side] + wide(swap_two[3, tile, side])
        for shift in (1, 2, 3):
            zbuf[0, shift - 1, tile] = whole[tile, (z_index + shift) % 4].astype(jnp.bfloat16)
            moved(4 + shift, tile).start()

    def add_z(tile):
        total = whole[tile, z_index]
        for shift in (1, 2, 3):
            moved(4 + shift, tile).wait_recv()
            total = total + wide(zbuf[1, shift - 1, tile])
        out_buf[tile] = total.astype(jnp.bfloat16)

    def finish(tile):
        for stage in range(1, 8):
            moved(stage, tile).wait_send()

    return add_core, add_first, add_second, add_z, finish


def core_copies(entries, scratch, where):
    core_buf, load_sems, send_sems, recv_sems = scratch[0], scratch[-3], scratch[-2], scratch[-1]
    copies = []
    for tile, (theirs, ours) in enumerate(entries):
        away = remote(theirs, core_buf.at[1, tile], send_sems.at[0, tile], recv_sems.at[0, tile], core_peer(where[1]))
        load = pltpu.make_async_copy(ours, core_buf.at[0, tile], load_sems.at[0, tile])
        load.start()
        copies.append((away, load))
    return copies


def reduce_body(counts, extra, plans, parts, *refs):
    groups = len(counts)
    tiles = sum(counts) * parts
    grads, refs = refs[:groups], refs[groups:]
    if extra:
        mod_grads, refs = refs[0], refs[1:]
    mix_sources = []
    for unused_kind, amount in plans:
        mix_sources.append(refs[:amount])
        refs = refs[amount:]
    out_ref, refs = refs[0], refs[1:]
    if extra:
        mod_out_ref, refs = refs[0], refs[1:]
    mixed_refs, refs = refs[: len(plans)], refs[len(plans) :]
    scratch, refs = refs[:10], refs[10:]
    if extra:
        mod_scratch, refs = refs[:10], refs[10:]
    where = places()
    dp_index, fsdp_index, core = where[0], where[1], where[3]
    peers = [dp_peer(dp_index, flip) for flip in (1, 2)]
    if plans:
        peers += fsdp_peers(fsdp_index)
    else:
        peers += [z_peer(fsdp_index, shift) for shift in (1, 2, 3)] + [core_peer(fsdp_index)]
    greet(peers)
    movings = []
    for place, (kind, amount) in enumerate(plans):
        mix_scratch, refs = refs[: 1 + amount], refs[1 + amount :]
        movings.append(mix_begin(kind, mix_sources[place], mixed_refs[place], mix_scratch, fsdp_index))
    rows = out_ref.shape[1]
    entries = [
        tuple(grads[group].at[tile, :, side, :, pl.ds(part * rows, rows)] for side in (1 - core, core))
        for group in range(groups)
        for tile in range(counts[group])
        for part in range(parts)
    ]
    mod_entry = [(mod_grads.at[0, :, 1 - core], mod_grads.at[0, :, core])] if extra else []
    mod_copies = core_copies(mod_entry, mod_scratch, where) if extra else []
    copies = core_copies(entries, scratch, where)
    for moving in movings:
        mix_own(moving)
    stages = reduce_stages(tiles, scratch, out_ref, where)
    if extra:
        mod_stages = reduce_stages(1, mod_scratch, mod_out_ref, where)
        mod_copies[0][0].wait()
        mod_copies[0][1].wait()
        mod_stages[0](0)

    def arrive(tile):
        pltpu.make_async_copy(scratch[0].at[0, tile], scratch[0].at[0, tile], scratch[-3].at[0, tile]).wait()
        pltpu.make_async_remote_copy(
            scratch[0].at[1, tile], scratch[0].at[1, tile], scratch[-2].at[0, tile], scratch[-1].at[0, tile],
            device_id=core_peer(fsdp_index), device_id_type=MESH,
        ).wait_recv()

    def step(position, carried):
        @pl.when(position < tiles)
        def _():
            arrive(position)
            stages[0](position)

        for place in (1, 2, 3):
            tile = position - place

            @pl.when((tile >= 0) & (tile < tiles))
            def _():
                stages[place](tile)

        return carried

    if extra:
        step(0, 0)
        mod_stages[1](0)
        step(1, 0)
        mod_stages[2](0)
        step(2, 0)
        mod_stages[3](0)
        lax.fori_loop(3, tiles + 3, step, 0)
        mod_stages[4](0)
    else:
        lax.fori_loop(0, tiles + 3, step, 0)

    store = pltpu.make_async_copy(scratch[6], out_ref, scratch[-3].at[1, 0])
    store.start()

    def close(tile, carried):
        stages[4](tile)
        return carried

    lax.fori_loop(0, tiles, close, 0)
    for away, load in copies:
        away.wait_send()
    if extra:
        mod_store = pltpu.make_async_copy(mod_scratch[6], mod_out_ref, mod_scratch[-3].at[1, 0])
        mod_store.start()
        mod_store.wait()
    store.wait()
    for moving in movings:
        mix_end(moving)


def reduce_tiles(grads, mods, mixes, collective, parts=1):
    counts = tuple(part.shape[0] for part in grads)
    tiles = sum(counts) * parts
    rows, width = grads[0].shape[-2:]
    rows = rows // parts
    bf = jnp.bfloat16
    operands = list(grads)
    out_shape = [jax.ShapeDtypeStruct((tiles, rows, width), bf)]
    scratch = reduce_scratch(tiles, rows, width)
    if mods is not None:
        operands.append(mods)
        out_shape.append(jax.ShapeDtypeStruct((1, MOD_ROWS, width), bf))
        scratch = scratch + reduce_scratch(1, MOD_ROWS, width)
    for mix in mixes:
        operands += list(mix[1])
        extra, result = mix_plan(mix)
        scratch, out_shape = scratch + extra, out_shape + [result]
    plans = tuple((kind, len(sources)) for kind, sources in mixes)
    results = pl.pallas_call(
        functools.partial(reduce_body, counts, mods is not None, plans, parts),
        in_specs=[ANY] * len(operands),
        out_specs=[ANY] * len(out_shape),
        scratch_shapes=scratch,
        out_shape=out_shape,
        compiler_params=comm_params(collective),
        cost_estimate=pl.CostEstimate(flops=0, bytes_accessed=tiles * 20_000_000, transcendentals=0),
    )(*operands)
    return [results[0].reshape(-1, rows * parts, width)] + list(results[1:])


def owner_body(counts, index_ref, *refs):
    sources, refs = refs[: len(counts)], refs[len(counts) :]
    out_ref, held, picked, load_sems, send_sems, recv_sems = refs
    dp_index = lax.axis_index("dp")
    loads, start = [], 0
    for place, count in enumerate(counts):
        load = pltpu.make_async_copy(sources[place], held.at[pl.ds(start, count)], load_sems.at[place])
        load.start()
        loads.append(load)
        start += count
    greet([dp_peer(dp_index, flip) for flip in (1, 2, 3)])
    for load in loads:
        load.wait()
    copies = []
    for flip in (3, 1, 2, 0):
        for slot in range(4):
            picked[flip, slot] = held[index_ref[4 * flip + slot]]
        target = out_ref.at[:, dp_index]
        if flip:
            copies.append(
                remote(picked.at[flip], target, send_sems.at[flip], recv_sems.at[flip], dp_peer(dp_index, flip))
            )
        else:
            here = pltpu.make_async_copy(picked.at[flip], target, load_sems.at[0])
            here.start()
            copies.append(here)
    for copy in copies:
        copy.wait()


def to_owners(sums, order, tile_slots, collective):
    rows, width = sums[0].shape[-2:]
    counts = tuple(part.shape[0] for part in sums)
    dp_index = lax.axis_index("dp")
    spots = jnp.arange(16, dtype=jnp.int32)
    wanted = ((spots // 4) ^ dp_index) * 4 + spots % 4
    slots = reorder(tile_slots, order)
    matches = slots[None, :] == wanted[:, None]
    index = jnp.sum(jnp.where(matches, spots[None, :], 0), axis=1).astype(jnp.int32)
    bf = jnp.bfloat16
    return pl.pallas_call(
        functools.partial(owner_body, counts),
        grid_spec=pltpu.PrefetchScalarGridSpec(
            num_scalar_prefetch=1,
            grid=(),
            in_specs=[ANY] * len(counts),
            out_specs=ANY,
            scratch_shapes=[
                pltpu.VMEM((16, rows, width), bf),
                pltpu.VMEM((4, 4, rows, width), bf),
                pltpu.SemaphoreType.DMA((len(counts),)),
                pltpu.SemaphoreType.DMA((4,)),
                pltpu.SemaphoreType.DMA((4,)),
            ],
        ),
        out_shape=jax.ShapeDtypeStruct((4, 4, rows, width), bf),
        compiler_params=comm_params(collective),
        cost_estimate=pl.CostEstimate(flops=0, bytes_accessed=50_000_000, transcendentals=0),
    )(index, *sums)


def tile_sums(form, left, right):
    total = contract(form, left, right).astype(jnp.bfloat16)
    return total.reshape(-1, 4, 2, 4, total.shape[-2] // 32, total.shape[-1])


def mod_sums(grad_modulation):
    rows, width = grad_modulation.shape
    columns_here = width // 32
    blocks = grad_modulation.reshape(rows, 4, 4, 2, columns_here).transpose(2, 3, 1, 0, 4)
    flat = blocks.astype(jnp.bfloat16).reshape(1, 4, 2, 4, rows * columns_here)
    flat = jnp.pad(flat, ((0, 0),) * 4 + ((0, MOD_ROWS * 1024 - rows * columns_here),))
    return flat.reshape(1, 4, 2, 4, MOD_ROWS, 1024)


def after(value, *others):
    return lax.optimization_barrier((value,) + others)[0]


def weight_source(master, modulation, tile_slots):
    if not fast_layout(master):
        chunks, mod_all = fetch_generic(master, modulation, tile_slots)
        generic = lambda number, mixes, *others: [chunks[number]] + [mix_generic(mix) for mix in mixes]
        return generic, mod_all
    slots_here, row_count, width = master.shape
    dp_index = lax.axis_index("dp")
    narrow = master.astype(jnp.bfloat16).reshape(slots_here, 4, row_count // 4, width)
    index = ((tile_slots // slots_here) ^ dp_index) * slots_here + tile_slots % slots_here
    index = reorder(index, [tile for chunk in CHUNKS for tile in chunk])
    mod_rows, mod_columns = modulation.shape
    mod_flat = modulation.astype(jnp.bfloat16).reshape(-1)
    mod_flat = jnp.pad(mod_flat, (0, MOD_ROWS * width - mod_flat.shape[0])).reshape(MOD_ROWS, width)
    first, mods, zoned, rest = first_gather(narrow, mod_flat, index)
    flat = mods.reshape(8, 4, MOD_ROWS * width)[:, :, : mod_rows * mod_columns]
    mod_all = flat.reshape(8, 4, mod_rows, mod_columns).transpose(2, 1, 0, 3).reshape(mod_rows, -1)

    last_zone = []

    def chunk(number, mixes, *others):
        tiles = len(CHUNKS[number])
        if number == 0:
            return [first.reshape(tiles, row_count * 8, width)]
        if number < 3:
            held = after(zoned, *others) if others else zoned
            return next_gather(held, tiles, (0, 3)[number - 1], True, mixes, None, number)
        if number == 3:
            *results, zone = next_gather(rest, tiles, 0, False, mixes, (tiles, 16 - EARLY - tiles), number)
            last_zone.append(zone)
            return results
        return next_gather(last_zone[0], tiles, 0, True, mixes, None, number)

    return chunk, mod_all


def pair_body(x_ref, w_ref, out_ref):
    objects, rows, width = x_ref.shape
    values = dot(x_ref[...].reshape(objects * rows, width), w_ref[0], NN).astype(jnp.bfloat16)
    for side in range(2):
        part = values[:, side * LANES : (side + 1) * LANES]
        out_ref[side, 0] = part.reshape(objects, rows, LANES)


def project_pairs(tokens, objects, tiles):
    unused_objects, rows, width = tokens.shape
    blocks = tiles.shape[0]
    return pl.pallas_call(
        pair_body,
        grid=(blocks, 4),
        in_specs=[
            pl.BlockSpec((objects, rows, width), lambda k, g: (0, 0, 0)),
            pl.BlockSpec((1, width, 2 * LANES), lambda k, g: (k, 0, g)),
        ],
        out_specs=pl.BlockSpec((2, 1, objects, rows, LANES), lambda k, g: (g, k, 0, 0, 0)),
        out_shape=jax.ShapeDtypeStruct((8, blocks, objects, rows, LANES), jnp.bfloat16),
        cost_estimate=pl.CostEstimate(
            flops=2 * objects * rows * width * blocks * 8 * LANES,
            bytes_accessed=2 * objects * rows * (width + blocks * 8 * LANES),
            transcendentals=0,
        ),
    )(tokens, tiles)


def exchange(pieces):
    return lax.all_to_all(pieces, "fsdp", split_axis=0, concat_axis=0, tiled=True)


def by_head(values, groups):
    blocks, objects, rows, width = values.shape
    moved = values.reshape(blocks, objects, rows, groups, width // groups)
    return moved.transpose(3, 0, 1, 2, 4)


def from_head(pieces):
    groups, blocks, objects, rows, share = pieces.shape
    return pieces.transpose(1, 2, 3, 0, 4).reshape(blocks, objects, rows, groups * share)


def mix_generic(mix):
    if mix is None:
        return None
    kind, sources = mix
    if kind == "heads":
        return exchange(by_head(sources[0], lax.axis_size("fsdp")))
    if kind == "objects":
        sources = [jnp.concatenate(sources, axis=1)]
    parts = [array if array.ndim == 5 else array[:, None] for array in sources]
    return from_head(exchange(jnp.concatenate(parts, axis=1)))


def adamw(weights, grads, first, second, rate):
    first_new = BETA_ONE * first + (1.0 - BETA_ONE) * grads
    second_new = BETA_TWO * second + (1.0 - BETA_TWO) * grads * grads
    first_hat = first_new / (1.0 - BETA_ONE**STEP)
    second_hat = second_new / (1.0 - BETA_TWO**STEP)
    weights_new = weights - rate * (
        first_hat / (jnp.sqrt(second_hat) + EPSILON) + WEIGHT_DECAY * weights
    )
    return (weights_new, first_new, second_new)


def shards(
    triplane,
    image_tokens,
    camera,
    view_tokens,
    master,
    moment1,
    moment2,
    tile_slots,
    modulation,
    mod_moment1,
    mod_moment2,
    cotangent,
):
    objects, tri_local, model_width = triplane.shape
    groups = lax.axis_size("fsdp")
    tri_total = tri_local * groups
    fast = fast_layout(master)
    partial_sums = tile_sums if fast else contract

    def reduced(grads, mods, mixes, collective, parts=1):
        if not fast:
            return [None] + [mix_generic(mix) for mix in mixes]
        return reduce_tiles(grads, mods, mixes, collective, parts)

    chunk, mod_all = weight_source(master, modulation, tile_slots)
    mod_full = mod_all.astype(jnp.float32)
    modulations = (
        jnp.dot(camera, mod_full[:-1], precision=HIGHEST, preferred_element_type=jnp.float32)
        + mod_full[-1]
    )
    blocks = [
        modulations[:, position * model_width : (position + 1) * model_width][:, None, :]
        for position in range(9)
    ]
    half = objects // 2
    (tiles_pair,) = chunk(0, [])
    if fast:
        pair_sent = project_pairs(image_tokens, half, tiles_pair)
    else:
        image_pairs = contract("oid,kde->koie", image_tokens[:half], tiles_pair).astype(jnp.bfloat16)
        pair_sent = by_head(image_pairs, groups)
    pair_early = exchange(pair_sent)
    (tiles_qkv,) = chunk(1, [], pair_sent)
    pairs_late = contract("oid,kde->koie", image_tokens[half:], tiles_pair).astype(jnp.bfloat16)
    residual_in = triplane.astype(jnp.float32)
    normed_one = modulate(residual_in, blocks[0], blocks[1]).astype(jnp.bfloat16)
    triples = contract("otd,kde->kote", normed_one, tiles_qkv).astype(jnp.bfloat16)
    tiles_mixed, triple_heads = chunk(2, [("heads", [triples])])
    tile_out_one, tile_query_two, tile_out_two = tiles_mixed[0], tiles_mixed[1], tiles_mixed[2]
    every_key = jnp.full((objects,), tri_total, jnp.int32)
    self_sources = [(triple_heads, index, 0) for index in range(3)]
    self_result, self_logsum = attend_forward(every_key, *self_sources, tri_total, VIEW, (0, objects))
    tiles_up, merged_one = chunk(3, [("tokens", [self_result])])
    merged_one = merged_one[0]
    branch_one = contract("otd,de->ote", merged_one, tile_out_one)
    residual_mid = residual_in + blocks[2] * branch_one
    normed_two = modulate(residual_mid, blocks[3], blocks[4]).astype(jnp.bfloat16)
    cross_query = contract("otd,de->ote", normed_two, tile_query_two).astype(jnp.bfloat16)
    tiles_down, query_heads, pair_late = chunk(4, [("heads", [cross_query[None]]), ("heads", [pairs_late])])
    cross_sources, cross_result, cross_logsum = [], [], []
    for place in range(objects):
        pair_heads, shift = (pair_early, place) if place < half else (pair_late, place - half)
        sources = [(query_heads, 0, place), (pair_heads, 0, shift), (pair_heads, 1, shift)]
        result, logsum = attend_forward(view_tokens, *sources, tri_total, VIEW, (place, 1))
        cross_sources.append(sources)
        cross_result.append(result)
        cross_logsum.append(logsum)
    cross_mix = ("objects", cross_result)
    merged_two = (mix_alone(cross_mix, 11) if fast else mix_generic(cross_mix))[0]
    branch_two = contract("otd,de->ote", merged_two, tile_out_two)
    residual_late = residual_mid + blocks[5] * branch_two
    normed_three = modulate(residual_late, blocks[6], blocks[7]).astype(jnp.bfloat16)
    hidden_pre = contract("otd,kde->otke", normed_three, tiles_up)
    hidden = gelu_tanh(hidden_pre).astype(jnp.bfloat16)
    branch_three = contract("otkd,kde->ote", hidden, tiles_down)
    block_output = (residual_late + blocks[8] * branch_three).astype(jnp.bfloat16)
    grad_final = cotangent.astype(jnp.float32)
    grad_gate_three = jnp.sum(grad_final * branch_three, axis=1)
    grad_branch_three = (blocks[8] * grad_final).astype(jnp.bfloat16)
    grad_hidden = contract("ote,kde->otkd", grad_branch_three, tiles_down)
    unused_gelu, gelu_pull = jax.vjp(gelu_tanh, hidden_pre)
    grad_pre = gelu_pull(grad_hidden)[0].astype(jnp.bfloat16)
    grad_normed_three = contract("otke,kde->otd", grad_pre, tiles_up)
    grad_late_norm, grad_shift_three, grad_scale_three = modulate_back(
        residual_late, blocks[6], blocks[7], grad_normed_three
    )
    grad_late = grad_final + grad_late_norm
    grad_gate_two = jnp.sum(grad_late * branch_two, axis=1)
    grad_branch_two = (blocks[5] * grad_late).astype(jnp.bfloat16)
    grad_merged_two = contract("ote,de->otd", grad_branch_two, tile_out_two).astype(jnp.bfloat16)
    grad_down = partial_sums("otkd,ote->kde", hidden, grad_branch_three)
    grad_up = partial_sums("otd,otke->kde", normed_three, grad_pre)
    grad_out_two = partial_sums("otd,ote->de", merged_two, grad_branch_two)
    sums_down, grad_cross_heads = reduced([grad_down], None, [("heads", [grad_merged_two[None]])], 5, 2)
    grad_query_heads, grad_pair_heads = [], []
    for place in range(objects):
        query_part, pair_part = attend_backward(
            view_tokens, *cross_sources[place], cross_result[place], cross_logsum[place], grad_cross_heads, VIEW, (place, 1)
        )
        grad_query_heads.append(query_part)
        grad_pair_heads.append(pair_part)
    pair_mixes = [("tokens", [part]) for part in grad_pair_heads]
    sums_up, grad_query_two, *grad_pairs = reduced(
        [grad_up], None, [("objects", grad_query_heads)] + pair_mixes[:half], 6
    )
    grad_query_two = grad_query_two[0]
    grad_tile_query = partial_sums("otd,ote->de", normed_two, grad_query_two)
    grad_normed_two = contract("ote,de->otd", grad_query_two, tile_query_two)
    grad_mid_norm, grad_shift_two, grad_scale_two = modulate_back(
        residual_mid, blocks[3], blocks[4], grad_normed_two
    )
    grad_mid = grad_late + grad_mid_norm
    grad_gate_one = jnp.sum(grad_mid * branch_one, axis=1)
    grad_branch_one = (blocks[2] * grad_mid).astype(jnp.bfloat16)
    grad_merged_one = contract("ote,de->otd", grad_branch_one, tile_out_one).astype(jnp.bfloat16)
    grad_out_one = partial_sums("otd,ote->de", merged_one, grad_branch_one)
    sums_mid, grad_self_heads, *more_pairs = reduced(
        [grad_out_two, grad_tile_query], None, [("heads", [grad_merged_one[None]])] + pair_mixes[half:], 7
    )
    grad_self_query, grad_self_pair = attend_backward(
        every_key, *self_sources, self_result, self_logsum, grad_self_heads, VIEW, (0, objects)
    )
    grad_pairs = jnp.concatenate(grad_pairs + more_pairs, axis=1)
    grad_tiles_pair = partial_sums("oid,koie->kde", image_tokens, grad_pairs)
    grad_image = contract("koie,kde->oid", grad_pairs, tiles_pair)
    sums_late, grad_triples = reduced(
        [grad_tiles_pair, grad_out_one], None, [("tokens", [grad_self_query, grad_self_pair])], 8
    )
    grad_qkv = partial_sums("otd,kote->kde", normed_one, grad_triples)
    grad_normed_one = contract("kote,kde->otd", grad_triples, tiles_qkv)
    grad_in_norm, grad_shift_one, grad_scale_one = modulate_back(
        residual_in, blocks[0], blocks[1], grad_normed_one
    )
    grad_triplane = grad_mid + grad_in_norm
    grad_mods = jnp.concatenate(
        [
            grad_shift_one[:, 0],
            grad_scale_one[:, 0],
            grad_gate_one,
            grad_shift_two[:, 0],
            grad_scale_two[:, 0],
            grad_gate_two,
            grad_shift_three[:, 0],
            grad_scale_three[:, 0],
            grad_gate_three,
        ],
        axis=-1,
    )
    grad_mod_rows = jnp.dot(
        camera.T, grad_mods, precision=HIGHEST, preferred_element_type=jnp.float32
    )
    grad_modulation = jnp.concatenate(
        [grad_mod_rows, jnp.sum(grad_mods, axis=0, keepdims=True)], axis=0
    )
    if fast:
        sums_qkv, mod_sum = reduce_tiles([grad_qkv], mod_sums(grad_modulation), [], 9, 2)
        sums = [sums_qkv, sums_late, sums_mid, sums_up, sums_down]
        order = (0, 1, 2, 5, 6, 3, 7, 4, 8, 9, 10, 11, 12, 13, 14, 15)
        tile_grad = to_owners(sums, order, tile_slots, 10).reshape(master.shape)
        mod_grad = mod_sum.reshape(-1)[: modulation.size].reshape(modulation.shape)
        tile_grad, mod_grad = tile_grad.astype(jnp.float32), mod_grad.astype(jnp.float32)
    else:
        logical = [grad_qkv[0], grad_qkv[1], grad_qkv[2], grad_out_one, grad_tile_query]
        logical = logical + [grad_tiles_pair[0], grad_tiles_pair[1], grad_out_two]
        logical = logical + [grad_up[tile] for tile in range(4)]
        logical = logical + [grad_down[tile] for tile in range(4)]
        tile_grad = sums_generic(logical, tile_slots).astype(jnp.float32)
        mod_grad = mod_generic(grad_modulation)
    new_master, new_moment1, new_moment2 = adamw(master, tile_grad, moment1, moment2, RATE_TILES)
    new_modulation, new_mod_moment1, new_mod_moment2 = adamw(
        modulation, mod_grad, mod_moment1, mod_moment2, RATE_MODULATION
    )
    return (
        block_output,
        grad_triplane,
        grad_image,
        new_master,
        new_moment1,
        new_moment2,
        new_master.astype(jnp.bfloat16),
        new_modulation,
        new_mod_moment1,
        new_mod_moment2,
    )


def solution(mesh):
    in_specs = (
        P("dp", "fsdp", None),
        P("dp", "fsdp", None),
        P("dp", None),
        P("dp"),
        P("dp", "fsdp", None),
        P("dp", "fsdp", None),
        P("dp", "fsdp", None),
        P(),
        P(None, ("dp", "fsdp")),
        P(None, ("dp", "fsdp")),
        P(None, ("dp", "fsdp")),
        P("dp", "fsdp", None),
    )
    out_specs = (
        P("dp", "fsdp", None),
        P("dp", "fsdp", None),
        P("dp", "fsdp", None),
        P("dp", "fsdp", None),
        P("dp", "fsdp", None),
        P("dp", "fsdp", None),
        P("dp", "fsdp", None),
        P(None, ("dp", "fsdp")),
        P(None, ("dp", "fsdp")),
        P(None, ("dp", "fsdp")),
    )
    return jax.shard_map(shards, mesh=mesh, in_specs=in_specs, out_specs=out_specs, check_vma=False)
```
